128 devices in a mesh: rows: 8 (over y, x_hi), seq: 16 (over z, x_lo, core).
Axes of the slice: x: 4 (x_hi: 2, x_lo: 2; x = x_hi * 2 + x_lo), y: 4, z: 4, core: 2. Of those that a mesh axis runs over, the one named last changes fastest.
Arguments:
- tokens: bfloat16 [8, 2048, 1024], P('rows', 'seq'), may hold values from -6 to 6
- cotangent: bfloat16 [8, 2048, 1024], P('rows', 'seq'), may hold values from -6 to 6
- segment: int32 [8, 2048], P('rows', 'seq'), may hold values from 0 to 3, never falling along the last dimension, each value on 1 to 1024 neighbouring positions
- routes: int32 [8, 2048, 2], P('rows', 'seq'), may hold values from 0 to 2, all different within a row
- attn_gain: bfloat16 [1024], replicated, may hold values from 0.5 to 1.5
- w_query: bfloat16 [1024, 1024], replicated, may hold values from -0.25 to 0.25
- w_key: bfloat16 [1024, 512], replicated, may hold values from -0.25 to 0.25
- w_value: bfloat16 [1024, 512], replicated, may hold values from -0.1875 to 0.1875
- w_output: bfloat16 [1024, 1024], replicated, may hold values from -0.75 to 0.75
- expert_norm_gain: bfloat16 [1024], replicated, may hold values from 0.5 to 1.5
- w_router: bfloat16 [1024, 3], replicated, may hold values from -0.375 to 0.375
- w_gate: bfloat16 [3, 1024, 512], replicated, may hold values from -0.1875 to 0.1875
- w_up: bfloat16 [3, 1024, 512], replicated, may hold values from -0.1875 to 0.1875
- w_down: bfloat16 [3, 512, 1024], replicated, may hold values from -0.5 to 0.5
Outputs:
- output: bfloat16 [8, 2048, 1024], P('rows', 'seq')
- token_grad: bfloat16 [8, 2048, 1024], P('rows', 'seq')
- attn_gain_grad: float32 [1024], replicated
- query_w_grad: float32 [1024, 1024], replicated
- key_w_grad: float32 [1024, 512], replicated
- value_w_grad: float32 [1024, 512], replicated
- output_w_grad: float32 [1024, 1024], replicated
- moe_gain_grad: float32 [1024], replicated
- router_grad: float32 [1024, 3], replicated
- gate_grad: float32 [3, 1024, 512], replicated
- up_grad: float32 [3, 1024, 512], replicated
- down_grad: float32 [3, 512, 1024], replicated
The draws below stay inside these ranges and needn't reach their ends.
Inputs may be any that keep to these rules, and one draw needn't show every extreme that they name: `segment`: in each packed row the ids never fall; each of the 4 ids names one document of 1 to 1024 tokens, and one document has exactly 1024. `routes`: each token names 2 different experts.
All inputs are finite; a program needn't handle non-finite values.
Results may differ from the reference program's by a relative error of at most 0.02.
The reference program's roundings to bfloat16 on the way count: a program that leaves them out, or rounds other values in their place, can miss the bound.
Values may be sent and summed in bfloat16 or wider, within the bound.
No kernel may reach another device: no remote copies, remote signals or barrier semaphores. Data moves between devices by JAX's collectives and lax.ppermute only.
A program may use at most 192 MiB of HBM per device.

```python
import math
import jax
import jax.numpy as jnp
import numpy as np
from jax import lax

MODEL_DIM = 1024
HQ = 16
HK = 8
HD = 64
FF = 512
EXPERT_COUNT = 3
CHOSEN_EXPERTS = 2
ROW_TOKENS = 2048
PACKED_ROWS = 8


def block_levels(own_key, dims, shards, low, largest):
    def one(axis_at, blocks):
        draws = jax.random.uniform(jax.random.fold_in(jax.random.fold_in(own_key, 6), axis_at), (blocks,), jnp.float32, low / len(shards), largest / len(shards))
        return jnp.repeat(jnp.exp(draws), dims[axis_at] // blocks).reshape((-1,) + (1,) * (len(dims) - axis_at - 1))

    factor_of = one(*shards[0])
    for cut in shards[1:]:
        factor_of = factor_of * one(*cut)
    return factor_of


def different_ones(key, rows, amount, top, lift):
    order = jax.random.permutation(jax.random.fold_in(key, 1), amount)
    pull = order
    for power in range(3):
        pull = pull * pull // amount
    pull = pull * lift // amount
    tickets = jax.random.randint(jax.random.fold_in(key, 2), (rows, amount), 0, 4096) + pull
    fixed_rows = jax.random.permutation(jax.random.fold_in(key, 3), rows)[jnp.arange(amount) % rows]
    tickets = jnp.where(jnp.arange(rows)[:, None] == fixed_rows[None, :], 1 << 14, tickets)
    score = tickets * amount + jnp.arange(amount)
    return lax.top_k(score.astype(jnp.int32), top)[1].astype(jnp.int32)


def profile(amount, total, most, lean):
    weights = [(1 << 20) // math.isqrt(rank ** lean) + 1 for rank in range(2, amount + 1)]
    rest, holding = total - most - (amount - 1), [1] * (amount - 1)
    while rest > 0:
        candidates = [i for i in range(amount - 1) if holding[i] < most]
        pool, budget = sum([weights[i] for i in candidates]), rest
        for i in candidates:
            more = min(most - holding[i], max(1, budget * weights[i] // pool), rest)
            holding[i] = holding[i] + more
            rest = rest - more
    return np.array([most] + holding)


def ragged(rng, count, total, bound, lean):
    if count == 2:
        one = jax.random.randint(rng, (), max(1, total - bound), min(bound, total - 1) + 1)
        return jnp.stack([one, total - one])
    sizes = jnp.asarray(profile(count, total, bound, lean), jnp.int32)
    twos = (count - 1) // 2
    giver, receiver = sizes[1:1 + 2 * twos:2], sizes[2:2 + 2 * twos:2]
    slack = jnp.minimum(giver - 1, bound - receiver)
    shifted = jax.random.randint(jax.random.fold_in(rng, 1), (twos,), 0, 1 << 20) % (slack + 1)
    sizes = sizes.at[1:1 + 2 * twos:2].set(giver - shifted).at[2:2 + 2 * twos:2].set(receiver + shifted)
    return sizes[jax.random.permutation(jax.random.fold_in(rng, 2), count)]


def scatter_about(key, extent, deviation, limit, cuts=(), held_as=jnp.bfloat16):
    factor_of = block_levels(key, extent, cuts, -0.22, 0.18) if cuts else 1.0
    array = jax.random.normal(key, extent, jnp.float32) * deviation * factor_of
    return jnp.minimum(jnp.maximum(array, -limit), limit).astype(held_as)


def setup_inputs(seed: int = 0) -> dict:
    streams_of = jax.random.split(jax.random.key(seed), 15)
    return {
        "tokens": scatter_about(streams_of[0], (PACKED_ROWS, ROW_TOKENS, MODEL_DIM), 1.0, 6.0, ((0, 8), (1, 16))),
        "cotangent": scatter_about(streams_of[1], (PACKED_ROWS, ROW_TOKENS, MODEL_DIM), 1.0, 6.0, ((0, 8), (1, 16))),
        "segment": jax.vmap(lambda own: jnp.searchsorted(jnp.cumsum(ragged(own, 4, ROW_TOKENS, ROW_TOKENS // 2, 0)), jnp.arange(ROW_TOKENS), side="right"))(jax.random.split(streams_of[2], PACKED_ROWS)).reshape((PACKED_ROWS, ROW_TOKENS)).astype(jnp.int32),
        "routes": different_ones(streams_of[3], PACKED_ROWS * ROW_TOKENS, EXPERT_COUNT, CHOSEN_EXPERTS, 0).reshape((PACKED_ROWS, ROW_TOKENS, CHOSEN_EXPERTS)),
        "attn_gain": jnp.clip(1.0 + 0.1 * jax.random.normal(streams_of[4], (MODEL_DIM,), jnp.float32), 0.5, 1.5).astype(jnp.bfloat16),
        "w_query": scatter_about(streams_of[5], (MODEL_DIM, HQ * HD), (MODEL_DIM // 2) ** -0.5, 0.25),
        "w_key": scatter_about(streams_of[6], (MODEL_DIM, HK * HD), (MODEL_DIM // 2) ** -0.5, 0.25),
        "w_value": scatter_about(streams_of[7], (MODEL_DIM, HK * HD), MODEL_DIM ** -0.5, 0.1875),
        "w_output": scatter_about(streams_of[8], (HQ * HD, MODEL_DIM), (HQ * HD // 16) ** -0.5, 0.75),
        "expert_norm_gain": jnp.clip(1.0 + 0.1 * jax.random.normal(streams_of[9], (MODEL_DIM,), jnp.float32), 0.5, 1.5).astype(jnp.bfloat16),
        "w_router": scatter_about(streams_of[10], (MODEL_DIM, EXPERT_COUNT), (MODEL_DIM // 4) ** -0.5, 0.375),
        "w_gate": scatter_about(streams_of[11], (EXPERT_COUNT, MODEL_DIM, FF), MODEL_DIM ** -0.5, 0.1875),
        "w_up": scatter_about(streams_of[12], (EXPERT_COUNT, MODEL_DIM, FF), MODEL_DIM ** -0.5, 0.1875),
        "w_down": scatter_about(streams_of[13], (EXPERT_COUNT, FF, MODEL_DIM), (FF // 4) ** -0.5, 0.5),
    }


EPSILON = 1e-06
THETA_BASE = 10000.0
SOFT_SCALE = 0.125
NEG_FILL = -1e+30

@jax.custom_vjp
def low(v):
    return lax.optimization_barrier(v.astype(jnp.bfloat16)).astype(jnp.float32)

@jax.custom_vjp
def low_back(v):
    return v

def low_keep(v):
    return (low(v), None)

def low_pass(kept, grad):
    return (grad,)

def back_keep(v):
    return (v, None)

def back_low(kept, grad):
    return (low(grad),)
low.defvjp(low_keep, low_pass)
low_back.defvjp(back_keep, back_low)

def matmul(left, right_side):
    return jnp.dot(left, right_side, precision=lax.Precision.HIGHEST, preferred_element_type=jnp.float32)

def rms_apply(hidden, gain):
    inverse = lax.rsqrt(lax.optimization_barrier(jnp.mean(hidden * hidden, axis=-1, keepdims=True)) + EPSILON)
    return hidden * inverse * gain

def rotate(heads, cosine_table, sine_table):
    half_size = heads.shape[-1] // 2
    turned = jnp.concatenate([-heads[..., half_size:], heads[..., :half_size]], axis=-1)
    return heads * cosine_table + turned * sine_table

def rope_tables(positions, head_size):
    frequency = jnp.exp(jnp.arange(head_size // 2, dtype=jnp.float32) * (-2.0 * math.log(THETA_BASE) / head_size))
    angles = positions[..., None] * frequency
    angles = jnp.concatenate([angles, angles], axis=-1)
    return (jnp.cos(angles)[..., None, :], jnp.sin(angles)[..., None, :])

def swiglu(gate_proj, up_proj):
    return jax.nn.silu(gate_proj) * up_proj

def route_weights(logits, routes):
    one_hot = (routes[..., None] == jnp.arange(logits.shape[-1], dtype=jnp.int32)).astype(jnp.float32)
    chosen = lax.optimization_barrier(jnp.sum(one_hot * logits[..., None, :], axis=-1))
    weights = jax.nn.softmax(chosen, axis=-1)
    return lax.optimization_barrier(jnp.sum(weights[..., None] * one_hot, axis=-2))

def layer_row(inputs, segment, routes, attn_gain, w_query, w_key, w_value, w_output, expert_norm_gain, w_router, w_gate, w_up, w_down):
    seq_len = inputs.shape[0]
    group_size = HQ // HK
    token_index = jnp.arange(seq_len, dtype=jnp.int32)
    starts = lax.optimization_barrier(jnp.sum((segment[None, :] < segment[:, None]).astype(jnp.int32), axis=1))
    positions = (token_index - starts).astype(jnp.float32)
    cosine_table, sine_table = rope_tables(positions, HD)
    normed = low(rms_apply(inputs, attn_gain))
    queries = low_back(matmul(normed, w_query)).reshape(seq_len, HQ, HD)
    keys_raw = low_back(matmul(normed, w_key)).reshape(seq_len, HK, HD)
    values = low(low_back(matmul(normed, w_value))).reshape(seq_len, HK, HD)
    queries = low(rotate(queries, cosine_table, sine_table)).reshape(seq_len, HK, group_size, HD)
    keys_rot = low(rotate(keys_raw, cosine_table, sine_table))
    block_rows = math.gcd(seq_len, 512)

    def attend(block_index):
        first_row = block_index * block_rows
        query_block = lax.dynamic_slice_in_dim(queries, first_row, block_rows, 0)
        query_index = first_row + jnp.arange(block_rows, dtype=jnp.int32)
        query_seg = lax.dynamic_slice_in_dim(segment, first_row, block_rows, 0)
        scores = low_back(SOFT_SCALE * jnp.einsum('skgd,nkd->kgsn', query_block, keys_rot, precision=lax.Precision.HIGHEST))
        allowed = (segment[None, :] == query_seg[:, None]) & (token_index[None, :] <= query_index[:, None])
        scores = jnp.where(allowed[None, None], scores, NEG_FILL)
        weights_low = low(jax.nn.softmax(scores, axis=-1))
        return jnp.einsum('kgsn,nkd->skgd', weights_low, values, precision=lax.Precision.HIGHEST)
    attended = lax.map(jax.checkpoint(attend), jnp.arange(seq_len // block_rows, dtype=jnp.int32))
    attended = low(low_back(attended.reshape(seq_len, HQ * HD)))
    resid = inputs + low_back(matmul(attended, w_output))
    moe_low = low(rms_apply(resid, expert_norm_gain))
    logits = low_back(matmul(moe_low, w_router))
    combine = route_weights(logits, routes)
    mixture = jnp.zeros_like(resid)
    for expert in range(w_gate.shape[0]):
        gate_proj = low_back(matmul(moe_low, w_gate[expert]))
        up_proj = low_back(matmul(moe_low, w_up[expert]))
        act_low = low(swiglu(gate_proj, up_proj))
        expert_out = low_back(matmul(act_low, w_down[expert]))
        mixture = mixture + combine[:, expert:expert + 1] * expert_out
    return resid + mixture

def reference(tokens, cotangent, segment, routes, attn_gain, w_query, w_key, w_value, w_output, expert_norm_gain, w_router, w_gate, w_up, w_down):

    def forward(inputs, gain_one, query_w, key_w, value_w, output_w, gain_two, router_w, gate_w, up_w, down_w):

        def one_row(row_data):
            return layer_row(row_data[0], row_data[1], row_data[2], gain_one, query_w, key_w, value_w, output_w, gain_two, router_w, gate_w, up_w, down_w)
        return lax.map(one_row, (inputs, segment, routes))
    output, pull_back = jax.vjp(forward, tokens.astype(jnp.float32), attn_gain.astype(jnp.float32), w_query.astype(jnp.float32), w_key.astype(jnp.float32), w_value.astype(jnp.float32), w_output.astype(jnp.float32), expert_norm_gain.astype(jnp.float32), w_router.astype(jnp.float32), w_gate.astype(jnp.float32), w_up.astype(jnp.float32), w_down.astype(jnp.float32))
    grads = pull_back(cotangent.astype(jnp.float32))
    return (output.astype(jnp.bfloat16), grads[0].astype(jnp.bfloat16), grads[1], grads[2], grads[3], grads[4], grads[5], grads[6], grads[7], grads[8], grads[9], grads[10])
```

```python
import math

import jax
import jax.numpy as jnp
from jax import lax
from jax.experimental import pallas as pl
from jax.experimental.pallas import tpu as pltpu
from jax.sharding import Mesh
from jax.sharding import PartitionSpec as P

BF = jnp.bfloat16
F32 = jnp.float32
D = 1024
HQ = 16
HK = 8
HD = 64
FF = 512
EXPERTS = 3
T = 128
S = 2048
BLK = 256
NB = S // BLK
HALF = HD // 2
PAY = 3 * HD + 16
FC = 256
NF = FF // FC

EPSILON = 1e-06
THETA_BASE = 10000.0
SOFT_SCALE = 0.125
NEG_FILL = -1e30

AXES = ("y", "xh", "z", "xl", "core")
ROWS = ("y", "xh")
SEQ = ("z", "xl", "core")

NN = (((1,), (0,)), ((), ()))
NT = (((1,), (1,)), ((), ()))
TN = (((0,), (0,)), ((), ()))


def dot(a, b, dims=NN):
    return lax.dot_general(a, b, dims, preferred_element_type=F32)


def swap(a):
    return jnp.transpose(a, (1, 0))


def project_kernel(tok_ref, seg_ref, gain_ref, wq_ref, wk_ref, wv_ref, out_ref):
    x = tok_ref[...].astype(F32)
    inverse = lax.rsqrt(jnp.mean(x * x, axis=1, keepdims=True) + EPSILON)
    normed = (x * inverse * gain_ref[...].astype(F32)).astype(BF)
    ids = jnp.broadcast_to(seg_ref[...].astype(F32), (16, T)).astype(BF)
    for h in range(HQ):
        out_ref[h, 3 * HD :, :] = ids
    for j in range(4):
        q = swap(dot(normed, wq_ref[:, 256 * j : 256 * (j + 1)])).astype(BF)
        for i in range(4):
            out_ref[4 * j + i, 0:HD, :] = q[HD * i : HD * (i + 1)]
    for w_ref, at in ((wk_ref, HD), (wv_ref, 2 * HD)):
        for j in range(2):
            a = swap(dot(normed, w_ref[:, 256 * j : 256 * (j + 1)])).astype(BF)
            for i in range(4):
                part = a[HD * i : HD * (i + 1)]
                head = 2 * (4 * j + i)
                out_ref[head, at : at + HD, :] = part
                out_ref[head + 1, at : at + HD, :] = part


def project(tokens, segment, gain, w_query, w_key, w_value):
    return pl.pallas_call(
        project_kernel,
        out_shape=jax.ShapeDtypeStruct((HQ, PAY, T), BF),
        name="project",
    )(tokens, segment, gain, w_query, w_key, w_value)


def starts_of(x_ref):
    ids = x_ref[:, 3 * HD :, :].astype(F32)
    counts = [
        (jnp.sum(jnp.where(ids == float(s), 1.0, 0.0)) * (1.0 / 16)).astype(jnp.int32)
        for s in range(3)
    ]
    first = counts[0]
    second = first + counts[1]
    return first, second, second + counts[2]


def start_at(index, bounds):
    b1, b2, b3 = bounds
    return jnp.where(index >= b3, b3, jnp.where(index >= b2, b2, jnp.where(index >= b1, b1, 0)))


def joined(ref, i, at):
    return jnp.concatenate([ref[2 * i, at : at + HD, :], ref[2 * i + 1, at : at + HD, :]], axis=1)


def allowed_of(i, j, bounds):
    query = i * BLK + lax.broadcasted_iota(jnp.int32, (1, BLK), 1)
    start = start_at(query, bounds)
    key = j * BLK + lax.broadcasted_iota(jnp.int32, (BLK, BLK), 0)
    return (key >= start) & (key <= query)


def attend_kernel(x_ref, att_ref, full_ref, log_ref, q_ref, k_ref, cos_ref, sin_ref, kt_ref, v_ref):
    bounds = starts_of(x_ref)
    frequency = jnp.exp(
        lax.broadcasted_iota(jnp.int32, (HALF, 1), 0).astype(F32)
        * (-2.0 * math.log(THETA_BASE) / HD)
    )

    def turn_block(i, carry):
        index = i * BLK + lax.broadcasted_iota(jnp.int32, (1, BLK), 1)
        positions = (index - start_at(index, bounds)).astype(F32)
        angles = positions * frequency
        cosine, sine = jnp.cos(angles), jnp.sin(angles)
        cos_ref[i] = cosine
        sin_ref[i] = sine

        def turned(at):
            a = joined(x_ref, i, at).astype(F32)
            low, high = a[:HALF], a[HALF:]
            return jnp.concatenate(
                [low * cosine - high * sine, high * cosine + low * sine], axis=0
            )

        q_ref[i] = (turned(0).astype(BF).astype(F32) * SOFT_SCALE).astype(BF)
        k = turned(HD)
        k_ref[i] = k.astype(BF)
        kt_ref[i] = swap(k).astype(BF)
        v_ref[i] = joined(x_ref, i, 2 * HD)
        return carry

    lax.fori_loop(0, NB, turn_block, 0)

    def query_block(i, carry):
        first = start_at(i * BLK, bounds) // BLK
        q = q_ref[i]

        def key_block(j, running):
            top, total, acc = running
            scores = jnp.where(allowed_of(i, j, bounds), dot(kt_ref[j], q), NEG_FILL)
            new_top = jnp.maximum(top, jnp.max(scores, axis=0, keepdims=True))
            weights = jnp.exp(scores - new_top)
            scale = jnp.exp(top - new_top)
            total = total * scale + jnp.sum(weights, axis=0, keepdims=True)
            acc = acc * scale + dot(v_ref[j], weights.astype(BF))
            return new_top, total, acc

        begin = (
            jnp.full((1, BLK), NEG_FILL, F32),
            jnp.zeros((1, BLK), F32),
            jnp.zeros((HD, BLK), F32),
        )
        begin = key_block(i, begin)
        top, total, acc = lax.fori_loop(first, i, key_block, begin)
        attended = acc / total
        log_ref[i] = top + jnp.log(total)
        full_ref[i] = attended
        low = attended.astype(BF)
        att_ref[2 * i] = low[:, :T]
        att_ref[2 * i + 1] = low[:, T:]
        return carry

    lax.fori_loop(0, NB, query_block, 0)


def attend(received):
    return pl.pallas_call(
        attend_kernel,
        out_shape=(
            jax.ShapeDtypeStruct((HQ, HD, T), BF),
            jax.ShapeDtypeStruct((NB, HD, BLK), F32),
            jax.ShapeDtypeStruct((NB, 1, BLK), F32),
            jax.ShapeDtypeStruct((NB, HD, BLK), BF),
            jax.ShapeDtypeStruct((NB, HD, BLK), BF),
            jax.ShapeDtypeStruct((NB, HALF, BLK), F32),
            jax.ShapeDtypeStruct((NB, HALF, BLK), F32),
        ),
        scratch_shapes=[pltpu.VMEM((NB, BLK, HD), BF), pltpu.VMEM((NB, HD, BLK), BF)],
        name="attend",
    )(received)


def attend_back_kernel(
    x_ref, g_ref, full_ref, log_ref, q_ref, k_ref, cos_ref, sin_ref, out_ref,
    kt_ref, vt_ref, dk_ref, dv_ref,
):
    bounds = starts_of(x_ref)

    def prepare(i, carry):
        kt_ref[i] = swap(k_ref[i].astype(F32)).astype(BF)
        vt_ref[i] = swap(joined(x_ref, i, 2 * HD).astype(F32)).astype(BF)
        dk_ref[i] = jnp.zeros((HD, BLK), F32)
        dv_ref[i] = jnp.zeros((HD, BLK), F32)
        return carry

    lax.fori_loop(0, NB, prepare, 0)

    def turn_back(i, a):
        cosine, sine = cos_ref[i], sin_ref[i]
        low, high = a[:HALF], a[HALF:]
        return jnp.concatenate([low * cosine + high * sine, high * cosine - low * sine], axis=0)

    def put(i, at, a):
        low = a.astype(BF)
        out_ref[2 * i, at : at + HD, :] = low[:, :T]
        out_ref[2 * i + 1, at : at + HD, :] = low[:, T:]

    def query_block(i, carry):
        first = start_at(i * BLK, bounds) // BLK
        q = q_ref[i]
        grad = joined(g_ref, i, 0)
        delta = jnp.sum(grad.astype(F32) * full_ref[i], axis=0, keepdims=True)
        log_total = log_ref[i]

        def key_block(j, dq):
            scores = dot(kt_ref[j], q)
            p = jnp.where(allowed_of(i, j, bounds), jnp.exp(scores - log_total), 0.0)
            dp = dot(vt_ref[j], grad)
            ds = (p * (dp - delta)).astype(BF)
            dv_ref[j] += dot(grad, p.astype(BF), NT)
            dk_ref[j] += dot(q, ds, NT)
            return dq + dot(k_ref[j], ds)

        dq = lax.fori_loop(first, i + 1, key_block, jnp.zeros((HD, BLK), F32))
        put(i, 0, turn_back(i, dq * SOFT_SCALE))
        return carry

    lax.fori_loop(0, NB, query_block, 0)

    def finish(i, carry):
        put(i, HD, turn_back(i, dk_ref[i]))
        put(i, 2 * HD, dv_ref[i])
        return carry

    lax.fori_loop(0, NB, finish, 0)


def attend_back(received, grad, full, log_total, q, k, cosine, sine):
    return pl.pallas_call(
        attend_back_kernel,
        out_shape=jax.ShapeDtypeStruct((HQ, 3 * HD, T), BF),
        scratch_shapes=[
            pltpu.VMEM((NB, BLK, HD), BF),
            pltpu.VMEM((NB, BLK, HD), BF),
            pltpu.VMEM((NB, HD, BLK), F32),
            pltpu.VMEM((NB, HD, BLK), F32),
        ],
        name="attend_back",
    )(received, grad, full, log_total, q, k, cosine, sine)


def experts_kernel(
    att_ref, tok_ref, cot_ref, routes_ref, gain_ref, wr_ref, wo_ref, wg_ref, wu_ref, wd_ref,
    out_ref, resid_grad_ref, grad_att_ref, dwo_ref, dwg_ref, dwu_ref, dwd_ref, small_ref,
    moe_ref, moe_t_ref, resid_ref, combine_ref, mix_ref, moe_grad_ref, cgrad_ref,
):
    e, f = pl.program_id(0), pl.program_id(1)
    lane = lax.broadcasted_iota(jnp.int32, (T, T), 1)

    @pl.when((e == 0) & (f == 0))
    def _():
        attended = swap(att_ref[...].astype(F32)).astype(BF)
        resid = tok_ref[...].astype(F32) + dot(attended, wo_ref[...])
        inverse = lax.rsqrt(jnp.mean(resid * resid, axis=1, keepdims=True) + EPSILON)
        normed = resid * inverse * gain_ref[...].astype(F32)
        moe_low = normed.astype(BF)
        resid_ref[...] = resid
        mix_ref[...] = resid
        moe_ref[...] = moe_low
        moe_t_ref[...] = swap(normed).astype(BF)
        logits = dot(moe_low, wr_ref[...], NT)
        r0, r1 = routes_ref[:, 0:1], routes_ref[:, 1:2]
        l0 = jnp.sum(jnp.where(lane[:, :8] == r0, logits, 0.0), axis=1, keepdims=True)
        l1 = jnp.sum(jnp.where(lane[:, :8] == r1, logits, 0.0), axis=1, keepdims=True)
        top = jnp.maximum(l0, l1)
        e0, e1 = jnp.exp(l0 - top), jnp.exp(l1 - top)
        total = e0 + e1
        combine_ref[...] = jnp.where(lane == r0, e0 / total, 0.0) + jnp.where(
            lane == r1, e1 / total, 0.0
        )
        moe_grad_ref[...] = jnp.zeros_like(moe_grad_ref)
        cgrad_ref[...] = jnp.zeros_like(cgrad_ref)

    moe_low = moe_ref[...]
    grad_out = cot_ref[...].astype(F32)
    combine = jnp.sum(jnp.where(lane == e, combine_ref[...], 0.0), axis=1, keepdims=True)
    expert_grad = (combine * grad_out).astype(BF)
    gate = dot(moe_low, wg_ref[0])
    up = dot(moe_low, wu_ref[0])
    sig = 1.0 / (1.0 + jnp.exp(-gate))
    silu = gate * sig
    act = silu * up
    act_low = act.astype(BF)
    down = dot(act_low, wd_ref[0])
    mix_ref[...] += combine * down
    cgrad_ref[...] += jnp.where(lane == e, jnp.sum(grad_out * down, axis=1, keepdims=True), 0.0)
    dwd_ref[0] = dot(swap(act).astype(BF), expert_grad).astype(BF)
    act_grad = dot(expert_grad, wd_ref[0], NT)
    gate_low = (act_grad * up * (sig * (1.0 + gate * (1.0 - sig)))).astype(BF)
    up_low = (act_grad * silu).astype(BF)
    moe_t = moe_t_ref[...]
    dwg_ref[0] = dot(moe_t, gate_low).astype(BF)
    dwu_ref[0] = dot(moe_t, up_low).astype(BF)
    moe_grad_ref[...] += dot(gate_low, wg_ref[0], NT) + dot(up_low, wu_ref[0], NT)

    @pl.when((e == EXPERTS - 1) & (f == NF - 1))
    def _():
        out_ref[...] = mix_ref[...].astype(BF)
        weights, cgrad = combine_ref[...], cgrad_ref[...]
        mean = jnp.sum(weights * cgrad, axis=1, keepdims=True)
        logit_grad = (weights * (cgrad - mean)).astype(BF)
        small_ref[0:8, :] = dot(logit_grad, moe_ref[...], TN)[0:8]
        moe_grad = moe_grad_ref[...] + dot(logit_grad[:, 0:8], wr_ref[...])
        resid = resid_ref[...]
        inverse = lax.rsqrt(jnp.mean(resid * resid, axis=1, keepdims=True) + EPSILON)
        n = resid * inverse
        small_ref[8:16, :] = jnp.broadcast_to(jnp.sum(moe_grad * n, axis=0, keepdims=True), (8, D))
        scaled = moe_grad * gain_ref[...].astype(F32)
        resid_grad = cot_ref[...].astype(F32) + inverse * (
            scaled - n * jnp.mean(n * scaled, axis=1, keepdims=True)
        )
        resid_grad_ref[...] = resid_grad
        low = resid_grad.astype(BF)
        dwo_ref[...] = dot(att_ref[...], low).astype(BF)
        grad_att_ref[...] = dot(wo_ref[...], low, NT).astype(BF)


def experts(attended, tokens, cotangent, routes, gain, w_router, w_output, w_gate, w_up, w_down):
    def whole(*shape):
        return pl.BlockSpec(shape, lambda e, f: (0,) * len(shape))

    def columns():
        return pl.BlockSpec((1, D, FC), lambda e, f: (e, 0, f))

    def rows():
        return pl.BlockSpec((1, FC, D), lambda e, f: (e, f, 0))

    return pl.pallas_call(
        experts_kernel,
        grid=(EXPERTS, NF),
        in_specs=[
            whole(D, T), whole(T, D), whole(T, D), whole(T, 2), whole(1, D), whole(8, D),
            whole(D, D), columns(), columns(), rows(),
        ],
        out_specs=(
            whole(T, D), whole(T, D), whole(D, T), whole(D, D), columns(), columns(), rows(),
            whole(16, D),
        ),
        out_shape=(
            jax.ShapeDtypeStruct((T, D), BF),
            jax.ShapeDtypeStruct((T, D), F32),
            jax.ShapeDtypeStruct((D, T), BF),
            jax.ShapeDtypeStruct((D, D), BF),
            jax.ShapeDtypeStruct((EXPERTS, D, FF), BF),
            jax.ShapeDtypeStruct((EXPERTS, D, FF), BF),
            jax.ShapeDtypeStruct((EXPERTS, FF, D), BF),
            jax.ShapeDtypeStruct((16, D), F32),
        ),
        scratch_shapes=[
            pltpu.VMEM((T, D), BF),
            pltpu.VMEM((D, T), BF),
            pltpu.VMEM((T, D), F32),
            pltpu.VMEM((T, T), F32),
            pltpu.VMEM((T, D), F32),
            pltpu.VMEM((T, D), F32),
            pltpu.VMEM((T, T), F32),
        ],
        name="experts",
    )(attended, tokens, cotangent, routes, gain, w_router, w_output, w_gate, w_up, w_down)


def project_back_kernel(
    g_ref, tok_ref, gain_ref, wq_ref, wk_ref, wv_ref, resid_grad_ref,
    out_ref, dwq_ref, dwk_ref, dwv_ref, small_ref,
):
    x = tok_ref[...].astype(F32)
    gain = gain_ref[...].astype(F32)
    inverse = lax.rsqrt(jnp.mean(x * x, axis=1, keepdims=True) + EPSILON)
    n = x * inverse
    normed_t = swap(n * gain).astype(BF)
    normed_grad = jnp.zeros((T, D), F32)
    dq = g_ref[:, 0:HD, :].reshape(D, T)
    dwq_ref[...] = dot(normed_t, dq, NT).astype(BF)
    normed_grad += dot(swap(dq.astype(F32)).astype(BF), wq_ref[...], NT)
    for at, w_ref, dw_ref in ((HD, wk_ref, dwk_ref), (2 * HD, wv_ref, dwv_ref)):
        parts = g_ref[:, at : at + HD, :].astype(F32).reshape(HK, 2, HD, T)
        summed = (parts[:, 0] + parts[:, 1]).reshape(HK * HD, T)
        low = summed.astype(BF)
        dw_ref[...] = dot(normed_t, low, NT).astype(BF)
        normed_grad += dot(swap(summed).astype(BF), w_ref[...], NT)
    scaled = normed_grad * gain
    out_ref[...] = (
        resid_grad_ref[...] + inverse * (scaled - n * jnp.mean(n * scaled, axis=1, keepdims=True))
    ).astype(BF)
    small_ref[...] = jnp.broadcast_to(jnp.sum(normed_grad * n, axis=0, keepdims=True), (16, D))


def project_back(grads, tokens, gain, w_query, w_key, w_value, resid_grad):
    return pl.pallas_call(
        project_back_kernel,
        out_shape=(
            jax.ShapeDtypeStruct((T, D), BF),
            jax.ShapeDtypeStruct((D, HQ * HD), BF),
            jax.ShapeDtypeStruct((D, HK * HD), BF),
            jax.ShapeDtypeStruct((D, HK * HD), BF),
            jax.ShapeDtypeStruct((16, D), F32),
        ),
        name="project_back",
    )(grads, tokens, gain, w_query, w_key, w_value, resid_grad)


def exchange(array):
    return lax.all_to_all(array, SEQ, 0, 0, tiled=True)


def shards(
    tokens, cotangent, segment, routes, attn_gain, w_query, w_key, w_value, w_output,
    expert_norm_gain, w_router, w_gate, w_up, w_down,
):
    tokens, cotangent = tokens[0], cotangent[0]
    attn_gain = attn_gain.reshape(1, D)
    expert_norm_gain = expert_norm_gain.reshape(1, D)
    router_rows = jnp.pad(w_router.T, ((0, 8 - EXPERTS), (0, 0)))

    received = exchange(project(tokens, segment, attn_gain, w_query, w_key, w_value))
    attended, full, log_total, q, k, cosine, sine = attend(received)
    attended = exchange(attended).reshape(D, T)
    output, resid_grad, grad_att, dwo, dwg, dwu, dwd, small_moe = experts(
        attended, tokens, cotangent, routes[0], expert_norm_gain, router_rows, w_output,
        w_gate, w_up, w_down,
    )
    grad_att = exchange(grad_att.reshape(HQ, HD, T))
    grads = exchange(
        attend_back(received, grad_att, full, log_total, q, k, cosine, sine)
    )
    token_grad, dwq, dwk, dwv, small_attn = project_back(
        grads, tokens, attn_gain, w_query, w_key, w_value, resid_grad
    )
    small = jnp.concatenate([small_moe[:9], small_attn[:7]], axis=0).astype(BF)
    dwq, dwk, dwv, dwo, dwg, dwu, dwd, small = (
        a.astype(F32) for a in lax.psum((dwq, dwk, dwv, dwo, dwg, dwu, dwd, small), AXES)
    )
    return (
        output[None], token_grad[None], small[9], dwq, dwk, dwv, dwo, small[8],
        small[:EXPERTS].T, dwg, dwu, dwd,
    )


def solution(mesh):
    fine = Mesh(mesh.devices.reshape(4, 2, 4, 2, 2), AXES)
    by_token = P(ROWS, SEQ, None)
    return jax.shard_map(
        shards,
        mesh=fine,
        in_specs=(by_token, by_token, P(ROWS, SEQ), by_token) + (P(),) * 10,
        out_specs=(by_token, by_token) + (P(),) * 10,
        check_vma=False,
    )
```

```python
import math

import jax
import jax.numpy as jnp
from jax import lax
from jax.experimental import pallas as pl
from jax.experimental.pallas import tpu as pltpu
from jax.sharding import Mesh
from jax.sharding import PartitionSpec as P

BF = jnp.bfloat16
F32 = jnp.float32
D = 1024
HQ = 16
HK = 8
HD = 64
FF = 512
EXPERTS = 3
T = 128
S = 2048
BLK = 256
NB = S // BLK
HALF = HD // 2
PAY = 3 * HD + 16
FC = 256
NF = FF // FC
NC = 8
NR = 16
FS = FF // NC
GU = 2 * FS * EXPERTS
ACTS = 3 * FS * EXPERTS
PIECE = 96
PART = 3 * PIECE
MINE = 2 * PIECE

EPSILON = 1e-06
THETA_BASE = 10000.0
SOFT_SCALE = 0.125
NEG_FILL = -1e30

AXES = ("y", "xh", "z", "xl", "core")
ROWS = ("y", "xh")
SEQ = ("z", "xl", "core")
CHIPS = ("z", "xl")
REST = ("y", "xh", "core")
RING = ("y", "core")
PLANE = ("z", "xh", "xl")
ALL = ("y", "z", "xh", "xl", "core")

NN = (((1,), (0,)), ((), ()))
NT = (((1,), (1,)), ((), ()))
TN = (((0,), (0,)), ((), ()))


def dot(a, b, dims=NN):
    return lax.dot_general(a, b, dims, preferred_element_type=F32)


def cost(us):
    return pl.CostEstimate(flops=int(us * 1e9), bytes_accessed=1 << 20, transcendentals=0)


def swap(a):
    return jnp.transpose(a, (1, 0))


def project_kernel(tok_ref, seg_ref, gain_ref, wq_ref, wk_ref, wv_ref, out_ref):
    x = tok_ref[...].astype(F32)
    inverse = lax.rsqrt(jnp.mean(x * x, axis=1, keepdims=True) + EPSILON)
    normed = (x * inverse * gain_ref[...].astype(F32)).astype(BF)
    ids = jnp.broadcast_to(seg_ref[...].astype(F32), (16, T)).astype(BF)
    for h in range(HQ):
        out_ref[h, 3 * HD :, :] = ids
    for j in range(4):
        q = swap(dot(normed, wq_ref[:, 256 * j : 256 * (j + 1)])).astype(BF)
        for i in range(4):
            out_ref[4 * j + i, 0:HD, :] = q[HD * i : HD * (i + 1)]
    for w_ref, at in ((wk_ref, HD), (wv_ref, 2 * HD)):
        for j in range(2):
            a = swap(dot(normed, w_ref[:, 256 * j : 256 * (j + 1)])).astype(BF)
            for i in range(4):
                part = a[HD * i : HD * (i + 1)]
                head = 2 * (4 * j + i)
                out_ref[head, at : at + HD, :] = part
                out_ref[head + 1, at : at + HD, :] = part


def project(tokens, segment, gain, w_query, w_key, w_value):
    return pl.pallas_call(
        project_kernel,
        out_shape=jax.ShapeDtypeStruct((HQ, PAY, T), BF),
        cost_estimate=cost(4),
        name="project",
    )(tokens, segment, gain, w_query, w_key, w_value)


def starts_of(x_ref):
    ids = x_ref[:, 3 * HD :, :].astype(F32)
    counts = [
        (jnp.sum(jnp.where(ids == float(s), 1.0, 0.0)) * (1.0 / 16)).astype(jnp.int32)
        for s in range(3)
    ]
    first = counts[0]
    second = first + counts[1]
    return first, second, second + counts[2]


def start_at(index, bounds):
    b1, b2, b3 = bounds
    return jnp.where(index >= b3, b3, jnp.where(index >= b2, b2, jnp.where(index >= b1, b1, 0)))


def joined(ref, i, at):
    return jnp.concatenate([ref[2 * i, at : at + HD, :], ref[2 * i + 1, at : at + HD, :]], axis=1)


def by_core(place_ref, a):
    even = place_ref[0] == 0
    low, high = a[:, :T], a[:, T:]
    return jnp.where(even, low, high).astype(BF), jnp.where(even, high, low).astype(BF)


def allowed_of(i, j, bounds):
    query = i * BLK + lax.broadcasted_iota(jnp.int32, (1, BLK), 1)
    start = start_at(query, bounds)
    key = j * BLK + lax.broadcasted_iota(jnp.int32, (BLK, BLK), 0)
    return (key >= start) & (key <= query)


def attend_kernel(place_ref, x_ref, att_ref, keep_ref, send_ref, full_ref, log_ref, q_ref, k_ref, cos_ref, sin_ref, kt_ref, v_ref):
    bounds = starts_of(x_ref)
    frequency = jnp.exp(
        lax.broadcasted_iota(jnp.int32, (HALF, 1), 0).astype(F32)
        * (-2.0 * math.log(THETA_BASE) / HD)
    )

    def turn_block(i, carry):
        index = i * BLK + lax.broadcasted_iota(jnp.int32, (1, BLK), 1)
        positions = (index - start_at(index, bounds)).astype(F32)
        angles = positions * frequency
        cosine, sine = jnp.cos(angles), jnp.sin(angles)
        cos_ref[i] = cosine
        sin_ref[i] = sine

        def turned(at):
            a = joined(x_ref, i, at).astype(F32)
            low, high = a[:HALF], a[HALF:]
            return jnp.concatenate(
                [low * cosine - high * sine, high * cosine + low * sine], axis=0
            )

        q_ref[i] = (turned(0).astype(BF).astype(F32) * SOFT_SCALE).astype(BF)
        k = turned(HD)
        k_ref[i] = k.astype(BF)
        kt_ref[i] = swap(k).astype(BF)
        v_ref[i] = joined(x_ref, i, 2 * HD)
        return carry

    lax.fori_loop(0, NB, turn_block, 0)

    def query_block(i, carry):
        first = start_at(i * BLK, bounds) // BLK
        q = q_ref[i]

        def key_block(j, running):
            top, total, acc = running
            scores = jnp.where(allowed_of(i, j, bounds), dot(kt_ref[j], q), NEG_FILL)
            new_top = jnp.maximum(top, jnp.max(scores, axis=0, keepdims=True))
            weights = jnp.exp(scores - new_top)
            scale = jnp.exp(top - new_top)
            total = total * scale + jnp.sum(weights, axis=0, keepdims=True)
            acc = acc * scale + dot(v_ref[j], weights.astype(BF))
            return new_top, total, acc

        begin = (
            jnp.full((1, BLK), NEG_FILL, F32),
            jnp.zeros((1, BLK), F32),
            jnp.zeros((HD, BLK), F32),
        )
        begin = key_block(i, begin)
        top, total, acc = lax.fori_loop(first, i, key_block, begin)
        attended = acc / total
        log_ref[i] = top + jnp.log(total)
        full_ref[i] = attended
        low = attended.astype(BF)
        att_ref[2 * i] = low[:, :T]
        att_ref[2 * i + 1] = low[:, T:]
        keep_ref[i], send_ref[i] = by_core(place_ref, attended)
        return carry

    lax.fori_loop(0, NB, query_block, 0)


PLACE = pl.BlockSpec(memory_space=pltpu.SMEM)


def in_vmem(count):
    return [pl.BlockSpec(memory_space=pltpu.VMEM)] * count


def attend(place, received):
    return pl.pallas_call(
        attend_kernel,
        in_specs=[PLACE] + in_vmem(1),
        out_shape=(
            jax.ShapeDtypeStruct((HQ, HD, T), BF),
            jax.ShapeDtypeStruct((NC, HD, T), BF),
            jax.ShapeDtypeStruct((NC, HD, T), BF),
            jax.ShapeDtypeStruct((NB, HD, BLK), F32),
            jax.ShapeDtypeStruct((NB, 1, BLK), F32),
            jax.ShapeDtypeStruct((NB, HD, BLK), BF),
            jax.ShapeDtypeStruct((NB, HD, BLK), BF),
            jax.ShapeDtypeStruct((NB, HALF, BLK), F32),
            jax.ShapeDtypeStruct((NB, HALF, BLK), F32),
        ),
        scratch_shapes=[pltpu.VMEM((NB, BLK, HD), BF), pltpu.VMEM((NB, HD, BLK), BF)],
        cost_estimate=cost(13),
        name="attend",
    )(place, received)


def attend_back_kernel(
    place_ref, x_ref, g_ref, full_ref, log_ref, q_ref, k_ref, cos_ref, sin_ref, keep_ref, send_ref,
    kt_ref, vt_ref, dk_ref, dv_ref,
):
    bounds = starts_of(x_ref)

    def prepare(i, carry):
        kt_ref[i] = swap(k_ref[i].astype(F32)).astype(BF)
        vt_ref[i] = swap(joined(x_ref, i, 2 * HD).astype(F32)).astype(BF)
        dk_ref[i] = jnp.zeros((HD, BLK), F32)
        dv_ref[i] = jnp.zeros((HD, BLK), F32)
        return carry

    lax.fori_loop(0, NB, prepare, 0)

    def turn_back(i, a):
        cosine, sine = cos_ref[i], sin_ref[i]
        low, high = a[:HALF], a[HALF:]
        return jnp.concatenate([low * cosine + high * sine, high * cosine - low * sine], axis=0)

    def put(i, at, a):
        rows = slice(at, at + HD)
        keep_ref[i, rows, :], send_ref[i, rows, :] = by_core(place_ref, a)

    def query_block(i, carry):
        first = start_at(i * BLK, bounds) // BLK
        q = q_ref[i]
        grad = joined(g_ref, i, 0)
        delta = jnp.sum(grad.astype(F32) * full_ref[i], axis=0, keepdims=True)
        log_total = log_ref[i]

        def key_block(j, dq):
            scores = dot(kt_ref[j], q)
            p = jnp.where(allowed_of(i, j, bounds), jnp.exp(scores - log_total), 0.0)
            dp = dot(vt_ref[j], grad)
            ds = (p * (dp - delta)).astype(BF)
            dv_ref[j] += dot(grad, p.astype(BF), NT)
            dk_ref[j] += dot(q, ds, NT)
            return dq + dot(k_ref[j], ds)

        dq = lax.fori_loop(first, i + 1, key_block, jnp.zeros((HD, BLK), F32))
        put(i, 0, turn_back(i, dq * SOFT_SCALE))
        return carry

    lax.fori_loop(0, NB, query_block, 0)

    def finish(i, carry):
        put(i, HD, turn_back(i, dk_ref[i]))
        put(i, 2 * HD, dv_ref[i])
        return carry

    lax.fori_loop(0, NB, finish, 0)


def attend_back(place, received, grad, full, log_total, q, k, cosine, sine):
    return pl.pallas_call(
        attend_back_kernel,
        in_specs=[PLACE] + in_vmem(8),
        out_shape=(
            jax.ShapeDtypeStruct((NC, 3 * HD, T), BF),
            jax.ShapeDtypeStruct((NC, 3 * HD, T), BF),
        ),
        scratch_shapes=[
            pltpu.VMEM((NB, BLK, HD), BF),
            pltpu.VMEM((NB, BLK, HD), BF),
            pltpu.VMEM((NB, HD, BLK), F32),
            pltpu.VMEM((NB, HD, BLK), F32),
        ],
        cost_estimate=cost(13),
        name="attend_back",
    )(place, received, grad, full, log_total, q, k, cosine, sine)


def normed_kernel(tok_ref, gain_ref, out_ref):
    x = tok_ref[...].astype(F32)
    inverse = lax.rsqrt(jnp.mean(x * x, axis=1, keepdims=True) + EPSILON)
    out_ref[...] = swap(x * inverse * gain_ref[...].astype(F32)).astype(BF)


def normed_columns(tokens, gain):
    return pl.pallas_call(
        normed_kernel, out_shape=jax.ShapeDtypeStruct((D, T), BF), cost_estimate=cost(2), name="normed_columns"
    )(tokens, gain)


def resid_kernel(
    att_ref, tok_ref, routes_ref, gain_ref, wr_ref, wo_ref, resid_ref, moe_ref, moe_t_ref, combine_ref
):
    attended = swap(att_ref[...].astype(F32)).astype(BF)
    resid = tok_ref[...].astype(F32) + dot(attended, wo_ref[...])
    inverse = lax.rsqrt(jnp.mean(resid * resid, axis=1, keepdims=True) + EPSILON)
    normed = resid * inverse * gain_ref[...].astype(F32)
    moe_low = normed.astype(BF)
    resid_ref[...] = resid
    moe_ref[...] = moe_low
    moe_t_ref[...] = swap(normed).astype(BF)
    logits = dot(moe_low, wr_ref[...], NT)
    lane = lax.broadcasted_iota(jnp.int32, (T, T), 1)
    r0, r1 = routes_ref[:, 0:1], routes_ref[:, 1:2]
    l0 = jnp.sum(jnp.where(lane[:, :8] == r0, logits, 0.0), axis=1, keepdims=True)
    l1 = jnp.sum(jnp.where(lane[:, :8] == r1, logits, 0.0), axis=1, keepdims=True)
    top = jnp.maximum(l0, l1)
    e0, e1 = jnp.exp(l0 - top), jnp.exp(l1 - top)
    total = e0 + e1
    combine_ref[...] = jnp.where(lane == r0, e0 / total, 0.0) + jnp.where(
        lane == r1, e1 / total, 0.0
    )


def residual(attended, tokens, routes, gain, w_router, w_output):
    return pl.pallas_call(
        resid_kernel,
        out_shape=(
            jax.ShapeDtypeStruct((T, D), F32),
            jax.ShapeDtypeStruct((T, D), BF),
            jax.ShapeDtypeStruct((D, T), BF),
            jax.ShapeDtypeStruct((T, T), F32),
        ),
        cost_estimate=cost(4),
        name="residual",
    )(attended, tokens, routes, gain, w_router, w_output)


def experts_kernel(
    resid_ref, moe_ref, combine_ref, cot_ref, gain_ref, wr_ref, wo_ref, wg_ref, wu_ref, wd_ref,
    out_ref, resid_grad_ref, grad_att_ref, grad_t_ref, acts_ref, small_ref,
    mix_ref, moe_grad_ref, cgrad_ref,
):
    e, f = pl.program_id(0), pl.program_id(1)
    lane = lax.broadcasted_iota(jnp.int32, (T, T), 1)

    @pl.when((e == 0) & (f == 0))
    def _():
        mix_ref[...] = resid_ref[...]
        moe_grad_ref[...] = jnp.zeros_like(moe_grad_ref)
        cgrad_ref[...] = jnp.zeros_like(cgrad_ref)

    moe_low = moe_ref[...]
    grad_out = cot_ref[...].astype(F32)
    combine = jnp.sum(jnp.where(lane == e, combine_ref[...], 0.0), axis=1, keepdims=True)
    expert_grad = (combine * grad_out).astype(BF)
    gate = dot(moe_low, wg_ref[0])
    up = dot(moe_low, wu_ref[0])
    act_grad = dot(expert_grad, wd_ref[0], NT)
    sig = 1.0 / (1.0 + jnp.exp(-gate))
    silu = gate * sig
    act_low = (silu * up).astype(BF)
    down = dot(act_low, wd_ref[0])
    mix_ref[...] += combine * down
    cgrad_ref[...] += jnp.where(lane == e, jnp.sum(grad_out * down, axis=1, keepdims=True), 0.0)
    gate_grad = act_grad * up * (sig * (1.0 + gate * (1.0 - sig)))
    up_grad = act_grad * silu
    moe_grad_ref[...] += dot(gate_grad.astype(BF), wg_ref[0], NT) + dot(
        up_grad.astype(BF), wu_ref[0], NT
    )
    gate_t = swap(gate_grad).astype(BF)
    up_t = swap(up_grad).astype(BF)
    act_t = swap(combine * act_low.astype(F32)).astype(BF)
    at_gu = pl.multiple_of(2 * FS * e, FS)
    at_down = pl.multiple_of(GU + FS * e, FS)
    for i in range(FC // FS):
        j = f * (FC // FS) + i
        acts_ref[j, pl.ds(at_gu, FS), :] = gate_t[FS * i : FS * (i + 1)]
        acts_ref[j, pl.ds(at_gu + FS, FS), :] = up_t[FS * i : FS * (i + 1)]
        acts_ref[j, pl.ds(at_down, FS), :] = act_t[FS * i : FS * (i + 1)]

    @pl.when((e == EXPERTS - 1) & (f == NF - 1))
    def _():
        out_ref[...] = mix_ref[...].astype(BF)
        weights, cgrad = combine_ref[...], cgrad_ref[...]
        mean = jnp.sum(weights * cgrad, axis=1, keepdims=True)
        logit_grad = (weights * (cgrad - mean)).astype(BF)
        small_ref[0:8, :] = dot(logit_grad, moe_low, TN)[0:8]
        moe_grad = moe_grad_ref[...] + dot(logit_grad[:, 0:8], wr_ref[...])
        resid = resid_ref[...]
        inverse = lax.rsqrt(jnp.mean(resid * resid, axis=1, keepdims=True) + EPSILON)
        n = resid * inverse
        small_ref[8:16, :] = jnp.broadcast_to(jnp.sum(moe_grad * n, axis=0, keepdims=True), (8, D))
        scaled = moe_grad * gain_ref[...].astype(F32)
        resid_grad = grad_out + inverse * (
            scaled - n * jnp.mean(n * scaled, axis=1, keepdims=True)
        )
        resid_grad_ref[...] = resid_grad
        grad_t_ref[...] = swap(resid_grad).astype(BF)
        grad_att_ref[...] = dot(wo_ref[...], resid_grad.astype(BF), NT).astype(BF)


def experts(resid, moe_low, combine, cotangent, gain, w_router, w_output, w_gate, w_up, w_down):
    def whole(*shape):
        return pl.BlockSpec(shape, lambda e, f: (0,) * len(shape))

    def columns():
        return pl.BlockSpec((1, D, FC), lambda e, f: (e, 0, f))

    def rows():
        return pl.BlockSpec((1, FC, D), lambda e, f: (e, f, 0))

    return pl.pallas_call(
        experts_kernel,
        grid=(EXPERTS, NF),
        in_specs=[
            whole(T, D), whole(T, D), whole(T, T), whole(T, D), whole(1, D), whole(8, D),
            whole(D, D), columns(), columns(), rows(),
        ],
        out_specs=(
            whole(T, D), whole(T, D), whole(D, T), whole(D, T), whole(NC, ACTS, T), whole(16, D),
        ),
        out_shape=(
            jax.ShapeDtypeStruct((T, D), BF),
            jax.ShapeDtypeStruct((T, D), F32),
            jax.ShapeDtypeStruct((D, T), BF),
            jax.ShapeDtypeStruct((D, T), BF),
            jax.ShapeDtypeStruct((NC, ACTS, T), BF),
            jax.ShapeDtypeStruct((16, D), F32),
        ),
        scratch_shapes=[
            pltpu.VMEM((T, D), F32),
            pltpu.VMEM((T, D), F32),
            pltpu.VMEM((T, T), F32),
        ],
        cost_estimate=cost(13),
        name="experts",
    )(resid, moe_low, combine, cotangent, gain, w_router, w_output, w_gate, w_up, w_down)


def side_by_side(ref, i, j):
    return jnp.concatenate([ref[i], ref[j]], axis=1)


def expert_weights_kernel(acts_ref, moe_ref, cot_ref, out_ref, wide_ref, down_ref):
    for b in range(0, NC, 2):
        acts = side_by_side(acts_ref, b, b + 1)
        wide = dot(side_by_side(moe_ref, b, b + 1), acts[0:GU], NT)
        down = dot(acts[GU:], jnp.concatenate([cot_ref[b], cot_ref[b + 1]], axis=0))
        if b == 0:
            wide_ref[...] = wide
            down_ref[...] = down
        else:
            wide_ref[...] += wide
            down_ref[...] += down
    for i in range(NR):
        for e in range(EXPERTS):
            out_ref[i, 64 * e : 64 * (e + 1), :] = wide_ref[
                64 * i : 64 * (i + 1), 128 * e : 128 * (e + 1)
            ].astype(BF)
        half, lanes = 96 * (i % 2), 128 * (i // 2)
        out_ref[i, 192:288, :] = down_ref[half : half + 96, lanes : lanes + 128].astype(BF)


def expert_weights(acts, moe, cotangent):
    return pl.pallas_call(
        expert_weights_kernel,
        out_shape=jax.ShapeDtypeStruct((NR, PART, T), BF),
        scratch_shapes=[pltpu.VMEM((D, GU), F32), pltpu.VMEM((FS * EXPERTS, D), F32)],
        cost_estimate=cost(5),
        name="expert_weights",
    )(acts, moe, cotangent)


def project_weights_kernel(
    place_ref, mine_ref, theirs_ref, att_ref, att_other_ref,
    normed0_ref, normed1_ref, normed2_ref, normed3_ref, grad_ref,
    back_ref, out_ref, heads_ref,
):
    core, z, xl = place_ref[0], place_ref[1], place_ref[2]
    own = pl.ds(pl.multiple_of(HD * core, HD), HD)
    partner = pl.ds(pl.multiple_of(HD * (1 - core), HD), HD)
    for b in range(NC):
        back_ref[b, own, :] = mine_ref[b, 0:HD, :]
        back_ref[b, partner, :] = theirs_ref[b, 0:HD, :]
        back_ref[b, 2 * HD :, :] = (
            mine_ref[b, HD:, :].astype(F32) + theirs_ref[b, HD:, :].astype(F32)
        ).astype(BF)
        heads_ref[b, own, :] = att_ref[b]
        heads_ref[b, partner, :] = att_other_ref[b]
    total = jnp.zeros((D, 4 * HD), F32)
    o = jnp.zeros((2 * HD, D), F32)
    for back, normed_ref in enumerate((normed0_ref, normed1_ref, normed2_ref, normed3_ref)):
        chip = 2 * ((z - back) & 3)
        near, far = chip + xl, chip + 1 - xl
        total += dot(side_by_side(normed_ref, 0, 1), side_by_side(back_ref, near, far), NT)
    for b in range(0, NC, 2):
        mine, later = 2 * b + core, 2 * b + 2 + core
        o += dot(side_by_side(heads_ref, b, b + 1), side_by_side(grad_ref, mine, later), NT)
    low, o_low = total.astype(BF), o.astype(BF)
    for i in range(NR):
        out_ref[i, 0:64, :] = low[64 * i : 64 * (i + 1), 0:128]
        out_ref[i, 64:128, :] = low[64 * i : 64 * (i + 1), 128:256]
        half, lanes = 64 * (i % 2), 128 * (i // 2)
        out_ref[i, 128:192, :] = o_low[half : half + 64, lanes : lanes + 128]


def project_weights(place, mine, theirs, attended, attended_other, normed, grad):
    return pl.pallas_call(
        project_weights_kernel,
        in_specs=[PLACE] + in_vmem(9),
        out_shape=(
            jax.ShapeDtypeStruct((NC, 4 * HD, T), BF),
            jax.ShapeDtypeStruct((NR, MINE, T), BF),
        ),
        scratch_shapes=[pltpu.VMEM((NC, 2 * HD, T), BF)],
        cost_estimate=cost(5),
        name="project_weights",
    )(place, mine, theirs, attended, attended_other, *normed, grad)


def project_back_kernel(
    g_ref, tok_ref, gain_ref, wq_ref, wk_ref, wv_ref, resid_grad_ref, small_ref, out_ref, sums_ref
):
    x = tok_ref[...].astype(F32)
    gain = gain_ref[...].astype(F32)
    inverse = lax.rsqrt(jnp.mean(x * x, axis=1, keepdims=True) + EPSILON)
    n = x * inverse

    def rows(first, last):
        a = g_ref[:, first:last, :]
        return swap(a.reshape(NC * (last - first), T).astype(F32)).astype(BF)

    normed_grad = dot(rows(0, 2 * HD), wq_ref[...], NT)
    normed_grad += dot(rows(2 * HD, 3 * HD), wk_ref[...], NT)
    normed_grad += dot(rows(3 * HD, 4 * HD), wv_ref[...], NT)
    scaled = normed_grad * gain
    out_ref[...] = (
        resid_grad_ref[...] + inverse * (scaled - n * jnp.mean(n * scaled, axis=1, keepdims=True))
    ).astype(BF)
    gain_grad = jnp.sum(normed_grad * n, axis=0, keepdims=True)
    row = lax.broadcasted_iota(jnp.int32, (8, D), 0)
    sums_ref[...] = jnp.where(
        row < EXPERTS, small_ref[0:8], jnp.where(row == EXPERTS, small_ref[8:16], gain_grad)
    )


def project_back(grads, tokens, gain, w_query, w_key, w_value, resid_grad, small):
    return pl.pallas_call(
        project_back_kernel,
        out_shape=(jax.ShapeDtypeStruct((T, D), BF), jax.ShapeDtypeStruct((8, D), F32)),
        cost_estimate=cost(5),
        name="project_back",
    )(grads, tokens, gain, w_query, w_key, w_value, resid_grad, small)


def assemble_kernel(
    g0_ref, g1_ref, g2_ref, p0_ref, p1_ref,
    q_ref, k_ref, v_ref, o_ref, g_ref, u_ref, d_ref,
):
    core = pl.program_id(2)
    low_half = lax.broadcasted_iota(jnp.int32, (64, T), 1) < 64

    def rows(refs, pick, first, last):
        found = []
        for at, ref in enumerate(refs):
            begin, end = max(first - PIECE * at, 0), min(last - PIECE * at, PIECE)
            if begin < end:
                found.append(pick(ref)[begin:end])
        whole = found[0] if len(found) == 1 else jnp.concatenate(found, axis=0)
        return whole.astype(F32)

    def expert_rows(j, first, last):
        refs = (g0_ref, g1_ref, g2_ref)
        return rows(refs, lambda ref: ref[j // 2, 0, 0, 0, j % 2], first, last)

    def project_rows(j, first, last):
        return rows((p0_ref, p1_ref), lambda ref: ref[0, j // 2, 0, j % 2, 0], first, last)

    def turned(a):
        return pltpu.roll(a, 64, 1)

    for m in range(NC // 2):
        tile = slice(T * m, T * (m + 1))
        for e in range(EXPERTS):
            a, b = (expert_rows(2 * m + i, 64 * e, 64 * (e + 1)) for i in range(2))
            g_ref[e, :, tile] = jnp.where(low_half, a, turned(b))
            u_ref[e, :, tile] = jnp.where(low_half, turned(a), b)
        a, b = (project_rows(2 * m + i, 64, 128) for i in range(2))
        k_ref[:, tile] = jnp.where(low_half, a, turned(b))
        v_ref[:, tile] = jnp.where(low_half, turned(a), b)
    for j in range(NC):
        q_ref[:, T * j : T * (j + 1)] = project_rows(j, 0, 64)
        o_ref[j, core] = project_rows(j, 128, 192)

    @pl.when(core == 0)
    def _():
        for j in range(NC):
            a = expert_rows(j, 192, 288)
            d_ref[0, j] = a[0:64]
            d_ref[1, j, 0:32] = a[64:96]

    @pl.when(core == 1)
    def _():
        for j in range(NC):
            a = expert_rows(j, 192, 288)
            d_ref[1, j, 32:64] = a[0:32]
            d_ref[2, j] = a[32:96]


def assemble(gathered):
    def experts_of(at):
        return pl.BlockSpec((4, 1, 1, 1, 2, PIECE, T), lambda a, b, c: (0, a, b, c, 0, at, 0))

    def project_of(at):
        return pl.BlockSpec((1, 4, 1, 2, 1, PIECE, T), lambda a, b, c: (a, 0, b, 0, c, at, 0))

    def rows(width):
        return pl.BlockSpec((64, width), lambda a, b, c: (4 * a + 2 * b + c, 0))

    def stack():
        return pl.BlockSpec((EXPERTS, 64, FF), lambda a, b, c: (0, 4 * a + 2 * b + c, 0))

    return pl.pallas_call(
        assemble_kernel,
        grid=(4, 2, 2),
        in_specs=[experts_of(0), experts_of(1), experts_of(2), project_of(3), project_of(4)],
        out_specs=(
            rows(D), rows(FF), rows(FF),
            pl.BlockSpec((NC, 2, HD, T), lambda a, b, c: (0, 0, 0, 2 * a + b)),
            stack(), stack(),
            pl.BlockSpec((EXPERTS, NC, FS, T), lambda a, b, c: (0, 0, 0, 2 * a + b)),
        ),
        out_shape=(
            jax.ShapeDtypeStruct((D, D), F32),
            jax.ShapeDtypeStruct((D, FF), F32),
            jax.ShapeDtypeStruct((D, FF), F32),
            jax.ShapeDtypeStruct((NC, 2, HD, D), F32),
            jax.ShapeDtypeStruct((EXPERTS, D, FF), F32),
            jax.ShapeDtypeStruct((EXPERTS, D, FF), F32),
            jax.ShapeDtypeStruct((EXPERTS, NC, FS, D), F32),
        ),
        cost_estimate=cost(20),
        name="assemble",
    )(*(gathered,) * 5)


def exchange(array, axes=SEQ):
    return lax.all_to_all(array, axes, 0, 0, tiled=True)


def swapped(array, axis):
    return lax.ppermute(array, axis, [(0, 1), (1, 0)])


def gather(array, axes):
    return lax.all_gather(array, axes, axis=0)


def spread_sum(part, axes, count):
    return jnp.sum(exchange(jnp.broadcast_to(part[None], (count, *part.shape)), axes), axis=0)


def part_sum(parts, axes):
    return jnp.sum(exchange(parts, axes).astype(F32), axis=0).astype(BF)


def after(array, *others):
    return lax.optimization_barrier((array, *others))


def shards(
    tokens, cotangent, segment, routes, attn_gain, w_query, w_key, w_value, w_output,
    expert_norm_gain, w_router, w_gate, w_up, w_down,
):
    tokens, cotangent = tokens[0], cotangent[0]
    attn_gain = attn_gain.reshape(1, D)
    expert_norm_gain = expert_norm_gain.reshape(1, D)
    router_rows = jnp.pad(w_router.T, ((0, 8 - EXPERTS), (0, 0)))
    place = jnp.stack([lax.axis_index(a) for a in ("core", "z", "xl")]).astype(jnp.int32)

    cot_all = gather(cotangent, RING)
    received = exchange(project(tokens, segment, attn_gain, w_query, w_key, w_value))
    normed = normed_columns(tokens, attn_gain)
    normed = jnp.stack([normed, swapped(normed, "xl")])
    received, normed = after(received, normed)
    normed_all = [normed] + [
        lax.ppermute(normed, "z", [(i, (i + back) % 4) for i in range(4)]) for back in (1, 2, 3)
    ]
    attended, att_mine, att_sent, full, log_total, q, k, cosine, sine = attend(place, received)
    attended, cot_all = after(attended, cot_all)
    attended = exchange(attended).reshape(D, T)
    att_theirs = swapped(att_sent, "core")
    resid, moe_low, moe_columns, combine = residual(
        attended, tokens, routes[0], expert_norm_gain, router_rows, w_output
    )
    moe_all = gather(moe_columns, RING)
    output, resid_grad, grad_att, grad_columns, acts, small = experts(
        resid, moe_low, combine, cotangent, expert_norm_gain, router_rows, w_output,
        w_gate, w_up, w_down,
    )
    acts = exchange(acts, RING)
    grad_all = gather(grad_columns, SEQ)
    grad_att, acts, moe_all = after(grad_att, acts, moe_all)
    grad_att = exchange(grad_att.reshape(HQ, HD, T))
    parts = expert_weights(acts, moe_all, cot_all)
    mine, sent = attend_back(place, received, grad_att, full, log_total, q, k, cosine, sine)
    expert_part = part_sum(parts, PLANE)
    grads, weights = project_weights(
        place, mine, swapped(sent, "core"), att_mine, att_theirs, normed_all, grad_all
    )
    project_part = part_sum(weights, REST)
    gathered = gather(jnp.concatenate([expert_part, project_part], axis=0), ALL)
    grads, project_part = after(grads, project_part)
    token_grad, small = project_back(
        exchange(grads, CHIPS), tokens, attn_gain, w_query, w_key, w_value, resid_grad, small
    )
    small = spread_sum(spread_sum(small, REST, NR), CHIPS, NC)
    dwq, dwk, dwv, dwo, dwg, dwu, dwd = assemble(
        gathered.reshape(4, 4, 2, 2, 2, PART + MINE, T)
    )
    return (
        output[None], token_grad[None], small[4], dwq, dwk, dwv, dwo.reshape(D, D), small[3],
        small[:EXPERTS].T, dwg, dwu, dwd.reshape(EXPERTS, FF, D),
    )


def solution(mesh):
    fine = Mesh(mesh.devices.reshape(4, 2, 4, 2, 2), AXES)
    by_token = P(ROWS, SEQ, None)
    return jax.shard_map(
        shards,
        mesh=fine,
        in_specs=(by_token, by_token, P(ROWS, SEQ), by_token) + (P(),) * 10,
        out_specs=(by_token, by_token) + (P(),) * 10,
        check_vma=False,
    )
```

```python
import functools
import math

import jax
import jax.numpy as jnp
from jax import lax
from jax.experimental import pallas as pl
from jax.experimental.pallas import tpu as pltpu
from jax.sharding import Mesh
from jax.sharding import PartitionSpec as P

BF = jnp.bfloat16
F32 = jnp.float32
D = 1024
HQ = 16
HK = 8
HD = 64
FF = 512
EXPERTS = 3
T = 128
S = 2048
BLK = 256
NB = S // BLK
WINDOW = 1024 // BLK + 1
HALF = HD // 2
PAY = 3 * HD + 16
FC = 512
NF = FF // FC
NC = 8
NR = 16
FS = FF // NC
GU = 2 * FS * EXPERTS
ACTS = 3 * FS * EXPERTS
PIECE = 96
PART = 3 * PIECE
MINE = 2 * PIECE

EPSILON = 1e-06
THETA_BASE = 10000.0
SOFT_SCALE = 0.125
NEG_FILL = -1e30

AXES = ("y", "xh", "z", "xl", "core")
ROWS = ("y", "xh")
SEQ = ("z", "xl", "core")
COLUMN = ("z", "core")
REST = ("y", "xh", "xl")
RING = ("y", "core")
PLANE = ("z", "xh", "xl")
ALL = ("y", "z", "xh", "xl", "core")

NN = (((1,), (0,)), ((), ()))
NT = (((1,), (1,)), ((), ()))
TN = (((0,), (0,)), ((), ()))


def device_of(head):
    return head // 4 * 4 + head % 2 * 2 + head // 2 % 2


def dot(a, b, dims=NN):
    return lax.dot_general(a, b, dims, preferred_element_type=F32)


def cost(us):
    return pl.CostEstimate(flops=int(us * 1e9), bytes_accessed=1 << 20, transcendentals=0)


def swap(a):
    return jnp.transpose(a, (1, 0))


def project_kernel(tok_ref, seg_ref, gain_ref, wq_ref, wk_ref, wv_ref, out_ref):
    x = tok_ref[...].astype(F32)
    inverse = lax.rsqrt(jnp.mean(x * x, axis=1, keepdims=True) + EPSILON)
    normed = (x * inverse * gain_ref[...].astype(F32)).astype(BF)
    ids = jnp.broadcast_to(seg_ref[...].astype(F32), (16, T)).astype(BF)
    for h in range(HQ):
        out_ref[h, 3 * HD :, :] = ids
    for j in range(4):
        q = swap(dot(normed, wq_ref[:, 256 * j : 256 * (j + 1)])).astype(BF)
        for i in range(4):
            out_ref[device_of(4 * j + i), 0:HD, :] = q[HD * i : HD * (i + 1)]
    for w_ref, at in ((wk_ref, HD), (wv_ref, 2 * HD)):
        for j in range(2):
            a = swap(dot(normed, w_ref[:, 256 * j : 256 * (j + 1)])).astype(BF)
            for i in range(4):
                part = a[HD * i : HD * (i + 1)]
                head = 2 * (4 * j + i)
                out_ref[device_of(head), at : at + HD, :] = part
                out_ref[device_of(head + 1), at : at + HD, :] = part


def project(tokens, segment, gain, w_query, w_key, w_value):
    return pl.pallas_call(
        project_kernel,
        out_shape=jax.ShapeDtypeStruct((HQ, PAY, T), BF),
        cost_estimate=cost(4),
        name="project",
    )(tokens, segment, gain, w_query, w_key, w_value)


def starts_of(x_ref):
    ids = x_ref[:, 3 * HD :, :].astype(F32)
    counts = [
        (jnp.sum(jnp.where(ids == float(s), 1.0, 0.0)) * (1.0 / 16)).astype(jnp.int32)
        for s in range(3)
    ]
    first = counts[0]
    second = first + counts[1]
    return first, second, second + counts[2]


def start_at(index, bounds):
    b1, b2, b3 = bounds
    return jnp.where(index >= b3, b3, jnp.where(index >= b2, b2, jnp.where(index >= b1, b1, 0)))


def joined(ref, i, at):
    return jnp.concatenate([ref[2 * i, at : at + HD, :], ref[2 * i + 1, at : at + HD, :]], axis=1)


def put_pair(place_ref, keep_ref, send_ref, i, rows, a):
    low = a.astype(BF)
    for ref, half in ((keep_ref, place_ref[2]), (send_ref, 1 - place_ref[2])):

        @pl.when((i & 1) == half)
        def _(ref=ref):
            ref[2 * (i // 2), rows, :] = low[:, :T]
            ref[2 * (i // 2) + 1, rows, :] = low[:, T:]


def windowed(i, bounds, body):
    blocks = i + 1 - start_at(i * BLK, bounds) // BLK
    for window in range(1, WINDOW + 1):
        pl.when(blocks == window)(functools.partial(body, window))


def masks_of(i, bounds):
    query = i * BLK + lax.broadcasted_iota(jnp.int32, (1, BLK), 1)
    first = start_at(query, bounds) - i * BLK
    key = lax.broadcasted_iota(jnp.int32, (BLK, BLK), 0)

    def allowed(back):
        inside = key >= first + back * BLK
        return inside & (key <= query - i * BLK) if back == 0 else inside

    return allowed


def attend_kernel(place_ref, x_ref, att_ref, keep_ref, send_ref, full_ref, log_ref, q_ref, k_ref, cos_ref, sin_ref, kt_ref, v_ref):
    bounds = starts_of(x_ref)
    frequency = jnp.exp(
        lax.broadcasted_iota(jnp.int32, (HALF, 1), 0).astype(F32)
        * (-2.0 * math.log(THETA_BASE) / HD)
    )

    def turn_block(i, carry):
        index = i * BLK + lax.broadcasted_iota(jnp.int32, (1, BLK), 1)
        positions = (index - start_at(index, bounds)).astype(F32)
        angles = positions * frequency
        cosine, sine = jnp.cos(angles), jnp.sin(angles)
        cos_ref[i] = cosine
        sin_ref[i] = sine

        def turned(at):
            a = joined(x_ref, i, at).astype(F32)
            low, high = a[:HALF], a[HALF:]
            return jnp.concatenate(
                [low * cosine - high * sine, high * cosine + low * sine], axis=0
            )

        q_ref[i] = (turned(0).astype(BF).astype(F32) * SOFT_SCALE).astype(BF)
        k = turned(HD)
        k_ref[i] = k.astype(BF)
        kt_ref[i] = swap(k).astype(BF)
        v_ref[i] = joined(x_ref, i, 2 * HD)
        return carry

    lax.fori_loop(0, NB, turn_block, 0, unroll=True)

    def query_block(i, carry):
        q = q_ref[i]
        allowed = masks_of(i, bounds)

        def attend_window(window):
            scores = [
                jnp.where(allowed(back), dot(kt_ref[i - back], q), NEG_FILL)
                for back in range(window)
            ]
            top = jnp.max(functools.reduce(jnp.maximum, scores), axis=0, keepdims=True)
            weights = [jnp.exp(a - top) for a in scores]
            total = jnp.sum(functools.reduce(jnp.add, weights), axis=0, keepdims=True)
            acc = functools.reduce(
                jnp.add, [dot(v_ref[i - back], weights[back].astype(BF)) for back in range(window)]
            )
            attended = acc / total
            log_ref[i] = top + jnp.log(total)
            full_ref[i] = attended
            low = attended.astype(BF)
            att_ref[2 * i] = low[:, :T]
            att_ref[2 * i + 1] = low[:, T:]
            put_pair(place_ref, keep_ref, send_ref, i, slice(0, HD), attended)

        windowed(i, bounds, attend_window)
        return carry

    lax.fori_loop(0, NB, query_block, 0)


PLACE = pl.BlockSpec(memory_space=pltpu.SMEM)


def in_vmem(count):
    return [pl.BlockSpec(memory_space=pltpu.VMEM)] * count


def attend(place, received):
    return pl.pallas_call(
        attend_kernel,
        in_specs=[PLACE] + in_vmem(1),
        out_shape=(
            jax.ShapeDtypeStruct((HQ, HD, T), BF),
            jax.ShapeDtypeStruct((NC, HD, T), BF),
            jax.ShapeDtypeStruct((NC, HD, T), BF),
            jax.ShapeDtypeStruct((NB, HD, BLK), F32),
            jax.ShapeDtypeStruct((NB, 1, BLK), F32),
            jax.ShapeDtypeStruct((NB, HD, BLK), BF),
            jax.ShapeDtypeStruct((NB, HD, BLK), BF),
            jax.ShapeDtypeStruct((NB, HALF, BLK), F32),
            jax.ShapeDtypeStruct((NB, HALF, BLK), F32),
        ),
        scratch_shapes=[pltpu.VMEM((NB, BLK, HD), BF), pltpu.VMEM((NB, HD, BLK), BF)],
        cost_estimate=cost(13),
        name="attend",
    )(place, received)


def attend_back_kernel(
    place_ref, x_ref, g_ref, full_ref, log_ref, q_ref, k_ref, cos_ref, sin_ref, keep_ref, send_ref,
    kt_ref, vt_ref, dk_ref, dv_ref,
):
    bounds = starts_of(x_ref)

    def prepare(i, carry):
        kt_ref[i] = swap(k_ref[i].astype(F32)).astype(BF)
        vt_ref[i] = swap(joined(x_ref, i, 2 * HD).astype(F32)).astype(BF)
        dk_ref[i] = jnp.zeros((HD, BLK), F32)
        dv_ref[i] = jnp.zeros((HD, BLK), F32)
        return carry

    lax.fori_loop(0, NB, prepare, 0, unroll=True)

    def turn_back(i, a):
        cosine, sine = cos_ref[i], sin_ref[i]
        low, high = a[:HALF], a[HALF:]
        return jnp.concatenate([low * cosine + high * sine, high * cosine - low * sine], axis=0)

    def put(i, at, a):
        put_pair(place_ref, keep_ref, send_ref, i, slice(at, at + HD), a)

    def query_block(i, carry):
        q = q_ref[i]
        allowed = masks_of(i, bounds)
        grad = joined(g_ref, i, 0)
        delta = jnp.sum(grad.astype(F32) * full_ref[i], axis=0, keepdims=True)
        log_total = log_ref[i]

        def back_window(window):
            dq = jnp.zeros((HD, BLK), F32)
            for back in range(window):
                j = i - back
                scores = dot(kt_ref[j], q)
                p = jnp.where(allowed(back), jnp.exp(scores - log_total), 0.0)
                dp = dot(vt_ref[j], grad)
                ds = (p * (dp - delta)).astype(BF)
                dv_ref[j] += dot(grad, p.astype(BF), NT)
                dk_ref[j] += dot(q, ds, NT)
                dq += dot(k_ref[j], ds)
            put(i, 0, turn_back(i, dq * SOFT_SCALE))

        windowed(i, bounds, back_window)
        return carry

    lax.fori_loop(0, NB, query_block, 0)

    def finish(i, carry):
        put(i, HD, turn_back(i, dk_ref[i]))
        put(i, 2 * HD, dv_ref[i])
        return carry

    lax.fori_loop(0, NB, finish, 0, unroll=True)


def attend_back(place, received, grad, full, log_total, q, k, cosine, sine):
    return pl.pallas_call(
        attend_back_kernel,
        in_specs=[PLACE] + in_vmem(8),
        out_shape=(
            jax.ShapeDtypeStruct((NC, 3 * HD, T), BF),
            jax.ShapeDtypeStruct((NC, 3 * HD, T), BF),
        ),
        scratch_shapes=[
            pltpu.VMEM((NB, BLK, HD), BF),
            pltpu.VMEM((NB, BLK, HD), BF),
            pltpu.VMEM((NB, HD, BLK), F32),
            pltpu.VMEM((NB, HD, BLK), F32),
        ],
        cost_estimate=cost(13),
        name="attend_back",
    )(place, received, grad, full, log_total, q, k, cosine, sine)


def normed_kernel(tok_ref, gain_ref, out_ref):
    x = tok_ref[...].astype(F32)
    inverse = lax.rsqrt(jnp.mean(x * x, axis=1, keepdims=True) + EPSILON)
    out_ref[...] = swap(x * inverse * gain_ref[...].astype(F32)).astype(BF)


def normed_columns(tokens, gain):
    return pl.pallas_call(
        normed_kernel, out_shape=jax.ShapeDtypeStruct((D, T), BF), cost_estimate=cost(2), name="normed_columns"
    )(tokens, gain)


def resid_kernel(
    att_ref, tok_ref, routes_ref, gain_ref, wr_ref, wo_ref, resid_ref, moe_ref, moe_t_ref, combine_ref
):
    heads = [att_ref[device_of(h)] for h in range(HQ)]
    attended = swap(jnp.concatenate(heads, axis=0).astype(F32)).astype(BF)
    resid = tok_ref[...].astype(F32) + dot(attended, wo_ref[...])
    inverse = lax.rsqrt(jnp.mean(resid * resid, axis=1, keepdims=True) + EPSILON)
    normed = resid * inverse * gain_ref[...].astype(F32)
    moe_low = normed.astype(BF)
    resid_ref[...] = resid
    moe_ref[...] = moe_low
    moe_t_ref[...] = swap(normed).astype(BF)
    logits = dot(moe_low, wr_ref[...], NT)
    lane = lax.broadcasted_iota(jnp.int32, (T, T), 1)
    r0, r1 = routes_ref[:, 0:1], routes_ref[:, 1:2]
    l0 = jnp.sum(jnp.where(lane[:, :8] == r0, logits, 0.0), axis=1, keepdims=True)
    l1 = jnp.sum(jnp.where(lane[:, :8] == r1, logits, 0.0), axis=1, keepdims=True)
    top = jnp.maximum(l0, l1)
    e0, e1 = jnp.exp(l0 - top), jnp.exp(l1 - top)
    total = e0 + e1
    combine_ref[...] = jnp.where(lane == r0, e0 / total, 0.0) + jnp.where(
        lane == r1, e1 / total, 0.0
    )


def residual(attended, tokens, routes, gain, w_router, w_output):
    return pl.pallas_call(
        resid_kernel,
        out_shape=(
            jax.ShapeDtypeStruct((T, D), F32),
            jax.ShapeDtypeStruct((T, D), BF),
            jax.ShapeDtypeStruct((D, T), BF),
            jax.ShapeDtypeStruct((T, T), F32),
        ),
        cost_estimate=cost(4),
        name="residual",
    )(attended, tokens, routes, gain, w_router, w_output)


def experts_kernel(
    place_ref, resid_ref, moe_ref, combine_ref, cot_ref, gain_ref, wr_ref, wo_ref, wg_ref, wu_ref, wd_ref,
    out_ref, resid_grad_ref, grad_att_ref, grad_t_ref, acts_ref, small_ref,
    mix_ref, moe_grad_ref, cgrad_ref,
):
    e, f = pl.program_id(0), pl.program_id(1)
    lane = lax.broadcasted_iota(jnp.int32, (T, T), 1)

    @pl.when((e == 0) & (f == 0))
    def _():
        mix_ref[...] = resid_ref[...]
        moe_grad_ref[...] = jnp.zeros_like(moe_grad_ref)
        cgrad_ref[...] = jnp.zeros_like(cgrad_ref)

    moe_low = moe_ref[...]
    grad_out = cot_ref[...].astype(F32)
    combine = jnp.sum(jnp.where(lane == e, combine_ref[...], 0.0), axis=1, keepdims=True)
    expert_grad = (combine * grad_out).astype(BF)
    gate = dot(moe_low, wg_ref[0])
    up = dot(moe_low, wu_ref[0])
    act_grad = dot(expert_grad, wd_ref[0], NT)
    sig = 1.0 / (1.0 + jnp.exp(-gate))
    silu = gate * sig
    act_low = (silu * up).astype(BF)
    down = dot(act_low, wd_ref[0])
    mix_ref[...] += combine * down
    cgrad_ref[...] += jnp.where(lane == e, jnp.sum(grad_out * down, axis=1, keepdims=True), 0.0)
    gate_grad = act_grad * up * (sig * (1.0 + gate * (1.0 - sig)))
    up_grad = act_grad * silu
    moe_grad_ref[...] += dot(gate_grad.astype(BF), wg_ref[0], NT) + dot(
        up_grad.astype(BF), wu_ref[0], NT
    )
    gate_t = swap(gate_grad).astype(BF)
    up_t = swap(up_grad).astype(BF)
    act_t = swap(combine * act_low.astype(F32)).astype(BF)
    at_gu = pl.multiple_of(2 * FS * e, FS)
    at_down = pl.multiple_of(GU + FS * e, FS)
    core, y = place_ref[0], place_ref[3]
    for i in range(FC // FS):
        j = f * (FC // FS) + i
        j = 2 * ((j // 2 - y) & 3) + ((j & 1) ^ core)
        acts_ref[j, pl.ds(at_gu, FS), :] = gate_t[FS * i : FS * (i + 1)]
        acts_ref[j, pl.ds(at_gu + FS, FS), :] = up_t[FS * i : FS * (i + 1)]
        acts_ref[j, pl.ds(at_down, FS), :] = act_t[FS * i : FS * (i + 1)]

    @pl.when((e == EXPERTS - 1) & (f == NF - 1))
    def _():
        out_ref[...] = mix_ref[...].astype(BF)
        weights, cgrad = combine_ref[...], cgrad_ref[...]
        mean = jnp.sum(weights * cgrad, axis=1, keepdims=True)
        logit_grad = (weights * (cgrad - mean)).astype(BF)
        small_ref[0:8, :] = dot(logit_grad, moe_low, TN)[0:8]
        moe_grad = moe_grad_ref[...] + dot(logit_grad[:, 0:8], wr_ref[...])
        resid = resid_ref[...]
        inverse = lax.rsqrt(jnp.mean(resid * resid, axis=1, keepdims=True) + EPSILON)
        n = resid * inverse
        small_ref[8:16, :] = jnp.broadcast_to(jnp.sum(moe_grad * n, axis=0, keepdims=True), (8, D))
        scaled = moe_grad * gain_ref[...].astype(F32)
        resid_grad = grad_out + inverse * (
            scaled - n * jnp.mean(n * scaled, axis=1, keepdims=True)
        )
        resid_grad_ref[...] = resid_grad
        grad_t_ref[...] = swap(resid_grad).astype(BF)
        grad_att = dot(wo_ref[...], resid_grad.astype(BF), NT).astype(BF)
        for h in range(HQ):
            grad_att_ref[device_of(h)] = grad_att[HD * h : HD * (h + 1)]


def experts(place, resid, moe_low, combine, cotangent, gain, w_router, w_output, w_gate, w_up, w_down):
    def whole(*shape):
        return pl.BlockSpec(shape, lambda e, f: (0,) * len(shape))

    def columns():
        return pl.BlockSpec((1, D, FC), lambda e, f: (e, 0, f))

    def rows():
        return pl.BlockSpec((1, FC, D), lambda e, f: (e, f, 0))

    return pl.pallas_call(
        experts_kernel,
        grid=(EXPERTS, NF),
        in_specs=[
            PLACE, whole(T, D), whole(T, D), whole(T, T), whole(T, D), whole(1, D), whole(8, D),
            whole(D, D), columns(), columns(), rows(),
        ],
        out_specs=(
            whole(T, D), whole(T, D), whole(HQ, HD, T), whole(D, T), whole(NC, ACTS, T),
            whole(16, D),
        ),
        out_shape=(
            jax.ShapeDtypeStruct((T, D), BF),
            jax.ShapeDtypeStruct((T, D), F32),
            jax.ShapeDtypeStruct((HQ, HD, T), BF),
            jax.ShapeDtypeStruct((D, T), BF),
            jax.ShapeDtypeStruct((NC, ACTS, T), BF),
            jax.ShapeDtypeStruct((16, D), F32),
        ),
        scratch_shapes=[
            pltpu.VMEM((T, D), F32),
            pltpu.VMEM((T, D), F32),
            pltpu.VMEM((T, T), F32),
        ],
        cost_estimate=cost(13),
        name="experts",
    )(place, resid, moe_low, combine, cotangent, gain, w_router, w_output, w_gate, w_up, w_down)


def side_by_side(ref, i, j):
    return jnp.concatenate([ref[i], ref[j]], axis=1)


def expert_weights_kernel(
    place_ref, acts0_ref, acts1_ref, acts2_ref, acts3_ref, other_ref, moe_ref, cot_ref,
    out_ref, wide_ref, down_ref,
):
    core, y = place_ref[0], place_ref[3]
    for back, acts_ref in enumerate((acts0_ref, acts1_ref, acts2_ref, acts3_ref)):
        chip = 2 * ((y - back) & 3)
        near, far = chip + core, chip + 1 - core
        acts = jnp.concatenate([acts_ref[...], other_ref[back]], axis=1)
        wide = dot(side_by_side(moe_ref, near, far), acts[0:GU], NT)
        down = dot(acts[GU:], jnp.concatenate([cot_ref[near], cot_ref[far]], axis=0))
        if back == 0:
            wide_ref[...] = wide
            down_ref[...] = down
        else:
            wide_ref[...] += wide
            down_ref[...] += down
    for i in range(NR):
        for e in range(EXPERTS):
            out_ref[i, 64 * e : 64 * (e + 1), :] = wide_ref[
                64 * i : 64 * (i + 1), 128 * e : 128 * (e + 1)
            ].astype(BF)
        half, lanes = 96 * (i % 2), 128 * (i // 2)
        out_ref[i, 192:288, :] = down_ref[half : half + 96, lanes : lanes + 128].astype(BF)


def expert_weights(place, acts, others, moe, cotangent):
    return pl.pallas_call(
        expert_weights_kernel,
        in_specs=[PLACE] + in_vmem(7),
        out_shape=jax.ShapeDtypeStruct((NR, PART, T), BF),
        scratch_shapes=[pltpu.VMEM((D, GU), F32), pltpu.VMEM((FS * EXPERTS, D), F32)],
        cost_estimate=cost(5),
        name="expert_weights",
    )(place, *acts, others, moe, cotangent)


def own_rows(half):
    return pl.ds(pl.multiple_of(HD * half, HD), HD), pl.ds(pl.multiple_of(HD * (1 - half), HD), HD)


def project_weights_kernel(
    place_ref, mine_ref, theirs_ref, normed_ref, back_ref, out_ref
):
    own, partner = own_rows(place_ref[2])
    for b in range(NC):
        back_ref[b, own, :] = mine_ref[b, 0:HD, :]
        back_ref[b, partner, :] = theirs_ref[b, 0:HD, :]
        back_ref[b, 2 * HD :, :] = (
            mine_ref[b, HD:, :].astype(F32) + theirs_ref[b, HD:, :].astype(F32)
        ).astype(BF)
    total = jnp.zeros((D, 4 * HD), F32)
    for b in range(0, NC, 2):
        total += dot(side_by_side(normed_ref, b, b + 1), side_by_side(back_ref, b, b + 1), NT)
    low = total.astype(BF)
    for i in range(NR):
        out_ref[i, 0:64, :] = low[64 * i : 64 * (i + 1), 0:128]
        out_ref[i, 64:128, :] = low[64 * i : 64 * (i + 1), 128:256]


def project_weights(place, mine, theirs, normed):
    return pl.pallas_call(
        project_weights_kernel,
        in_specs=[PLACE] + in_vmem(3),
        out_shape=(
            jax.ShapeDtypeStruct((NC, 4 * HD, T), BF),
            jax.ShapeDtypeStruct((NR, MINE, T), BF),
        ),
        cost_estimate=cost(4),
        name="project_weights",
    )(place, mine, theirs, normed)


def output_weights_kernel(
    place_ref, att_ref, att_other_ref, grad_ref, parts_ref, out_ref, heads_ref
):
    own, partner = own_rows(place_ref[2])
    o = jnp.zeros((2 * HD, D), F32)
    for b in range(NC):
        heads_ref[b, own, :] = att_ref[b]
        heads_ref[b, partner, :] = att_other_ref[b]
    for b in range(0, NC, 2):
        o += dot(side_by_side(heads_ref, b, b + 1), side_by_side(grad_ref, b, b + 1), NT)
    low = o.astype(BF)
    for i in range(NR):
        half, lanes = 64 * (i % 2), 128 * (i // 2)
        out_ref[i, 0:128, :] = parts_ref[i, 0:128, :]
        out_ref[i, 128:192, :] = low[half : half + 64, lanes : lanes + 128]


def output_weights(place, attended, attended_other, grad, parts):
    return pl.pallas_call(
        output_weights_kernel,
        in_specs=[PLACE] + in_vmem(4),
        out_shape=jax.ShapeDtypeStruct((NR, MINE, T), BF),
        scratch_shapes=[pltpu.VMEM((NC, 2 * HD, T), BF)],
        cost_estimate=cost(3),
        name="output_weights",
    )(place, attended, attended_other, grad, parts)


def project_back_kernel(
    g_ref, tok_ref, gain_ref, wq_ref, wk_ref, wv_ref, resid_grad_ref, small_ref, out_ref, sums_ref
):
    x = tok_ref[...].astype(F32)
    gain = gain_ref[...].astype(F32)
    inverse = lax.rsqrt(jnp.mean(x * x, axis=1, keepdims=True) + EPSILON)
    n = x * inverse

    def rows(first, last):
        a = g_ref[:, first:last, :]
        return swap(a.reshape(NC * (last - first), T).astype(F32)).astype(BF)

    normed_grad = dot(rows(0, 2 * HD), wq_ref[...], NT)
    normed_grad += dot(rows(2 * HD, 3 * HD), wk_ref[...], NT)
    normed_grad += dot(rows(3 * HD, 4 * HD), wv_ref[...], NT)
    scaled = normed_grad * gain
    out_ref[...] = (
        resid_grad_ref[...] + inverse * (scaled - n * jnp.mean(n * scaled, axis=1, keepdims=True))
    ).astype(BF)
    gain_grad = jnp.sum(normed_grad * n, axis=0, keepdims=True)
    row = lax.broadcasted_iota(jnp.int32, (8, D), 0)
    sums_ref[...] = jnp.where(
        row < EXPERTS, small_ref[0:8], jnp.where(row == EXPERTS, small_ref[8:16], gain_grad)
    )


def project_back(grads, tokens, gain, w_query, w_key, w_value, resid_grad, small):
    return pl.pallas_call(
        project_back_kernel,
        out_shape=(jax.ShapeDtypeStruct((T, D), BF), jax.ShapeDtypeStruct((8, D), F32)),
        cost_estimate=cost(5),
        name="project_back",
    )(grads, tokens, gain, w_query, w_key, w_value, resid_grad, small)


def assemble_kernel(
    g0_ref, g1_ref, g2_ref, p0_ref, p1_ref,
    q_ref, k_ref, v_ref, o_ref, g_ref, u_ref, d_ref,
):
    low_half = lax.broadcasted_iota(jnp.int32, (64, T), 1) < 64

    def rows(refs, pick, first, last):
        found = []
        for at, ref in enumerate(refs):
            begin, end = max(first - PIECE * at, 0), min(last - PIECE * at, PIECE)
            if begin < end:
                found.append(pick(ref)[begin:end])
        whole = found[0] if len(found) == 1 else jnp.concatenate(found, axis=0)
        return whole.astype(F32)

    def turned(a):
        return pltpu.roll(a, 64, 1)

    for c in range(2):
        here = slice(64 * c, 64 * (c + 1))

        def expert_rows(j, first, last, c=c):
            refs = (g0_ref, g1_ref, g2_ref)
            return rows(refs, lambda ref: ref[j // 2, 0, 0, c, j % 2], first, last)

        def project_rows(j, first, last, c=c):
            return rows((p0_ref, p1_ref), lambda ref: ref[0, j // 2, 0, c, j % 2], first, last)

        for m in range(NC // 2):
            tile = slice(T * m, T * (m + 1))
            for e in range(EXPERTS):
                a, b = (expert_rows(2 * m + i, 64 * e, 64 * (e + 1)) for i in range(2))
                g_ref[e, here, tile] = jnp.where(low_half, a, turned(b))
                u_ref[e, here, tile] = jnp.where(low_half, turned(a), b)
            a, b = (project_rows(2 * m + i, 64, 128) for i in range(2))
            k_ref[here, tile] = jnp.where(low_half, a, turned(b))
            v_ref[here, tile] = jnp.where(low_half, turned(a), b)
        for j in range(NC):
            q_ref[here, T * j : T * (j + 1)] = project_rows(j, 0, 64)
            o_ref[j, c] = project_rows(j, 128, 192)
            a = expert_rows(j, 192, 288)
            if c == 0:
                d_ref[0, j] = a[0:64]
                d_ref[1, j, 0:32] = a[64:96]
            else:
                d_ref[1, j, 32:64] = a[0:32]
                d_ref[2, j] = a[32:96]


def assemble(gathered):
    def experts_of(at):
        return pl.BlockSpec((4, 1, 1, 2, 2, PIECE, T), lambda a, b: (0, a, b, 0, 0, at, 0))

    def project_of(at):
        return pl.BlockSpec((1, 4, 1, 2, 2, PIECE, T), lambda a, b: (a, 0, b, 0, 0, at, 0))

    def rows(width):
        return pl.BlockSpec((T, width), lambda a, b: (2 * a + b, 0))

    def stack():
        return pl.BlockSpec((EXPERTS, T, FF), lambda a, b: (0, 2 * a + b, 0))

    return pl.pallas_call(
        assemble_kernel,
        grid=(4, 2),
        in_specs=[experts_of(0), experts_of(1), experts_of(2), project_of(3), project_of(4)],
        out_specs=(
            rows(D), rows(FF), rows(FF),
            pl.BlockSpec((NC, 2, HD, T), lambda a, b: (0, 0, 0, 2 * a + b)),
            stack(), stack(),
            pl.BlockSpec((EXPERTS, NC, FS, T), lambda a, b: (0, 0, 0, 2 * a + b)),
        ),
        out_shape=(
            jax.ShapeDtypeStruct((D, D), F32),
            jax.ShapeDtypeStruct((D, FF), F32),
            jax.ShapeDtypeStruct((D, FF), F32),
            jax.ShapeDtypeStruct((NC, 2, HD, D), F32),
            jax.ShapeDtypeStruct((EXPERTS, D, FF), F32),
            jax.ShapeDtypeStruct((EXPERTS, D, FF), F32),
            jax.ShapeDtypeStruct((EXPERTS, NC, FS, D), F32),
        ),
        cost_estimate=cost(20),
        name="assemble",
    )(*(gathered,) * 5)


def exchange(array, axes=SEQ):
    return lax.all_to_all(array, axes, 0, 0, tiled=True)


def swapped(array, axis):
    return lax.ppermute(array, axis, [(0, 1), (1, 0)])


def gather(array, axes):
    return lax.all_gather(array, axes, axis=0)


def spread_sum(part, axes, count):
    return jnp.sum(exchange(jnp.broadcast_to(part[None], (count, *part.shape)), axes), axis=0)


def part_sum(parts, axes):
    return jnp.sum(exchange(parts, axes).astype(F32), axis=0).astype(BF)


def after(array, *others):
    return lax.optimization_barrier((array, *others))


def shards(
    tokens, cotangent, segment, routes, attn_gain, w_query, w_key, w_value, w_output,
    expert_norm_gain, w_router, w_gate, w_up, w_down,
):
    tokens, cotangent = tokens[0], cotangent[0]
    attn_gain = attn_gain.reshape(1, D)
    expert_norm_gain = expert_norm_gain.reshape(1, D)
    router_rows = jnp.pad(w_router.T, ((0, 8 - EXPERTS), (0, 0)))
    place = jnp.stack([lax.axis_index(a) for a in ("core", "z", "xl", "y")]).astype(jnp.int32)

    cot_all = gather(cotangent, RING)
    received = exchange(project(tokens, segment, attn_gain, w_query, w_key, w_value))
    received, normed = after(received, normed_columns(tokens, attn_gain))
    normed_all = gather(normed, COLUMN)
    attended, att_mine, att_sent, full, log_total, q, k, cosine, sine = attend(place, received)
    attended, cot_all = after(attended, cot_all)
    attended = exchange(attended)
    att_theirs = swapped(att_sent, "xl")
    resid, moe_low, moe_columns, combine = residual(
        attended, tokens, routes[0], expert_norm_gain, router_rows, w_output
    )
    moe_all = gather(moe_columns, RING)
    output, resid_grad, grad_att, grad_columns, acts, small = experts(
        place, resid, moe_low, combine, cotangent, expert_norm_gain, router_rows, w_output,
        w_gate, w_up, w_down,
    )
    grad_att, normed_all = after(grad_att, normed_all)
    acts = [acts[0:2]] + [
        lax.ppermute(acts[2 * back : 2 * back + 2], "y", [(i, (i + back) % 4) for i in range(4)])
        for back in (1, 2, 3)
    ]
    grad_all = gather(grad_columns, COLUMN)
    grad_att = exchange(grad_att)
    mine, sent = attend_back(
        place, received, grad_att, full, log_total, q, k, cosine, sine
    )
    sent, *acts = after(sent, *acts)
    theirs = swapped(sent, "xl")
    acts_theirs = swapped(jnp.stack([a[1] for a in acts]), "core")
    parts = expert_weights(place, [a[0] for a in acts], acts_theirs, moe_all, cot_all)
    theirs, parts = after(theirs, parts)
    expert_part = part_sum(parts, PLANE)
    grads, weights = project_weights(place, mine, theirs, normed_all)
    expert_part, weights = after(expert_part, weights)
    weights = output_weights(place, att_mine, att_theirs, grad_all, weights)
    project_part = part_sum(weights, REST)
    gathered = gather(jnp.concatenate([expert_part, project_part], axis=0), ALL)
    grads, project_part = after(grads, project_part)
    token_grad, small = project_back(
        exchange(grads, COLUMN), tokens, attn_gain, w_query, w_key, w_value, resid_grad, small
    )
    small = spread_sum(spread_sum(small, REST, NR), COLUMN, NC)
    dwq, dwk, dwv, dwo, dwg, dwu, dwd = assemble(
        gathered.reshape(4, 4, 2, 2, 2, PART + MINE, T)
    )
    return (
        output[None], token_grad[None], small[4], dwq, dwk, dwv, dwo.reshape(D, D), small[3],
        small[:EXPERTS].T, dwg, dwu, dwd.reshape(EXPERTS, FF, D),
    )


def solution(mesh):
    fine = Mesh(mesh.devices.reshape(4, 2, 4, 2, 2), AXES)
    by_token = P(ROWS, SEQ, None)
    return jax.shard_map(
        shards,
        mesh=fine,
        in_specs=(by_token, by_token, P(ROWS, SEQ), by_token) + (P(),) * 10,
        out_specs=(by_token, by_token) + (P(),) * 10,
        check_vma=False,
    )
```

```python
import functools
import math

import jax
import jax.numpy as jnp
from jax import lax
from jax.experimental import pallas as pl
from jax.experimental.pallas import tpu as pltpu
from jax.sharding import Mesh
from jax.sharding import PartitionSpec as P

BF = jnp.bfloat16
F32 = jnp.float32
D = 1024
HQ = 16
HK = 8
HD = 64
FF = 512
EXPERTS = 3
T = 128
S = 2048
BLK = 256
NB = S // BLK
WINDOW = 1024 // BLK + 1
HALF = HD // 2
PAY = 3 * HD + 16
FC = 512
NF = FF // FC
NC = 8
NR = 16
FS = FF // NC
GU = 2 * FS * EXPERTS
ACTS = 3 * FS * EXPERTS
PIECE = 96
PART = 3 * PIECE
MINE = 2 * PIECE

EPSILON = 1e-06
THETA_BASE = 10000.0
SOFT_SCALE = 0.125
NEG_FILL = -1e30

AXES = ("y", "xh", "z", "xl", "core")
ROWS = ("y", "xh")
SEQ = ("z", "xl", "core")
COLUMN = ("z", "core")
REST = ("y", "xh", "xl")
RING = ("y", "core")
PLANE = ("z", "xh", "xl")
ALL = ("y", "z", "xh", "xl", "core")

NN = (((1,), (0,)), ((), ()))
NT = (((1,), (1,)), ((), ()))
TN = (((0,), (0,)), ((), ()))


def device_of(head):
    return head // 4 * 4 + head % 2 * 2 + head // 2 % 2


def dot(a, b, dims=NN):
    return lax.dot_general(a, b, dims, preferred_element_type=F32)


def cost(us):
    return pl.CostEstimate(flops=int(us * 1e9), bytes_accessed=1 << 20, transcendentals=0)


def swap(a):
    return jnp.transpose(a, (1, 0))


def project_kernel(tok_ref, seg_ref, gain_ref, wq_ref, wk_ref, wv_ref, out_ref):
    x = tok_ref[...].astype(F32)
    inverse = lax.rsqrt(jnp.mean(x * x, axis=1, keepdims=True) + EPSILON)
    normed = (x * inverse * gain_ref[...].astype(F32).reshape(1, D)).astype(BF)
    ids = jnp.broadcast_to(seg_ref[...].astype(F32), (16, T)).astype(BF)
    for h in range(HQ):
        out_ref[h, 3 * HD :, :] = ids
    for j in range(4):
        q = swap(dot(normed, wq_ref[:, 256 * j : 256 * (j + 1)])).astype(BF)
        for i in range(4):
            out_ref[device_of(4 * j + i), 0:HD, :] = q[HD * i : HD * (i + 1)]
    for w_ref, at in ((wk_ref, HD), (wv_ref, 2 * HD)):
        for j in range(2):
            a = swap(dot(normed, w_ref[:, 256 * j : 256 * (j + 1)])).astype(BF)
            for i in range(4):
                part = a[HD * i : HD * (i + 1)]
                head = 2 * (4 * j + i)
                out_ref[device_of(head), at : at + HD, :] = part
                out_ref[device_of(head + 1), at : at + HD, :] = part


def project(tokens, segment, gain, w_query, w_key, w_value):
    return pl.pallas_call(
        project_kernel,
        out_shape=jax.ShapeDtypeStruct((HQ, PAY, T), BF),
        cost_estimate=cost(4),
        name="project",
    )(tokens, segment, gain, w_query, w_key, w_value)


def starts_of(x_ref):
    ids = x_ref[:, 3 * HD :, :].astype(F32)
    counts = [
        (jnp.sum(jnp.where(ids == float(s), 1.0, 0.0)) * (1.0 / 16)).astype(jnp.int32)
        for s in range(3)
    ]
    first = counts[0]
    second = first + counts[1]
    return first, second, second + counts[2]


def start_at(index, bounds):
    b1, b2, b3 = bounds
    return jnp.where(index >= b3, b3, jnp.where(index >= b2, b2, jnp.where(index >= b1, b1, 0)))


def joined(ref, i, at):
    return jnp.concatenate([ref[2 * i, at : at + HD, :], ref[2 * i + 1, at : at + HD, :]], axis=1)


def put_pair(keep_ref, send_ref, i, rows, a):
    low = a.astype(BF)
    for ref, half in ((keep_ref, lax.axis_index("xl")), (send_ref, 1 - lax.axis_index("xl"))):

        @pl.when((i & 1) == half)
        def _(ref=ref):
            ref[2 * (i // 2), rows, :] = low[:, :T]
            ref[2 * (i // 2) + 1, rows, :] = low[:, T:]


def windowed(i, bounds, body):
    blocks = i + 1 - start_at(i * BLK, bounds) // BLK
    for window in range(1, WINDOW + 1):
        pl.when(blocks == window)(functools.partial(body, window))


def masks_of(i, bounds):
    query = i * BLK + lax.broadcasted_iota(jnp.int32, (1, BLK), 1)
    first = start_at(query, bounds) - i * BLK
    key = lax.broadcasted_iota(jnp.int32, (BLK, BLK), 0)

    def allowed(back):
        inside = key >= first + back * BLK
        return inside & (key <= query - i * BLK) if back == 0 else inside

    return allowed


def attend_kernel(x_ref, att_ref, keep_ref, send_ref, full_ref, log_ref, q_ref, k_ref, cos_ref, sin_ref, kt_ref, v_ref):
    bounds = starts_of(x_ref)
    frequency = jnp.exp(
        lax.broadcasted_iota(jnp.int32, (HALF, 1), 0).astype(F32)
        * (-2.0 * math.log(THETA_BASE) / HD)
    )

    def turn_block(i, carry):
        index = i * BLK + lax.broadcasted_iota(jnp.int32, (1, BLK), 1)
        positions = (index - start_at(index, bounds)).astype(F32)
        angles = positions * frequency
        cosine, sine = jnp.cos(angles), jnp.sin(angles)
        cos_ref[i] = cosine
        sin_ref[i] = sine

        def turned(at):
            a = joined(x_ref, i, at).astype(F32)
            low, high = a[:HALF], a[HALF:]
            return jnp.concatenate(
                [low * cosine - high * sine, high * cosine + low * sine], axis=0
            )

        q_ref[i] = (turned(0).astype(BF).astype(F32) * SOFT_SCALE).astype(BF)
        k = turned(HD)
        k_ref[i] = k.astype(BF)
        kt_ref[i] = swap(k).astype(BF)
        v_ref[i] = joined(x_ref, i, 2 * HD)
        return carry

    lax.fori_loop(0, NB, turn_block, 0, unroll=True)

    def query_block(i, carry):
        q = q_ref[i]
        allowed = masks_of(i, bounds)

        def attend_window(window):
            scores = [
                jnp.where(allowed(back), dot(kt_ref[i - back], q), NEG_FILL)
                for back in range(window)
            ]
            top = jnp.max(functools.reduce(jnp.maximum, scores), axis=0, keepdims=True)
            weights = [jnp.exp(a - top) for a in scores]
            total = jnp.sum(functools.reduce(jnp.add, weights), axis=0, keepdims=True)
            acc = functools.reduce(
                jnp.add, [dot(v_ref[i - back], weights[back].astype(BF)) for back in range(window)]
            )
            attended = acc / total
            log_ref[i] = top + jnp.log(total)
            full_ref[i] = attended
            low = attended.astype(BF)
            att_ref[2 * i] = low[:, :T]
            att_ref[2 * i + 1] = low[:, T:]
            put_pair(keep_ref, send_ref, i, slice(0, HD), attended)

        windowed(i, bounds, attend_window)
        return carry

    lax.fori_loop(0, NB, query_block, 0)


def attend(received):
    return pl.pallas_call(
        attend_kernel,
        out_shape=(
            jax.ShapeDtypeStruct((HQ, HD, T), BF),
            jax.ShapeDtypeStruct((NC, HD, T), BF),
            jax.ShapeDtypeStruct((NC, HD, T), BF),
            jax.ShapeDtypeStruct((NB, HD, BLK), F32),
            jax.ShapeDtypeStruct((NB, 1, BLK), F32),
            jax.ShapeDtypeStruct((NB, HD, BLK), BF),
            jax.ShapeDtypeStruct((NB, HD, BLK), BF),
            jax.ShapeDtypeStruct((NB, HALF, BLK), F32),
            jax.ShapeDtypeStruct((NB, HALF, BLK), F32),
        ),
        scratch_shapes=[pltpu.VMEM((NB, BLK, HD), BF), pltpu.VMEM((NB, HD, BLK), BF)],
        cost_estimate=cost(13),
        name="attend",
    )(received)


def attend_back_kernel(
    x_ref, g_ref, full_ref, log_ref, q_ref, k_ref, cos_ref, sin_ref, keep_ref, send_ref,
    kt_ref, vt_ref, dk_ref, dv_ref,
):
    bounds = starts_of(x_ref)

    def prepare(i, carry):
        kt_ref[i] = swap(k_ref[i].astype(F32)).astype(BF)
        vt_ref[i] = swap(joined(x_ref, i, 2 * HD).astype(F32)).astype(BF)
        dk_ref[i] = jnp.zeros((HD, BLK), F32)
        dv_ref[i] = jnp.zeros((HD, BLK), F32)
        return carry

    lax.fori_loop(0, NB, prepare, 0, unroll=True)

    def turn_back(i, a):
        cosine, sine = cos_ref[i], sin_ref[i]
        low, high = a[:HALF], a[HALF:]
        return jnp.concatenate([low * cosine + high * sine, high * cosine - low * sine], axis=0)

    def put(i, at, a):
        put_pair(keep_ref, send_ref, i, slice(at, at + HD), a)

    def query_block(i, carry):
        q = q_ref[i]
        allowed = masks_of(i, bounds)
        grad = joined(g_ref, i, 0)
        delta = jnp.sum(grad.astype(F32) * full_ref[i], axis=0, keepdims=True)
        log_total = log_ref[i]

        def back_window(window):
            dq = jnp.zeros((HD, BLK), F32)
            for back in range(window):
                j = i - back
                scores = dot(kt_ref[j], q)
                p = jnp.where(allowed(back), jnp.exp(scores - log_total), 0.0)
                dp = dot(vt_ref[j], grad)
                ds = (p * (dp - delta)).astype(BF)
                dv_ref[j] += dot(grad, p.astype(BF), NT)
                dk_ref[j] += dot(q, ds, NT)
                dq += dot(k_ref[j], ds)
            put(i, 0, turn_back(i, dq * SOFT_SCALE))

        windowed(i, bounds, back_window)
        return carry

    lax.fori_loop(0, NB, query_block, 0)

    def finish(i, carry):
        put(i, HD, turn_back(i, dk_ref[i]))
        put(i, 2 * HD, dv_ref[i])
        return carry

    lax.fori_loop(0, NB, finish, 0, unroll=True)


def attend_back(received, grad, full, log_total, q, k, cosine, sine):
    return pl.pallas_call(
        attend_back_kernel,
        out_shape=(
            jax.ShapeDtypeStruct((NC, 3 * HD, T), BF),
            jax.ShapeDtypeStruct((NC, 3 * HD, T), BF),
        ),
        scratch_shapes=[
            pltpu.VMEM((NB, BLK, HD), BF),
            pltpu.VMEM((NB, BLK, HD), BF),
            pltpu.VMEM((NB, HD, BLK), F32),
            pltpu.VMEM((NB, HD, BLK), F32),
        ],
        cost_estimate=cost(13),
        name="attend_back",
    )(received, grad, full, log_total, q, k, cosine, sine)


def normed_kernel(tok_ref, gain_ref, out_ref):
    x = tok_ref[...].astype(F32)
    inverse = lax.rsqrt(jnp.mean(x * x, axis=1, keepdims=True) + EPSILON)
    out_ref[...] = swap(x * inverse * gain_ref[...].astype(F32).reshape(1, D)).astype(BF)


def normed_columns(tokens, gain):
    return pl.pallas_call(
        normed_kernel, out_shape=jax.ShapeDtypeStruct((D, T), BF), cost_estimate=cost(2), name="normed_columns"
    )(tokens, gain)


def resid_kernel(
    att_ref, tok_ref, routes_ref, gain_ref, wr_ref, wo_ref, resid_ref, moe_ref, moe_t_ref, combine_ref
):
    heads = [att_ref[device_of(h)] for h in range(HQ)]
    attended = swap(jnp.concatenate(heads, axis=0).astype(F32)).astype(BF)
    resid = tok_ref[...].astype(F32) + dot(attended, wo_ref[...])
    inverse = lax.rsqrt(jnp.mean(resid * resid, axis=1, keepdims=True) + EPSILON)
    normed = resid * inverse * gain_ref[...].astype(F32).reshape(1, D)
    moe_low = normed.astype(BF)
    resid_ref[...] = resid
    moe_ref[...] = moe_low
    moe_t_ref[...] = swap(normed).astype(BF)
    logits = dot(moe_low, wr_ref[...], NT)
    lane = lax.broadcasted_iota(jnp.int32, (T, T), 1)
    r0, r1 = routes_ref[:, 0:1], routes_ref[:, 1:2]
    l0 = jnp.sum(jnp.where(lane[:, :8] == r0, logits, 0.0), axis=1, keepdims=True)
    l1 = jnp.sum(jnp.where(lane[:, :8] == r1, logits, 0.0), axis=1, keepdims=True)
    top = jnp.maximum(l0, l1)
    e0, e1 = jnp.exp(l0 - top), jnp.exp(l1 - top)
    total = e0 + e1
    combine_ref[...] = jnp.where(lane == r0, e0 / total, 0.0) + jnp.where(
        lane == r1, e1 / total, 0.0
    )


def residual(attended, tokens, routes, gain, w_router, w_output):
    return pl.pallas_call(
        resid_kernel,
        out_shape=(
            jax.ShapeDtypeStruct((T, D), F32),
            jax.ShapeDtypeStruct((T, D), BF),
            jax.ShapeDtypeStruct((D, T), BF),
            jax.ShapeDtypeStruct((T, T), F32),
        ),
        cost_estimate=cost(4),
        name="residual",
    )(attended, tokens, routes, gain, w_router, w_output)


def experts_kernel(
    resid_ref, moe_ref, combine_ref, cot_ref, gain_ref, wr_ref, wo_ref, wg_ref, wu_ref, wd_ref,
    out_ref, resid_grad_ref, grad_att_ref, grad_t_ref, acts_ref, small_ref,
    mix_ref, moe_grad_ref, cgrad_ref,
):
    e, f = pl.program_id(0), pl.program_id(1)
    lane = lax.broadcasted_iota(jnp.int32, (T, T), 1)

    @pl.when((e == 0) & (f == 0))
    def _():
        mix_ref[...] = resid_ref[...]
        moe_grad_ref[...] = jnp.zeros_like(moe_grad_ref)
        cgrad_ref[...] = jnp.zeros_like(cgrad_ref)

    moe_low = moe_ref[...]
    grad_out = cot_ref[...].astype(F32)
    combine = jnp.sum(jnp.where(lane == e, combine_ref[...], 0.0), axis=1, keepdims=True)
    expert_grad = (combine * grad_out).astype(BF)
    gate = dot(moe_low, wg_ref[0])
    up = dot(moe_low, wu_ref[0])
    act_grad = dot(expert_grad, wd_ref[0], NT)
    sig = 1.0 / (1.0 + jnp.exp(-gate))
    silu = gate * sig
    act_low = (silu * up).astype(BF)
    down = dot(act_low, wd_ref[0])
    mix_ref[...] += combine * down
    cgrad_ref[...] += jnp.where(lane == e, jnp.sum(grad_out * down, axis=1, keepdims=True), 0.0)
    gate_grad = act_grad * up * (sig * (1.0 + gate * (1.0 - sig)))
    up_grad = act_grad * silu
    moe_grad_ref[...] += dot(gate_grad.astype(BF), wg_ref[0], NT) + dot(
        up_grad.astype(BF), wu_ref[0], NT
    )
    gate_t = swap(gate_grad).astype(BF)
    up_t = swap(up_grad).astype(BF)
    act_t = swap(combine * act_low.astype(F32)).astype(BF)
    at_gu = pl.multiple_of(2 * FS * e, FS)
    at_down = pl.multiple_of(GU + FS * e, FS)
    core, y = lax.axis_index("core"), lax.axis_index("y")
    for i in range(FC // FS):
        j = f * (FC // FS) + i
        j = 2 * ((j // 2 - y) & 3) + ((j & 1) ^ core)
        acts_ref[j, pl.ds(at_gu, FS), :] = gate_t[FS * i : FS * (i + 1)]
        acts_ref[j, pl.ds(at_gu + FS, FS), :] = up_t[FS * i : FS * (i + 1)]
        acts_ref[j, pl.ds(at_down, FS), :] = act_t[FS * i : FS * (i + 1)]

    @pl.when((e == EXPERTS - 1) & (f == NF - 1))
    def _():
        out_ref[...] = mix_ref[...].astype(BF)
        weights, cgrad = combine_ref[...], cgrad_ref[...]
        mean = jnp.sum(weights * cgrad, axis=1, keepdims=True)
        logit_grad = (weights * (cgrad - mean)).astype(BF)
        small_ref[0:8, :] = dot(logit_grad, moe_low, TN)[0:8]
        moe_grad = moe_grad_ref[...] + dot(logit_grad[:, 0:8], wr_ref[...])
        resid = resid_ref[...]
        inverse = lax.rsqrt(jnp.mean(resid * resid, axis=1, keepdims=True) + EPSILON)
        n = resid * inverse
        small_ref[8:16, :] = jnp.broadcast_to(jnp.sum(moe_grad * n, axis=0, keepdims=True), (8, D))
        scaled = moe_grad * gain_ref[...].astype(F32).reshape(1, D)
        resid_grad = grad_out + inverse * (
            scaled - n * jnp.mean(n * scaled, axis=1, keepdims=True)
        )
        resid_grad_ref[...] = resid_grad
        grad_t_ref[...] = swap(resid_grad).astype(BF)
        grad_att = dot(wo_ref[...], resid_grad.astype(BF), NT).astype(BF)
        for h in range(HQ):
            grad_att_ref[device_of(h)] = grad_att[HD * h : HD * (h + 1)]


def experts(resid, moe_low, combine, cotangent, gain, w_router, w_output, w_gate, w_up, w_down):
    def whole(*shape):
        return pl.BlockSpec(shape, lambda e, f: (0,) * len(shape))

    def columns():
        return pl.BlockSpec((1, D, FC), lambda e, f: (e, 0, f))

    def rows():
        return pl.BlockSpec((1, FC, D), lambda e, f: (e, f, 0))

    return pl.pallas_call(
        experts_kernel,
        grid=(EXPERTS, NF),
        in_specs=[
            whole(T, D), whole(T, D), whole(T, T), whole(T, D), whole(D), whole(8, D),
            whole(D, D), columns(), columns(), rows(),
        ],
        out_specs=(
            whole(T, D), whole(T, D), whole(HQ, HD, T), whole(D, T), whole(NC, ACTS, T),
            whole(16, D),
        ),
        out_shape=(
            jax.ShapeDtypeStruct((T, D), BF),
            jax.ShapeDtypeStruct((T, D), F32),
            jax.ShapeDtypeStruct((HQ, HD, T), BF),
            jax.ShapeDtypeStruct((D, T), BF),
            jax.ShapeDtypeStruct((NC, ACTS, T), BF),
            jax.ShapeDtypeStruct((16, D), F32),
        ),
        scratch_shapes=[
            pltpu.VMEM((T, D), F32),
            pltpu.VMEM((T, D), F32),
            pltpu.VMEM((T, T), F32),
        ],
        cost_estimate=cost(13),
        name="experts",
    )(resid, moe_low, combine, cotangent, gain, w_router, w_output, w_gate, w_up, w_down)


def side_by_side(ref, i, j):
    return jnp.concatenate([ref[i], ref[j]], axis=1)


def expert_weights_kernel(
    acts0_ref, acts1_ref, acts2_ref, acts3_ref, other_ref, moe_ref,
    cot0_ref, cot1_ref, cot2_ref, cot3_ref, out_ref, wide_ref, down_ref,
):
    core, y = lax.axis_index("core"), lax.axis_index("y")
    cot_refs = (cot0_ref, cot1_ref, cot2_ref, cot3_ref)
    for back, acts_ref in enumerate((acts0_ref, acts1_ref, acts2_ref, acts3_ref)):
        chip = 2 * ((y - back) & 3)
        near, far = chip + core, chip + 1 - core
        acts = jnp.concatenate([acts_ref[0], other_ref[back]], axis=1)
        wide = dot(side_by_side(moe_ref, near, far), acts[0:GU], NT)
        down = dot(acts[GU:], cot_refs[back][...].reshape(2 * T, D))
        if back == 0:
            wide_ref[...] = wide
            down_ref[...] = down
        else:
            wide_ref[...] += wide
            down_ref[...] += down
    for i in range(NR):
        for e in range(EXPERTS):
            out_ref[i, 64 * e : 64 * (e + 1), :] = wide_ref[
                64 * i : 64 * (i + 1), 128 * e : 128 * (e + 1)
            ].astype(BF)
        half, lanes = 96 * (i % 2), 128 * (i // 2)
        out_ref[i, 192:288, :] = down_ref[half : half + 96, lanes : lanes + 128].astype(BF)


def expert_weights(acts, others, moe, cotangent):
    return pl.pallas_call(
        expert_weights_kernel,
        out_shape=jax.ShapeDtypeStruct((NR, PART, T), BF),
        scratch_shapes=[pltpu.VMEM((D, GU), F32), pltpu.VMEM((FS * EXPERTS, D), F32)],
        cost_estimate=cost(5),
        name="expert_weights",
    )(*acts, others, moe, *cotangent)


def own_rows(half):
    return pl.ds(pl.multiple_of(HD * half, HD), HD), pl.ds(pl.multiple_of(HD * (1 - half), HD), HD)


def project_weights_kernel(
    mine_ref, theirs_ref, normed_ref, back_ref, out_ref
):
    own, partner = own_rows(lax.axis_index("xl"))
    for b in range(NC):
        back_ref[b, own, :] = mine_ref[b, 0:HD, :]
        back_ref[b, partner, :] = theirs_ref[b, 0:HD, :]
        back_ref[b, 2 * HD :, :] = (
            mine_ref[b, HD:, :].astype(F32) + theirs_ref[b, HD:, :].astype(F32)
        ).astype(BF)
    total = jnp.zeros((D, 4 * HD), F32)
    for b in range(0, NC, 2):
        total += dot(side_by_side(normed_ref, b, b + 1), side_by_side(back_ref, b, b + 1), NT)
    low = total.astype(BF)
    for i in range(NR):
        out_ref[i, 0:64, :] = low[64 * i : 64 * (i + 1), 0:128]
        out_ref[i, 64:128, :] = low[64 * i : 64 * (i + 1), 128:256]


def project_weights(mine, theirs, normed):
    return pl.pallas_call(
        project_weights_kernel,
        out_shape=(
            jax.ShapeDtypeStruct((NC, 4 * HD, T), BF),
            jax.ShapeDtypeStruct((NR, MINE, T), BF),
        ),
        cost_estimate=cost(4),
        name="project_weights",
    )(mine, theirs, normed)


def output_weights_kernel(
    att_ref, att_other_ref, grad_ref, parts_ref, out_ref, heads_ref
):
    own, partner = own_rows(lax.axis_index("xl"))
    o = jnp.zeros((2 * HD, D), F32)
    for b in range(NC):
        heads_ref[b, own, :] = att_ref[b]
        heads_ref[b, partner, :] = att_other_ref[b]
    for b in range(0, NC, 2):
        o += dot(side_by_side(heads_ref, b, b + 1), side_by_side(grad_ref, b, b + 1), NT)
    low = o.astype(BF)
    for i in range(NR):
        half, lanes = 64 * (i % 2), 128 * (i // 2)
        out_ref[i, 0:128, :] = parts_ref[i, 0:128, :]
        out_ref[i, 128:192, :] = low[half : half + 64, lanes : lanes + 128]


def output_weights(attended, attended_other, grad, parts):
    return pl.pallas_call(
        output_weights_kernel,
        out_shape=jax.ShapeDtypeStruct((NR, MINE, T), BF),
        scratch_shapes=[pltpu.VMEM((NC, 2 * HD, T), BF)],
        cost_estimate=cost(3),
        name="output_weights",
    )(attended, attended_other, grad, parts)


def project_back_kernel(
    g_ref, tok_ref, gain_ref, wq_ref, wk_ref, wv_ref, resid_grad_ref, small_ref, out_ref, sums_ref
):
    x = tok_ref[...].astype(F32)
    gain = gain_ref[...].astype(F32).reshape(1, D)
    inverse = lax.rsqrt(jnp.mean(x * x, axis=1, keepdims=True) + EPSILON)
    n = x * inverse

    def rows(first, last):
        a = g_ref[:, first:last, :]
        return swap(a.reshape(NC * (last - first), T).astype(F32)).astype(BF)

    normed_grad = dot(rows(0, 2 * HD), wq_ref[...], NT)
    normed_grad += dot(rows(2 * HD, 3 * HD), wk_ref[...], NT)
    normed_grad += dot(rows(3 * HD, 4 * HD), wv_ref[...], NT)
    scaled = normed_grad * gain
    out_ref[...] = (
        resid_grad_ref[...] + inverse * (scaled - n * jnp.mean(n * scaled, axis=1, keepdims=True))
    ).astype(BF)
    gain_grad = jnp.sum(normed_grad * n, axis=0, keepdims=True)
    row = lax.broadcasted_iota(jnp.int32, (8, D), 0)
    sums_ref[...] = jnp.where(
        row < EXPERTS, small_ref[0:8], jnp.where(row == EXPERTS, small_ref[8:16], gain_grad)
    )


def project_back(grads, tokens, gain, w_query, w_key, w_value, resid_grad, small):
    return pl.pallas_call(
        project_back_kernel,
        out_shape=(jax.ShapeDtypeStruct((T, D), BF), jax.ShapeDtypeStruct((8, D), F32)),
        cost_estimate=cost(5),
        name="project_back",
    )(grads, tokens, gain, w_query, w_key, w_value, resid_grad, small)


def assemble_kernel(
    g0_ref, g1_ref, g2_ref, p0_ref, p1_ref,
    q_ref, k_ref, v_ref, o_ref, g_ref, u_ref, d_ref,
):
    low_half = lax.broadcasted_iota(jnp.int32, (64, T), 1) < 64

    def rows(refs, pick, first, last):
        found = []
        for at, ref in enumerate(refs):
            begin, end = max(first - PIECE * at, 0), min(last - PIECE * at, PIECE)
            if begin < end:
                found.append(pick(ref)[begin:end])
        whole = found[0] if len(found) == 1 else jnp.concatenate(found, axis=0)
        return whole.astype(F32)

    def turned(a):
        return pltpu.roll(a, 64, 1)

    for c in range(2):
        here = slice(64 * c, 64 * (c + 1))

        def expert_rows(j, first, last, c=c):
            refs = (g0_ref, g1_ref, g2_ref)
            return rows(refs, lambda ref: ref[j // 2, 0, 0, c, j % 2], first, last)

        def project_rows(j, first, last, c=c):
            return rows((p0_ref, p1_ref), lambda ref: ref[0, j // 2, 0, c, j % 2], first, last)

        for m in range(NC // 2):
            tile = slice(T * m, T * (m + 1))
            for e in range(EXPERTS):
                a, b = (expert_rows(2 * m + i, 64 * e, 64 * (e + 1)) for i in range(2))
                g_ref[e, here, tile] = jnp.where(low_half, a, turned(b))
                u_ref[e, here, tile] = jnp.where(low_half, turned(a), b)
            a, b = (project_rows(2 * m + i, 64, 128) for i in range(2))
            k_ref[here, tile] = jnp.where(low_half, a, turned(b))
            v_ref[here, tile] = jnp.where(low_half, turned(a), b)
        for j in range(NC):
            q_ref[here, T * j : T * (j + 1)] = project_rows(j, 0, 64)
            o_ref[j, c] = project_rows(j, 128, 192)
            a = expert_rows(j, 192, 288)
            if c == 0:
                d_ref[0, j] = a[0:64]
                d_ref[1, j, 0:32] = a[64:96]
            else:
                d_ref[1, j, 32:64] = a[0:32]
                d_ref[2, j] = a[32:96]


def assemble(gathered):
    def experts_of(at):
        return pl.BlockSpec((4, 1, 1, 2, 2, PIECE, T), lambda a, b: (0, a, b, 0, 0, at, 0))

    def project_of(at):
        return pl.BlockSpec((1, 4, 1, 2, 2, PIECE, T), lambda a, b: (a, 0, b, 0, 0, at, 0))

    def rows(width):
        return pl.BlockSpec((T, width), lambda a, b: (2 * a + b, 0))

    def stack():
        return pl.BlockSpec((EXPERTS, T, FF), lambda a, b: (0, 2 * a + b, 0))

    return pl.pallas_call(
        assemble_kernel,
        grid=(4, 2),
        in_specs=[experts_of(0), experts_of(1), experts_of(2), project_of(3), project_of(4)],
        out_specs=(
            rows(D), rows(FF), rows(FF),
            pl.BlockSpec((NC, 2, HD, T), lambda a, b: (0, 0, 0, 2 * a + b)),
            stack(), stack(),
            pl.BlockSpec((EXPERTS, NC, FS, T), lambda a, b: (0, 0, 0, 2 * a + b)),
        ),
        out_shape=(
            jax.ShapeDtypeStruct((D, D), F32),
            jax.ShapeDtypeStruct((D, FF), F32),
            jax.ShapeDtypeStruct((D, FF), F32),
            jax.ShapeDtypeStruct((NC, 2, HD, D), F32),
            jax.ShapeDtypeStruct((EXPERTS, D, FF), F32),
            jax.ShapeDtypeStruct((EXPERTS, D, FF), F32),
            jax.ShapeDtypeStruct((EXPERTS, NC, FS, D), F32),
        ),
        cost_estimate=cost(20),
        name="assemble",
    )(*(gathered,) * 5)


def exchange(array, axes=SEQ):
    return lax.all_to_all(array, axes, 0, 0, tiled=True)


def swapped(array, axis):
    return lax.ppermute(array, axis, [(0, 1), (1, 0)])


def ring_moved(array, back):
    return lax.ppermute(array, "y", [(i, (i + back) % 4) for i in range(4)])


def gather(array, axes):
    return lax.all_gather(array, axes, axis=0)


def spread_sum(part, axes, count):
    return jnp.sum(exchange(jnp.broadcast_to(part[None], (count, *part.shape)), axes), axis=0)


def part_sum(parts, axes):
    return jnp.sum(exchange(parts, axes).astype(F32), axis=0).astype(BF)


def after(array, *others):
    return lax.optimization_barrier((array, *others))


def shards(
    tokens, cotangent, segment, routes, attn_gain, w_query, w_key, w_value, w_output,
    expert_norm_gain, w_router, w_gate, w_up, w_down,
):
    tokens, cotangent = tokens[0], cotangent[0]
    router_rows = jnp.pad(w_router.T, ((0, 8 - EXPERTS), (0, 0)))

    projected = project(tokens, segment, attn_gain, w_query, w_key, w_value)
    projected, cot = after(projected, cotangent)
    received = exchange(projected)
    cot = jnp.stack([cot, swapped(cot, "core")])
    received, normed, cot, cot3 = after(
        received, normed_columns(tokens, attn_gain), cot, ring_moved(cot, 3)
    )
    cot1, cot2 = ring_moved(cot, 1), ring_moved(cot, 2)
    normed_all = gather(normed, COLUMN)
    attended, att_mine, att_sent, full, log_total, q, k, cosine, sine = attend(received)
    attended, cot1, cot2 = after(exchange(attended), cot1, cot2)
    att_theirs = swapped(att_sent, "xl")
    resid, moe_low, moe_columns, combine = residual(
        attended, tokens, routes[0], expert_norm_gain, router_rows, w_output
    )
    moe_all = gather(moe_columns, RING)
    output, resid_grad, grad_att, grad_columns, acts, small = experts(
        resid, moe_low, combine, cotangent, expert_norm_gain, router_rows, w_output,
        w_gate, w_up, w_down,
    )
    grad_att, normed_all, att_theirs = after(grad_att, normed_all, att_theirs)
    acts = [acts[0:2]] + [
        ring_moved(acts[2 * back : 2 * back + 2], back) for back in (1, 2, 3)
    ]
    grad_all = gather(grad_columns, COLUMN)
    grad_att = exchange(grad_att)
    mine, sent = attend_back(
        received, grad_att, full, log_total, q, k, cosine, sine
    )
    sent, *acts = after(sent, *acts)
    theirs = swapped(sent, "xl")
    acts_theirs = swapped(jnp.stack([a[1] for a in acts]), "core")
    parts = expert_weights(acts, acts_theirs, moe_all, (cot, cot1, cot2, cot3))
    theirs, parts = after(theirs, parts)
    expert_part = part_sum(parts, PLANE)
    grads, weights = project_weights(mine, theirs, normed_all)
    weights = output_weights(att_mine, att_theirs, grad_all, weights)
    expert_part, weights = after(expert_part, weights)
    project_part = part_sum(weights, REST)
    gathered = gather(jnp.concatenate([expert_part, project_part], axis=0), ALL)
    grads, project_part = after(grads, project_part)
    token_grad, small = project_back(
        exchange(grads, COLUMN), tokens, attn_gain, w_query, w_key, w_value, resid_grad, small
    )
    small = spread_sum(spread_sum(small, REST, NR), COLUMN, NC)
    dwq, dwk, dwv, dwo, dwg, dwu, dwd = assemble(
        gathered.reshape(4, 4, 2, 2, 2, PART + MINE, T)
    )
    return (
        output[None], token_grad[None], small[4], dwq, dwk, dwv, dwo.reshape(D, D), small[3],
        small[:EXPERTS].T, dwg, dwu, dwd.reshape(EXPERTS, FF, D),
    )


def solution(mesh):
    fine = Mesh(mesh.devices.reshape(4, 2, 4, 2, 2), AXES)
    by_token = P(ROWS, SEQ, None)
    return jax.shard_map(
        shards,
        mesh=fine,
        in_specs=(by_token, by_token, P(ROWS, SEQ), by_token) + (P(),) * 10,
        out_specs=(by_token, by_token) + (P(),) * 10,
        check_vma=False,
    )
```

```python
import functools
import math

import jax
import jax.numpy as jnp
from jax import lax
from jax.experimental import pallas as pl
from jax.experimental.pallas import tpu as pltpu
from jax.sharding import Mesh
from jax.sharding import PartitionSpec as P

BF = jnp.bfloat16
F32 = jnp.float32
D = 1024
HQ = 16
HK = 8
HD = 64
FF = 512
EXPERTS = 3
T = 128
S = 2048
BLK = 256
NB = S // BLK
WINDOW = 1024 // BLK + 1
HALF = HD // 2
PAY = 3 * HD + 16
FC = 512
NF = FF // FC
NC = 8
NR = 16
FS = FF // NC
GU = 2 * FS * EXPERTS
SLOTS = 6 * FS
ACTS = SLOTS + 16
PIECE = 96
PART = 3 * PIECE
MINE = 2 * PIECE

EPSILON = 1e-06
THETA_BASE = 10000.0
SOFT_SCALE = 0.125
NEG_FILL = -1e30

AXES = ("y", "xh", "z", "xl", "core")
ROWS = ("y", "xh")
SEQ = ("z", "xl", "core")
COLUMN = ("z", "core")
REST = ("y", "xh", "xl")
RING = ("y", "core")
PLANE = ("z", "xh", "xl")
ALL = ("y", "z", "xh", "xl", "core")

NN = (((1,), (0,)), ((), ()))
NT = (((1,), (1,)), ((), ()))
TN = (((0,), (0,)), ((), ()))


def device_of(head):
    return head // 4 * 4 + head % 2 * 2 + head // 2 % 2


def dot(a, b, dims=NN):
    return lax.dot_general(a, b, dims, preferred_element_type=F32)


def cost(us):
    return pl.CostEstimate(flops=int(us * 1e9), bytes_accessed=1 << 20, transcendentals=0)


def swap(a):
    return jnp.transpose(a, (1, 0))


def project_kernel(tok_ref, seg_ref, gain_ref, wq_ref, wk_ref, wv_ref, out_ref):
    x = tok_ref[...].astype(F32)
    inverse = lax.rsqrt(jnp.mean(x * x, axis=1, keepdims=True) + EPSILON)
    normed = (x * inverse * gain_ref[...].astype(F32).reshape(1, D)).astype(BF)
    ids = jnp.broadcast_to(seg_ref[...].astype(F32), (16, T)).astype(BF)
    for h in range(HQ):
        out_ref[h, 3 * HD :, :] = ids
    for j in range(4):
        q = swap(dot(normed, wq_ref[:, 256 * j : 256 * (j + 1)])).astype(BF)
        for i in range(4):
            out_ref[device_of(4 * j + i), 0:HD, :] = q[HD * i : HD * (i + 1)]
    for w_ref, at in ((wk_ref, HD), (wv_ref, 2 * HD)):
        for j in range(2):
            a = swap(dot(normed, w_ref[:, 256 * j : 256 * (j + 1)])).astype(BF)
            for i in range(4):
                part = a[HD * i : HD * (i + 1)]
                head = 2 * (4 * j + i)
                out_ref[device_of(head), at : at + HD, :] = part
                out_ref[device_of(head + 1), at : at + HD, :] = part


def project(tokens, segment, gain, w_query, w_key, w_value):
    return pl.pallas_call(
        project_kernel,
        out_shape=jax.ShapeDtypeStruct((HQ, PAY, T), BF),
        cost_estimate=cost(4),
        name="project",
    )(tokens, segment, gain, w_query, w_key, w_value)


def starts_of(x_ref):
    ids = x_ref[:, 3 * HD :, :].astype(F32)
    counts = [
        (jnp.sum(jnp.where(ids == float(s), 1.0, 0.0)) * (1.0 / 16)).astype(jnp.int32)
        for s in range(3)
    ]
    first = counts[0]
    second = first + counts[1]
    return first, second, second + counts[2]


def start_at(index, bounds):
    b1, b2, b3 = bounds
    return jnp.where(index >= b3, b3, jnp.where(index >= b2, b2, jnp.where(index >= b1, b1, 0)))


def joined(ref, i, at):
    return jnp.concatenate([ref[2 * i, at : at + HD, :], ref[2 * i + 1, at : at + HD, :]], axis=1)


def put_pair(keep_ref, send_ref, i, rows, a):
    low = a.astype(BF)
    for ref, half in ((keep_ref, lax.axis_index("xl")), (send_ref, 1 - lax.axis_index("xl"))):

        @pl.when((i & 1) == half)
        def _(ref=ref):
            ref[2 * (i // 2), rows, :] = low[:, :T]
            ref[2 * (i // 2) + 1, rows, :] = low[:, T:]


def windowed(i, bounds, body):
    blocks = i + 1 - start_at(i * BLK, bounds) // BLK
    for window in range(1, WINDOW + 1):
        pl.when(blocks == window)(functools.partial(body, window))


def masks_of(i, bounds):
    query = i * BLK + lax.broadcasted_iota(jnp.int32, (1, BLK), 1)
    first = start_at(query, bounds) - i * BLK
    key = lax.broadcasted_iota(jnp.int32, (BLK, BLK), 0)

    def allowed(back):
        inside = key >= first + back * BLK
        return inside & (key <= query - i * BLK) if back == 0 else inside

    return allowed


def attend_kernel(x_ref, att_ref, keep_ref, send_ref, full_ref, log_ref, q_ref, k_ref, cos_ref, sin_ref, kt_ref, v_ref):
    bounds = starts_of(x_ref)
    frequency = jnp.exp(
        lax.broadcasted_iota(jnp.int32, (HALF, 1), 0).astype(F32)
        * (-2.0 * math.log(THETA_BASE) / HD)
    )

    def turn_block(i, carry):
        index = i * BLK + lax.broadcasted_iota(jnp.int32, (1, BLK), 1)
        positions = (index - start_at(index, bounds)).astype(F32)
        angles = positions * frequency
        cosine, sine = jnp.cos(angles), jnp.sin(angles)
        cos_ref[i] = cosine
        sin_ref[i] = sine

        def turned(at):
            a = joined(x_ref, i, at).astype(F32)
            low, high = a[:HALF], a[HALF:]
            return jnp.concatenate(
                [low * cosine - high * sine, high * cosine + low * sine], axis=0
            )

        q_ref[i] = (turned(0).astype(BF).astype(F32) * SOFT_SCALE).astype(BF)
        k = turned(HD)
        k_ref[i] = k.astype(BF)
        kt_ref[i] = swap(k).astype(BF)
        v_ref[i] = joined(x_ref, i, 2 * HD)
        return carry

    lax.fori_loop(0, NB, turn_block, 0, unroll=True)

    def query_block(i, carry):
        q = q_ref[i]
        allowed = masks_of(i, bounds)

        def attend_window(window):
            scores = [
                jnp.where(allowed(back), dot(kt_ref[i - back], q), NEG_FILL)
                for back in range(window)
            ]
            top = jnp.max(functools.reduce(jnp.maximum, scores), axis=0, keepdims=True)
            weights = [jnp.exp(a - top) for a in scores]
            total = jnp.sum(functools.reduce(jnp.add, weights), axis=0, keepdims=True)
            acc = functools.reduce(
                jnp.add, [dot(v_ref[i - back], weights[back].astype(BF)) for back in range(window)]
            )
            attended = acc / total
            log_ref[i] = top + jnp.log(total)
            full_ref[i] = attended
            low = attended.astype(BF)
            att_ref[2 * i] = low[:, :T]
            att_ref[2 * i + 1] = low[:, T:]
            put_pair(keep_ref, send_ref, i, slice(0, HD), attended)

        windowed(i, bounds, attend_window)
        return carry

    lax.fori_loop(0, NB, query_block, 0)


def attend(received):
    return pl.pallas_call(
        attend_kernel,
        out_shape=(
            jax.ShapeDtypeStruct((HQ, HD, T), BF),
            jax.ShapeDtypeStruct((NC, HD, T), BF),
            jax.ShapeDtypeStruct((NC, HD, T), BF),
            jax.ShapeDtypeStruct((NB, HD, BLK), F32),
            jax.ShapeDtypeStruct((NB, 1, BLK), F32),
            jax.ShapeDtypeStruct((NB, HD, BLK), BF),
            jax.ShapeDtypeStruct((NB, HD, BLK), BF),
            jax.ShapeDtypeStruct((NB, HALF, BLK), F32),
            jax.ShapeDtypeStruct((NB, HALF, BLK), F32),
        ),
        scratch_shapes=[pltpu.VMEM((NB, BLK, HD), BF), pltpu.VMEM((NB, HD, BLK), BF)],
        cost_estimate=cost(13),
        name="attend",
    )(received)


def attend_back_kernel(
    x_ref, g_ref, full_ref, log_ref, q_ref, k_ref, cos_ref, sin_ref, keep_ref, send_ref,
    kt_ref, vt_ref, dk_ref, dv_ref,
):
    bounds = starts_of(x_ref)

    def prepare(i, carry):
        kt_ref[i] = swap(k_ref[i].astype(F32)).astype(BF)
        vt_ref[i] = swap(joined(x_ref, i, 2 * HD).astype(F32)).astype(BF)
        dk_ref[i] = jnp.zeros((HD, BLK), F32)
        dv_ref[i] = jnp.zeros((HD, BLK), F32)
        return carry

    lax.fori_loop(0, NB, prepare, 0, unroll=True)

    def turn_back(i, a):
        cosine, sine = cos_ref[i], sin_ref[i]
        low, high = a[:HALF], a[HALF:]
        return jnp.concatenate([low * cosine + high * sine, high * cosine - low * sine], axis=0)

    def put(i, at, a):
        put_pair(keep_ref, send_ref, i, slice(at, at + HD), a)

    def query_block(i, carry):
        q = q_ref[i]
        allowed = masks_of(i, bounds)
        grad = joined(g_ref, i, 0)
        delta = jnp.sum(grad.astype(F32) * full_ref[i], axis=0, keepdims=True)
        log_total = log_ref[i]

        def back_window(window):
            dq = jnp.zeros((HD, BLK), F32)
            for back in range(window):
                j = i - back
                scores = dot(kt_ref[j], q)
                p = jnp.where(allowed(back), jnp.exp(scores - log_total), 0.0)
                dp = dot(vt_ref[j], grad)
                ds = (p * (dp - delta)).astype(BF)
                dv_ref[j] += dot(grad, p.astype(BF), NT)
                dk_ref[j] += dot(q, ds, NT)
                dq += dot(k_ref[j], ds)
            put(i, 0, turn_back(i, dq * SOFT_SCALE))

        windowed(i, bounds, back_window)
        return carry

    lax.fori_loop(0, NB, query_block, 0)

    def finish(i, carry):
        put(i, HD, turn_back(i, dk_ref[i]))
        put(i, 2 * HD, dv_ref[i])
        return carry

    lax.fori_loop(0, NB, finish, 0, unroll=True)


def attend_back(received, grad, full, log_total, q, k, cosine, sine):
    return pl.pallas_call(
        attend_back_kernel,
        out_shape=(
            jax.ShapeDtypeStruct((NC, 3 * HD, T), BF),
            jax.ShapeDtypeStruct((NC, 3 * HD, T), BF),
        ),
        scratch_shapes=[
            pltpu.VMEM((NB, BLK, HD), BF),
            pltpu.VMEM((NB, BLK, HD), BF),
            pltpu.VMEM((NB, HD, BLK), F32),
            pltpu.VMEM((NB, HD, BLK), F32),
        ],
        cost_estimate=cost(13),
        name="attend_back",
    )(received, grad, full, log_total, q, k, cosine, sine)


def normed_kernel(tok_ref, gain_ref, out_ref):
    x = tok_ref[...].astype(F32)
    inverse = lax.rsqrt(jnp.mean(x * x, axis=1, keepdims=True) + EPSILON)
    out_ref[...] = swap(x * inverse * gain_ref[...].astype(F32).reshape(1, D)).astype(BF)


def normed_columns(tokens, gain):
    return pl.pallas_call(
        normed_kernel, out_shape=jax.ShapeDtypeStruct((D, T), BF), cost_estimate=cost(2), name="normed_columns"
    )(tokens, gain)


def resid_kernel(
    att_ref, tok_ref, routes_ref, gain_ref, wr_ref, wo_ref, resid_ref, moe_ref, moe_t_ref, combine_ref,
    missing_ref,
):
    heads = [att_ref[device_of(h)] for h in range(HQ)]
    attended = swap(jnp.concatenate(heads, axis=0).astype(F32)).astype(BF)
    resid = tok_ref[...].astype(F32) + dot(attended, wo_ref[...])
    inverse = lax.rsqrt(jnp.mean(resid * resid, axis=1, keepdims=True) + EPSILON)
    normed = resid * inverse * gain_ref[...].astype(F32).reshape(1, D)
    moe_low = normed.astype(BF)
    resid_ref[...] = resid
    moe_ref[...] = moe_low
    moe_t_ref[...] = swap(normed).astype(BF)
    logits = dot(moe_low, wr_ref[...], NT)
    lane = lax.broadcasted_iota(jnp.int32, (T, T), 1)
    r0, r1 = routes_ref[:, 0:1], routes_ref[:, 1:2]
    l0 = jnp.sum(jnp.where(lane[:, :8] == r0, logits, 0.0), axis=1, keepdims=True)
    l1 = jnp.sum(jnp.where(lane[:, :8] == r1, logits, 0.0), axis=1, keepdims=True)
    missing = (EXPERTS - r0 - r1).astype(F32)
    missing_ref[...] = swap(jnp.broadcast_to(missing, (T, T)))[0:16].astype(BF)
    top = jnp.maximum(l0, l1)
    e0, e1 = jnp.exp(l0 - top), jnp.exp(l1 - top)
    total = e0 + e1
    combine_ref[...] = jnp.where(lane == r0, e0 / total, 0.0) + jnp.where(
        lane == r1, e1 / total, 0.0
    )


def residual(attended, tokens, routes, gain, w_router, w_output):
    return pl.pallas_call(
        resid_kernel,
        out_shape=(
            jax.ShapeDtypeStruct((T, D), F32),
            jax.ShapeDtypeStruct((T, D), BF),
            jax.ShapeDtypeStruct((D, T), BF),
            jax.ShapeDtypeStruct((T, T), F32),
            jax.ShapeDtypeStruct((16, T), BF),
        ),
        cost_estimate=cost(4),
        name="residual",
    )(attended, tokens, routes, gain, w_router, w_output)


def experts_kernel(
    resid_ref, moe_ref, combine_ref, missing_ref, cot_ref, gain_ref, wr_ref, wo_ref,
    wg_ref, wu_ref, wd_ref, out_ref, resid_grad_ref, grad_att_ref, grad_t_ref, acts_ref, small_ref,
    mix_ref, moe_grad_ref, cgrad_ref,
):
    e, f = pl.program_id(0), pl.program_id(1)
    lane = lax.broadcasted_iota(jnp.int32, (T, T), 1)

    @pl.when((e == 0) & (f == 0))
    def _():
        mix_ref[...] = resid_ref[...]
        moe_grad_ref[...] = jnp.zeros_like(moe_grad_ref)
        cgrad_ref[...] = jnp.zeros_like(cgrad_ref)

    moe_low = moe_ref[...]
    grad_out = cot_ref[...].astype(F32)
    combine = jnp.sum(jnp.where(lane == e, combine_ref[...], 0.0), axis=1, keepdims=True)
    expert_grad = (combine * grad_out).astype(BF)
    gate = dot(moe_low, wg_ref[0])
    up = dot(moe_low, wu_ref[0])
    act_grad = dot(expert_grad, wd_ref[0], NT)
    sig = 1.0 / (1.0 + jnp.exp(-gate))
    silu = gate * sig
    act_low = (silu * up).astype(BF)
    down = dot(act_low, wd_ref[0])
    mix_ref[...] += combine * down
    cgrad_ref[...] += jnp.where(lane == e, jnp.sum(grad_out * down, axis=1, keepdims=True), 0.0)
    gate_grad = act_grad * up * (sig * (1.0 + gate * (1.0 - sig)))
    up_grad = act_grad * silu
    moe_grad_ref[...] += dot(gate_grad.astype(BF), wg_ref[0], NT) + dot(
        up_grad.astype(BF), wu_ref[0], NT
    )
    gate_t, up_t = swap(gate_grad), swap(up_grad)
    act_t = swap(combine * act_low.astype(F32))
    core, y = lax.axis_index("core"), lax.axis_index("y")
    missing = missing_ref[0:1].astype(F32)

    def slices(put):
        for i in range(FC // FS):
            j = f * (FC // FS) + i
            j = 2 * ((j // 2 - y) & 3) + ((j & 1) ^ core)
            for k, a in enumerate((gate_t, up_t, act_t)):
                put(j, (0, FS, 4 * FS)[k], (2 * FS, 3 * FS, 5 * FS)[k], a[FS * i : FS * (i + 1)])

    @pl.when(e == 0)
    def _():
        def put(j, at_a, at_b, a):
            acts_ref[j, at_a : at_a + FS, :] = a.astype(BF)

        slices(put)
        for j in range(NC):
            acts_ref[j, SLOTS:, :] = missing_ref[...]

    @pl.when(e == 1)
    def _():
        def put(j, at_a, at_b, a):
            rows = slice(at_a, at_a + FS)
            old = acts_ref[j, rows, :].astype(F32)
            acts_ref[j, rows, :] = jnp.where(missing == 0.0, a, old).astype(BF)
            acts_ref[j, at_b : at_b + FS, :] = a.astype(BF)

        slices(put)

    @pl.when(e == 2)
    def _():
        def put(j, at_a, at_b, a):
            rows = slice(at_b, at_b + FS)
            old = acts_ref[j, rows, :].astype(F32)
            acts_ref[j, rows, :] = jnp.where(missing == 2.0, old, a).astype(BF)

        slices(put)

    @pl.when((e == EXPERTS - 1) & (f == NF - 1))
    def _():
        out_ref[...] = mix_ref[...].astype(BF)
        weights, cgrad = combine_ref[...], cgrad_ref[...]
        mean = jnp.sum(weights * cgrad, axis=1, keepdims=True)
        logit_grad = (weights * (cgrad - mean)).astype(BF)
        small_ref[0:8, :] = dot(logit_grad, moe_low, TN)[0:8]
        moe_grad = moe_grad_ref[...] + dot(logit_grad[:, 0:8], wr_ref[...])
        resid = resid_ref[...]
        inverse = lax.rsqrt(jnp.mean(resid * resid, axis=1, keepdims=True) + EPSILON)
        n = resid * inverse
        small_ref[8:16, :] = jnp.broadcast_to(jnp.sum(moe_grad * n, axis=0, keepdims=True), (8, D))
        scaled = moe_grad * gain_ref[...].astype(F32).reshape(1, D)
        resid_grad = grad_out + inverse * (
            scaled - n * jnp.mean(n * scaled, axis=1, keepdims=True)
        )
        resid_grad_ref[...] = resid_grad
        grad_t_ref[...] = swap(resid_grad).astype(BF)
        grad_att = dot(wo_ref[...], resid_grad.astype(BF), NT).astype(BF)
        for h in range(HQ):
            grad_att_ref[device_of(h)] = grad_att[HD * h : HD * (h + 1)]


def experts(resid, moe_low, combine, missing, cotangent, gain, w_router, w_output, w_gate, w_up, w_down):
    def whole(*shape):
        return pl.BlockSpec(shape, lambda e, f: (0,) * len(shape))

    def columns():
        return pl.BlockSpec((1, D, FC), lambda e, f: (e, 0, f))

    def rows():
        return pl.BlockSpec((1, FC, D), lambda e, f: (e, f, 0))

    return pl.pallas_call(
        experts_kernel,
        grid=(EXPERTS, NF),
        in_specs=[
            whole(T, D), whole(T, D), whole(T, T), whole(16, T), whole(T, D), whole(D), whole(8, D),
            whole(D, D), columns(), columns(), rows(),
        ],
        out_specs=(
            whole(T, D), whole(T, D), whole(HQ, HD, T), whole(D, T), whole(NC, ACTS, T),
            whole(16, D),
        ),
        out_shape=(
            jax.ShapeDtypeStruct((T, D), BF),
            jax.ShapeDtypeStruct((T, D), F32),
            jax.ShapeDtypeStruct((HQ, HD, T), BF),
            jax.ShapeDtypeStruct((D, T), BF),
            jax.ShapeDtypeStruct((NC, ACTS, T), BF),
            jax.ShapeDtypeStruct((16, D), F32),
        ),
        scratch_shapes=[
            pltpu.VMEM((T, D), F32),
            pltpu.VMEM((T, D), F32),
            pltpu.VMEM((T, T), F32),
        ],
        cost_estimate=cost(13),
        name="experts",
    )(resid, moe_low, combine, missing, cotangent, gain, w_router, w_output, w_gate, w_up, w_down)


def side_by_side(ref, i, j):
    return jnp.concatenate([ref[i], ref[j]], axis=1)


def expert_weights_kernel(
    acts0_ref, acts1_ref, acts2_ref, acts3_ref, other_ref, moe_ref,
    cot0_ref, cot1_ref, cot2_ref, cot3_ref, out_ref, wide_ref, down_ref,
):
    core, y = lax.axis_index("core"), lax.axis_index("y")
    cot_refs = (cot0_ref, cot1_ref, cot2_ref, cot3_ref)
    for back, acts_ref in enumerate((acts0_ref, acts1_ref, acts2_ref, acts3_ref)):
        chip = 2 * ((y - back) & 3)
        near, far = chip + core, chip + 1 - core
        acts = jnp.concatenate([acts_ref[0], other_ref[back]], axis=1)
        missing = acts[SLOTS : SLOTS + 1].astype(F32)
        first, last = (jnp.where(missing == e, 0.0, 1.0).astype(BF) for e in (0.0, 2.0))

        def by_expert(at, rows):
            a, b = acts[at : at + rows], acts[at + rows : at + 2 * rows]
            middle = a * (1 - first) + b * (1 - last)
            return jnp.concatenate([a * first, middle, b * last], axis=0)

        wide = dot(side_by_side(moe_ref, near, far), by_expert(0, 2 * FS), NT)
        down = dot(by_expert(4 * FS, FS), cot_refs[back][...].reshape(2 * T, D))
        if back == 0:
            wide_ref[...] = wide
            down_ref[...] = down
        else:
            wide_ref[...] += wide
            down_ref[...] += down
    for i in range(NR):
        for e in range(EXPERTS):
            out_ref[i, 64 * e : 64 * (e + 1), :] = wide_ref[
                64 * i : 64 * (i + 1), 128 * e : 128 * (e + 1)
            ].astype(BF)
        half, lanes = 96 * (i % 2), 128 * (i // 2)
        out_ref[i, 192:288, :] = down_ref[half : half + 96, lanes : lanes + 128].astype(BF)


def expert_weights(acts, others, moe, cotangent):
    return pl.pallas_call(
        expert_weights_kernel,
        out_shape=jax.ShapeDtypeStruct((NR, PART, T), BF),
        scratch_shapes=[pltpu.VMEM((D, GU), F32), pltpu.VMEM((FS * EXPERTS, D), F32)],
        cost_estimate=cost(5),
        name="expert_weights",
    )(*acts, others, moe, *cotangent)


def own_rows(half):
    return pl.ds(pl.multiple_of(HD * half, HD), HD), pl.ds(pl.multiple_of(HD * (1 - half), HD), HD)


def project_weights_kernel(
    mine_ref, theirs_ref, normed_ref, back_ref, out_ref
):
    own, partner = own_rows(lax.axis_index("xl"))
    for b in range(NC):
        back_ref[b, own, :] = mine_ref[b, 0:HD, :]
        back_ref[b, partner, :] = theirs_ref[b, 0:HD, :]
        back_ref[b, 2 * HD :, :] = (
            mine_ref[b, HD:, :].astype(F32) + theirs_ref[b, HD:, :].astype(F32)
        ).astype(BF)
    total = jnp.zeros((D, 4 * HD), F32)
    for b in range(0, NC, 2):
        total += dot(side_by_side(normed_ref, b, b + 1), side_by_side(back_ref, b, b + 1), NT)
    low = total.astype(BF)
    for i in range(NR):
        out_ref[i, 0:64, :] = low[64 * i : 64 * (i + 1), 0:128]
        out_ref[i, 64:128, :] = low[64 * i : 64 * (i + 1), 128:256]


def project_weights(mine, theirs, normed):
    return pl.pallas_call(
        project_weights_kernel,
        out_shape=(
            jax.ShapeDtypeStruct((NC, 4 * HD, T), BF),
            jax.ShapeDtypeStruct((NR, MINE, T), BF),
        ),
        cost_estimate=cost(4),
        name="project_weights",
    )(mine, theirs, normed)


def output_weights_kernel(
    att_ref, att_other_ref, grad_ref, parts_ref, out_ref, heads_ref
):
    own, partner = own_rows(lax.axis_index("xl"))
    y = lax.axis_index("y")
    o = jnp.zeros((2 * HD, D), F32)
    for b in range(NC):
        heads_ref[b, own, :] = att_ref[b]
        heads_ref[b, partner, :] = att_other_ref[b]
    for b in range(0, NC, 2):
        o += dot(side_by_side(heads_ref, b, b + 1), side_by_side(grad_ref, b, b + 1), NT)
    low = o.astype(BF)
    for i in range(NR):
        half, lanes = 64 * (i % 2), 128 * (i // 2)
        at = 4 * ((i // 4 - y) & 3) + i % 4
        out_ref[at, 0:128, :] = parts_ref[i, 0:128, :]
        out_ref[at, 128:192, :] = low[half : half + 64, lanes : lanes + 128]


def output_weights(attended, attended_other, grad, parts):
    return pl.pallas_call(
        output_weights_kernel,
        out_shape=jax.ShapeDtypeStruct((NR, MINE, T), BF),
        scratch_shapes=[pltpu.VMEM((NC, 2 * HD, T), BF)],
        cost_estimate=cost(3),
        name="output_weights",
    )(attended, attended_other, grad, parts)


def project_back_kernel(
    g_ref, tok_ref, gain_ref, wq_ref, wk_ref, wv_ref, resid_grad_ref, small_ref, out_ref, sums_ref
):
    x = tok_ref[...].astype(F32)
    gain = gain_ref[...].astype(F32).reshape(1, D)
    inverse = lax.rsqrt(jnp.mean(x * x, axis=1, keepdims=True) + EPSILON)
    n = x * inverse

    def rows(first, last):
        a = g_ref[:, first:last, :]
        return swap(a.reshape(NC * (last - first), T).astype(F32)).astype(BF)

    normed_grad = dot(rows(0, 2 * HD), wq_ref[...], NT)
    normed_grad += dot(rows(2 * HD, 3 * HD), wk_ref[...], NT)
    normed_grad += dot(rows(3 * HD, 4 * HD), wv_ref[...], NT)
    scaled = normed_grad * gain
    out_ref[...] = (
        resid_grad_ref[...] + inverse * (scaled - n * jnp.mean(n * scaled, axis=1, keepdims=True))
    ).astype(BF)
    gain_grad = jnp.sum(normed_grad * n, axis=0, keepdims=True)
    row = lax.broadcasted_iota(jnp.int32, (8, D), 0)
    sums_ref[...] = jnp.where(
        row < EXPERTS, small_ref[0:8], jnp.where(row == EXPERTS, small_ref[8:16], gain_grad)
    )


def project_back(grads, tokens, gain, w_query, w_key, w_value, resid_grad, small):
    return pl.pallas_call(
        project_back_kernel,
        out_shape=(jax.ShapeDtypeStruct((T, D), BF), jax.ShapeDtypeStruct((8, D), F32)),
        cost_estimate=cost(5),
        name="project_back",
    )(grads, tokens, gain, w_query, w_key, w_value, resid_grad, small)


def assemble_kernel(
    g0_ref, g1_ref, g2_ref, p0_ref, p1_ref,
    q_ref, k_ref, v_ref, o_ref, g_ref, u_ref, d_ref,
):
    low_half = lax.broadcasted_iota(jnp.int32, (64, T), 1) < 64

    def rows(refs, pick, first, last):
        found = []
        for at, ref in enumerate(refs):
            begin, end = max(first - PIECE * at, 0), min(last - PIECE * at, PIECE)
            if begin < end:
                found.append(pick(ref)[begin:end])
        whole = found[0] if len(found) == 1 else jnp.concatenate(found, axis=0)
        return whole.astype(F32)

    def turned(a):
        return pltpu.roll(a, 64, 1)

    for c in range(2):
        here = slice(64 * c, 64 * (c + 1))

        def expert_rows(j, first, last, c=c):
            refs = (g0_ref, g1_ref, g2_ref)
            return rows(refs, lambda ref: ref[j // 2, 0, 0, c, j % 2], first, last)

        def project_rows(j, first, last, c=c):
            return rows((p0_ref, p1_ref), lambda ref: ref[0, j // 2, 0, c, j % 2], first, last)

        for m in range(NC // 2):
            tile = slice(T * m, T * (m + 1))
            for e in range(EXPERTS):
                a, b = (expert_rows(2 * m + i, 64 * e, 64 * (e + 1)) for i in range(2))
                g_ref[e, here, tile] = jnp.where(low_half, a, turned(b))
                u_ref[e, here, tile] = jnp.where(low_half, turned(a), b)
            a, b = (project_rows(2 * m + i, 64, 128) for i in range(2))
            k_ref[here, tile] = jnp.where(low_half, a, turned(b))
            v_ref[here, tile] = jnp.where(low_half, turned(a), b)
        for j in range(NC):
            q_ref[here, T * j : T * (j + 1)] = project_rows(j, 0, 64)
            o_ref[j, c] = project_rows(j, 128, 192)
            a = expert_rows(j, 192, 288)
            if c == 0:
                d_ref[0, j] = a[0:64]
                d_ref[1, j, 0:32] = a[64:96]
            else:
                d_ref[1, j, 32:64] = a[0:32]
                d_ref[2, j] = a[32:96]


def assemble(gathered):
    def experts_of(at):
        return pl.BlockSpec((4, 1, 1, 2, 2, PIECE, T), lambda a, b: (0, a, b, 0, 0, at, 0))

    def project_of(at):
        return pl.BlockSpec((1, 4, 1, 2, 2, PIECE, T), lambda a, b: (a, 0, b, 0, 0, at, 0))

    def rows(width):
        return pl.BlockSpec((T, width), lambda a, b: (2 * a + b, 0))

    def stack():
        return pl.BlockSpec((EXPERTS, T, FF), lambda a, b: (0, 2 * a + b, 0))

    return pl.pallas_call(
        assemble_kernel,
        grid=(4, 2),
        in_specs=[experts_of(0), experts_of(1), experts_of(2), project_of(3), project_of(4)],
        out_specs=(
            rows(D), rows(FF), rows(FF),
            pl.BlockSpec((NC, 2, HD, T), lambda a, b: (0, 0, 0, 2 * a + b)),
            stack(), stack(),
            pl.BlockSpec((EXPERTS, NC, FS, T), lambda a, b: (0, 0, 0, 2 * a + b)),
        ),
        out_shape=(
            jax.ShapeDtypeStruct((D, D), F32),
            jax.ShapeDtypeStruct((D, FF), F32),
            jax.ShapeDtypeStruct((D, FF), F32),
            jax.ShapeDtypeStruct((NC, 2, HD, D), F32),
            jax.ShapeDtypeStruct((EXPERTS, D, FF), F32),
            jax.ShapeDtypeStruct((EXPERTS, D, FF), F32),
            jax.ShapeDtypeStruct((EXPERTS, NC, FS, D), F32),
        ),
        cost_estimate=cost(20),
        name="assemble",
    )(*(gathered,) * 5)


def exchange(array, axes=SEQ):
    return lax.all_to_all(array, axes, 0, 0, tiled=True)


def swapped(array, axis):
    return lax.ppermute(array, axis, [(0, 1), (1, 0)])


def ring_moved(array, back):
    return lax.ppermute(array, "y", [(i, (i + back) % 4) for i in range(4)])


def gather(array, axes):
    return lax.all_gather(array, axes, axis=0)


def spread_sum(part, axes, count):
    parts = exchange(jnp.broadcast_to(part[None], (count, *part.shape)), axes)
    return jnp.sum(parts.astype(F32), axis=0)


def part_sum(parts, axes):
    return jnp.sum(exchange(parts, axes).astype(F32), axis=0).astype(BF)


def after(array, *others):
    return lax.optimization_barrier((array, *others))


def shards(
    tokens, cotangent, segment, routes, attn_gain, w_query, w_key, w_value, w_output,
    expert_norm_gain, w_router, w_gate, w_up, w_down,
):
    tokens, cotangent = tokens[0], cotangent[0]
    router_rows = jnp.pad(w_router.T, ((0, 8 - EXPERTS), (0, 0)))

    projected = project(tokens, segment, attn_gain, w_query, w_key, w_value)
    projected, cot = after(projected, cotangent)
    received = exchange(projected)
    cot = jnp.stack([cot, swapped(cot, "core")])
    received, normed, cot, cot3 = after(
        received, normed_columns(tokens, attn_gain), cot, ring_moved(cot, 3)
    )
    cot1, cot2 = ring_moved(cot, 1), ring_moved(cot, 2)
    normed_all = gather(normed, COLUMN)
    attended, att_mine, att_sent, full, log_total, q, k, cosine, sine = attend(received)
    attended, cot1, cot2 = after(exchange(attended), cot1, cot2)
    att_theirs = swapped(att_sent, "xl")
    resid, moe_low, moe_columns, combine, missing = residual(
        attended, tokens, routes[0], expert_norm_gain, router_rows, w_output
    )
    moe_all = gather(moe_columns, RING)
    output, resid_grad, grad_att, grad_columns, acts, small = experts(
        resid, moe_low, combine, missing, cotangent, expert_norm_gain, router_rows, w_output,
        w_gate, w_up, w_down,
    )
    grad_att, normed_all, att_theirs = after(grad_att, normed_all, att_theirs)
    acts = [acts[0:2]] + [
        ring_moved(acts[2 * back : 2 * back + 2], back) for back in (1, 2, 3)
    ]
    grad_all = gather(grad_columns, COLUMN)
    grad_att = exchange(grad_att)
    mine, sent = attend_back(
        received, grad_att, full, log_total, q, k, cosine, sine
    )
    sent, *acts = after(sent, *acts)
    theirs = swapped(sent, "xl")
    acts_theirs = swapped(jnp.stack([a[1] for a in acts]), "core")
    parts = expert_weights(acts, acts_theirs, moe_all, (cot, cot1, cot2, cot3))
    theirs, parts = after(theirs, parts)
    expert_part = part_sum(parts, PLANE)
    grads, weights = project_weights(mine, theirs, normed_all)
    weights = output_weights(att_mine, att_theirs, grad_all, weights)
    ring = [weights[0:4]] + [ring_moved(weights[4 * r : 4 * r + 4], r) for r in (1, 2, 3)]
    weights = sum(a.astype(F32) for a in ring).astype(BF)
    expert_part, weights = after(expert_part, weights)
    project_part = part_sum(weights, ("xh", "xl"))
    gathered = gather(jnp.concatenate([expert_part, project_part], axis=0), ALL)
    grads, project_part = after(grads, project_part)
    token_grad, small = project_back(
        exchange(grads, COLUMN), tokens, attn_gain, w_query, w_key, w_value, resid_grad, small
    )
    small = spread_sum(spread_sum(small.astype(BF), REST, NR), COLUMN, NC)
    dwq, dwk, dwv, dwo, dwg, dwu, dwd = assemble(
        gathered.reshape(4, 4, 2, 2, 2, PART + MINE, T)
    )
    return (
        output[None], token_grad[None], small[4], dwq, dwk, dwv, dwo.reshape(D, D), small[3],
        small[:EXPERTS].T, dwg, dwu, dwd.reshape(EXPERTS, FF, D),
    )


def solution(mesh):
    fine = Mesh(mesh.devices.reshape(4, 2, 4, 2, 2), AXES)
    by_token = P(ROWS, SEQ, None)
    return jax.shard_map(
        shards,
        mesh=fine,
        in_specs=(by_token, by_token, P(ROWS, SEQ), by_token) + (P(),) * 10,
        out_specs=(by_token, by_token) + (P(),) * 10,
        check_vma=False,
    )
```

```python
import functools
import math

import jax
import jax.numpy as jnp
from jax import lax
from jax.experimental import pallas as pl
from jax.experimental.pallas import tpu as pltpu
from jax.sharding import Mesh
from jax.sharding import PartitionSpec as P

BF = jnp.bfloat16
F32 = jnp.float32
D = 1024
HQ = 16
HK = 8
HD = 64
FF = 512
EXPERTS = 3
T = 128
S = 2048
BLK = 256
NB = S // BLK
WINDOW = 1024 // BLK + 1
HALF = HD // 2
PAY = 3 * HD + 16
FC = 512
NF = FF // FC
NC = 8
NR = 16
FS = FF // NC
GU = 2 * FS * EXPERTS
SLOTS = 6 * FS
ACTS = SLOTS + 16
PIECE = 96
PART = 3 * PIECE
MINE = 2 * PIECE

EPSILON = 1e-06
THETA_BASE = 10000.0
SOFT_SCALE = 0.125
NEG_FILL = -1e30

AXES = ("y", "xh", "z", "xl", "core")
ROWS = ("y", "xh")
SEQ = ("z", "xl", "core")
COLUMN = ("z", "core")
REST = ("y", "xh", "xl")
RING = ("y", "core")
PLANE = ("z", "xh", "xl")
ALL = ("y", "z", "xh", "xl", "core")

NN = (((1,), (0,)), ((), ()))
NT = (((1,), (1,)), ((), ()))
TN = (((0,), (0,)), ((), ()))


def device_of(head):
    return head // 4 * 4 + head % 2 * 2 + head // 2 % 2


def dot(a, b, dims=NN):
    return lax.dot_general(a, b, dims, preferred_element_type=F32)


def cost(us):
    return pl.CostEstimate(flops=int(us * 1e9), bytes_accessed=1 << 20, transcendentals=0)


def swap(a):
    return jnp.transpose(a, (1, 0))


def project_kernel(tok_ref, seg_ref, gain_ref, wq_ref, wk_ref, wv_ref, out_ref):
    x = tok_ref[...].astype(F32)
    inverse = lax.rsqrt(jnp.mean(x * x, axis=1, keepdims=True) + EPSILON)
    normed = (x * inverse * gain_ref[...].astype(F32).reshape(1, D)).astype(BF)
    ids = jnp.broadcast_to(seg_ref[...].astype(F32), (16, T)).astype(BF)
    for h in range(HQ):
        out_ref[h, 3 * HD :, :] = ids
    for j in range(4):
        q = swap(dot(normed, wq_ref[:, 256 * j : 256 * (j + 1)])).astype(BF)
        for i in range(4):
            out_ref[device_of(4 * j + i), 0:HD, :] = q[HD * i : HD * (i + 1)]
    for w_ref, at in ((wk_ref, HD), (wv_ref, 2 * HD)):
        for j in range(2):
            a = swap(dot(normed, w_ref[:, 256 * j : 256 * (j + 1)])).astype(BF)
            for i in range(4):
                part = a[HD * i : HD * (i + 1)]
                head = 2 * (4 * j + i)
                out_ref[device_of(head), at : at + HD, :] = part
                out_ref[device_of(head + 1), at : at + HD, :] = part


def project(tokens, segment, gain, w_query, w_key, w_value):
    return pl.pallas_call(
        project_kernel,
        out_shape=jax.ShapeDtypeStruct((HQ, PAY, T), BF),
        cost_estimate=cost(4),
        name="project",
    )(tokens, segment, gain, w_query, w_key, w_value)


def starts_of(x_ref):
    ids = x_ref[:, 3 * HD :, :].astype(F32)
    counts = [
        (jnp.sum(jnp.where(ids == float(s), 1.0, 0.0)) * (1.0 / 16)).astype(jnp.int32)
        for s in range(3)
    ]
    first = counts[0]
    second = first + counts[1]
    return first, second, second + counts[2]


def start_at(index, bounds):
    b1, b2, b3 = bounds
    return jnp.where(index >= b3, b3, jnp.where(index >= b2, b2, jnp.where(index >= b1, b1, 0)))


def joined(ref, i, at):
    return jnp.concatenate([ref[2 * i, at : at + HD, :], ref[2 * i + 1, at : at + HD, :]], axis=1)


def put_pair(keep_ref, send_ref, i, rows, a):
    low = a.astype(BF)
    for ref, half in ((keep_ref, lax.axis_index("xl")), (send_ref, 1 - lax.axis_index("xl"))):

        @pl.when((i & 1) == half)
        def _(ref=ref):
            ref[2 * (i // 2), rows, :] = low[:, :T]
            ref[2 * (i // 2) + 1, rows, :] = low[:, T:]


def windowed(i, bounds, body):
    blocks = i + 1 - start_at(i * BLK, bounds) // BLK
    for window in range(1, WINDOW + 1):
        pl.when(blocks == window)(functools.partial(body, window))


def masks_of(i, bounds):
    query = i * BLK + lax.broadcasted_iota(jnp.int32, (1, BLK), 1)
    first = start_at(query, bounds) - i * BLK
    key = lax.broadcasted_iota(jnp.int32, (BLK, BLK), 0)

    def allowed(back):
        inside = key >= first + back * BLK
        return inside & (key <= query - i * BLK) if back == 0 else inside

    return allowed


def attend_kernel(x_ref, att_ref, keep_ref, send_ref, full_ref, log_ref, q_ref, k_ref, cos_ref, sin_ref, kt_ref, v_ref):
    bounds = starts_of(x_ref)
    frequency = jnp.exp(
        lax.broadcasted_iota(jnp.int32, (HALF, 1), 0).astype(F32)
        * (-2.0 * math.log(THETA_BASE) / HD)
    )

    def turn_block(i, carry):
        index = i * BLK + lax.broadcasted_iota(jnp.int32, (1, BLK), 1)
        positions = (index - start_at(index, bounds)).astype(F32)
        angles = positions * frequency
        cosine, sine = jnp.cos(angles), jnp.sin(angles)
        cos_ref[i] = cosine
        sin_ref[i] = sine

        def turned(at):
            a = joined(x_ref, i, at).astype(F32)
            low, high = a[:HALF], a[HALF:]
            return jnp.concatenate(
                [low * cosine - high * sine, high * cosine + low * sine], axis=0
            )

        q_ref[i] = (turned(0).astype(BF).astype(F32) * SOFT_SCALE).astype(BF)
        k = turned(HD)
        k_ref[i] = k.astype(BF)
        kt_ref[i] = swap(k).astype(BF)
        v_ref[i] = joined(x_ref, i, 2 * HD)
        return carry

    lax.fori_loop(0, NB, turn_block, 0, unroll=True)

    def query_block(i, carry):
        q = q_ref[i]
        allowed = masks_of(i, bounds)

        def attend_window(window):
            scores = [
                jnp.where(allowed(back), dot(kt_ref[i - back], q), NEG_FILL)
                for back in range(window)
            ]
            top = jnp.max(functools.reduce(jnp.maximum, scores), axis=0, keepdims=True)
            weights = [jnp.exp(a - top) for a in scores]
            total = jnp.sum(functools.reduce(jnp.add, weights), axis=0, keepdims=True)
            acc = functools.reduce(
                jnp.add, [dot(v_ref[i - back], weights[back].astype(BF)) for back in range(window)]
            )
            attended = acc / total
            log_ref[i] = top + jnp.log(total)
            full_ref[i] = attended
            low = attended.astype(BF)
            att_ref[2 * i] = low[:, :T]
            att_ref[2 * i + 1] = low[:, T:]
            put_pair(keep_ref, send_ref, i, slice(0, HD), attended)

        windowed(i, bounds, attend_window)
        return carry

    lax.fori_loop(0, NB, query_block, 0)


def attend(received):
    return pl.pallas_call(
        attend_kernel,
        out_shape=(
            jax.ShapeDtypeStruct((HQ, HD, T), BF),
            jax.ShapeDtypeStruct((NC, HD, T), BF),
            jax.ShapeDtypeStruct((NC, HD, T), BF),
            jax.ShapeDtypeStruct((NB, HD, BLK), F32),
            jax.ShapeDtypeStruct((NB, 1, BLK), F32),
            jax.ShapeDtypeStruct((NB, HD, BLK), BF),
            jax.ShapeDtypeStruct((NB, HD, BLK), BF),
            jax.ShapeDtypeStruct((NB, HALF, BLK), F32),
            jax.ShapeDtypeStruct((NB, HALF, BLK), F32),
        ),
        scratch_shapes=[pltpu.VMEM((NB, BLK, HD), BF), pltpu.VMEM((NB, HD, BLK), BF)],
        cost_estimate=cost(13),
        name="attend",
    )(received)


def attend_back_kernel(
    x_ref, g_ref, full_ref, log_ref, q_ref, k_ref, cos_ref, sin_ref, keep_ref, send_ref,
    kt_ref, vt_ref, dk_ref, dv_ref,
):
    bounds = starts_of(x_ref)

    def prepare(i, carry):
        kt_ref[i] = swap(k_ref[i].astype(F32)).astype(BF)
        vt_ref[i] = swap(joined(x_ref, i, 2 * HD).astype(F32)).astype(BF)
        dk_ref[i] = jnp.zeros((HD, BLK), F32)
        dv_ref[i] = jnp.zeros((HD, BLK), F32)
        return carry

    lax.fori_loop(0, NB, prepare, 0, unroll=True)

    def turn_back(i, a):
        cosine, sine = cos_ref[i], sin_ref[i]
        low, high = a[:HALF], a[HALF:]
        return jnp.concatenate([low * cosine + high * sine, high * cosine - low * sine], axis=0)

    def put(i, at, a):
        put_pair(keep_ref, send_ref, i, slice(at, at + HD), a)

    def query_block(i, carry):
        q = q_ref[i]
        allowed = masks_of(i, bounds)
        grad = joined(g_ref, i, 0)
        delta = jnp.sum(grad.astype(F32) * full_ref[i], axis=0, keepdims=True)
        log_total = log_ref[i]

        def back_window(window):
            dq = jnp.zeros((HD, BLK), F32)
            for back in range(window):
                j = i - back
                scores = dot(kt_ref[j], q)
                p = jnp.where(allowed(back), jnp.exp(scores - log_total), 0.0)
                dp = dot(vt_ref[j], grad)
                ds = (p * (dp - delta)).astype(BF)
                dv_ref[j] += dot(grad, p.astype(BF), NT)
                dk_ref[j] += dot(q, ds, NT)
                dq += dot(k_ref[j], ds)
            put(i, 0, turn_back(i, dq * SOFT_SCALE))

        windowed(i, bounds, back_window)
        return carry

    lax.fori_loop(0, NB, query_block, 0)

    def finish(i, carry):
        put(i, HD, turn_back(i, dk_ref[i]))
        put(i, 2 * HD, dv_ref[i])
        return carry

    lax.fori_loop(0, NB, finish, 0, unroll=True)


def attend_back(received, grad, full, log_total, q, k, cosine, sine):
    return pl.pallas_call(
        attend_back_kernel,
        out_shape=(
            jax.ShapeDtypeStruct((NC, 3 * HD, T), BF),
            jax.ShapeDtypeStruct((NC, 3 * HD, T), BF),
        ),
        scratch_shapes=[
            pltpu.VMEM((NB, BLK, HD), BF),
            pltpu.VMEM((NB, BLK, HD), BF),
            pltpu.VMEM((NB, HD, BLK), F32),
            pltpu.VMEM((NB, HD, BLK), F32),
        ],
        cost_estimate=cost(13),
        name="attend_back",
    )(received, grad, full, log_total, q, k, cosine, sine)


def normed_kernel(tok_ref, gain_ref, out_ref):
    x = tok_ref[...].astype(F32)
    inverse = lax.rsqrt(jnp.mean(x * x, axis=1, keepdims=True) + EPSILON)
    out_ref[...] = swap(x * inverse * gain_ref[...].astype(F32).reshape(1, D)).astype(BF)


def normed_columns(tokens, gain):
    return pl.pallas_call(
        normed_kernel, out_shape=jax.ShapeDtypeStruct((D, T), BF), cost_estimate=cost(2), name="normed_columns"
    )(tokens, gain)


def resid_kernel(
    att_ref, tok_ref, routes_ref, gain_ref, wr_ref, wo_ref, resid_ref, moe_ref, moe_t_ref, combine_ref,
    missing_ref,
):
    heads = [att_ref[device_of(h)] for h in range(HQ)]
    attended = swap(jnp.concatenate(heads, axis=0).astype(F32)).astype(BF)
    resid = tok_ref[...].astype(F32) + dot(attended, wo_ref[...])
    inverse = lax.rsqrt(jnp.mean(resid * resid, axis=1, keepdims=True) + EPSILON)
    normed = resid * inverse * gain_ref[...].astype(F32).reshape(1, D)
    moe_low = normed.astype(BF)
    resid_ref[...] = resid
    moe_ref[...] = moe_low
    moe_t_ref[...] = swap(normed).astype(BF)
    logits = dot(moe_low, wr_ref[...], NT)
    lane = lax.broadcasted_iota(jnp.int32, (T, T), 1)
    r0, r1 = routes_ref[:, 0:1], routes_ref[:, 1:2]
    l0 = jnp.sum(jnp.where(lane[:, :8] == r0, logits, 0.0), axis=1, keepdims=True)
    l1 = jnp.sum(jnp.where(lane[:, :8] == r1, logits, 0.0), axis=1, keepdims=True)
    missing = (EXPERTS - r0 - r1).astype(F32)
    missing_ref[...] = swap(jnp.broadcast_to(missing, (T, T)))[0:16].astype(BF)
    top = jnp.maximum(l0, l1)
    e0, e1 = jnp.exp(l0 - top), jnp.exp(l1 - top)
    total = e0 + e1
    combine_ref[...] = jnp.where(lane == r0, e0 / total, 0.0) + jnp.where(
        lane == r1, e1 / total, 0.0
    )


def residual(attended, tokens, routes, gain, w_router, w_output):
    return pl.pallas_call(
        resid_kernel,
        out_shape=(
            jax.ShapeDtypeStruct((T, D), F32),
            jax.ShapeDtypeStruct((T, D), BF),
            jax.ShapeDtypeStruct((D, T), BF),
            jax.ShapeDtypeStruct((T, T), F32),
            jax.ShapeDtypeStruct((16, T), BF),
        ),
        cost_estimate=cost(4),
        name="residual",
    )(attended, tokens, routes, gain, w_router, w_output)


def experts_kernel(
    resid_ref, moe_ref, combine_ref, missing_ref, cot_ref, gain_ref, wr_ref, wo_ref,
    wg_ref, wu_ref, wd_ref, out_ref, resid_grad_ref, grad_att_ref, grad_t_ref, acts_ref, small_ref,
    mix_ref, moe_grad_ref, cgrad_ref,
):
    e, f = pl.program_id(0), pl.program_id(1)
    lane = lax.broadcasted_iota(jnp.int32, (T, T), 1)

    @pl.when((e == 0) & (f == 0))
    def _():
        mix_ref[...] = resid_ref[...]
        moe_grad_ref[...] = jnp.zeros_like(moe_grad_ref)
        cgrad_ref[...] = jnp.zeros_like(cgrad_ref)

    moe_low = moe_ref[...]
    grad_out = cot_ref[...].astype(F32)
    combine = jnp.sum(jnp.where(lane == e, combine_ref[...], 0.0), axis=1, keepdims=True)
    expert_grad = (combine * grad_out).astype(BF)
    gate = dot(moe_low, wg_ref[0])
    up = dot(moe_low, wu_ref[0])
    act_grad = dot(expert_grad, wd_ref[0], NT)
    sig = 1.0 / (1.0 + jnp.exp(-gate))
    silu = gate * sig
    act_low = (silu * up).astype(BF)
    down = dot(act_low, wd_ref[0])
    mix_ref[...] += combine * down
    cgrad_ref[...] += jnp.where(lane == e, jnp.sum(grad_out * down, axis=1, keepdims=True), 0.0)
    gate_grad = act_grad * up * (sig * (1.0 + gate * (1.0 - sig)))
    up_grad = act_grad * silu
    moe_grad_ref[...] += dot(gate_grad.astype(BF), wg_ref[0], NT) + dot(
        up_grad.astype(BF), wu_ref[0], NT
    )
    gate_t, up_t = swap(gate_grad), swap(up_grad)
    act_t = swap(combine * act_low.astype(F32))
    core, y = lax.axis_index("core"), lax.axis_index("y")
    missing = missing_ref[0:1].astype(F32)

    def slices(put):
        for i in range(FC // FS):
            j = f * (FC // FS) + i
            j = 2 * ((j // 2 - y) & 3) + ((j & 1) ^ core)
            for k, a in enumerate((gate_t, up_t, act_t)):
                put(j, (0, FS, 4 * FS)[k], (2 * FS, 3 * FS, 5 * FS)[k], a[FS * i : FS * (i + 1)])

    @pl.when(e == 0)
    def _():
        def put(j, at_a, at_b, a):
            acts_ref[j, at_a : at_a + FS, :] = a.astype(BF)

        slices(put)
        for j in range(NC):
            acts_ref[j, SLOTS:, :] = missing_ref[...]

    @pl.when(e == 1)
    def _():
        def put(j, at_a, at_b, a):
            rows = slice(at_a, at_a + FS)
            old = acts_ref[j, rows, :].astype(F32)
            acts_ref[j, rows, :] = jnp.where(missing == 0.0, a, old).astype(BF)
            acts_ref[j, at_b : at_b + FS, :] = a.astype(BF)

        slices(put)

    @pl.when(e == 2)
    def _():
        def put(j, at_a, at_b, a):
            rows = slice(at_b, at_b + FS)
            old = acts_ref[j, rows, :].astype(F32)
            acts_ref[j, rows, :] = jnp.where(missing == 2.0, old, a).astype(BF)

        slices(put)

    @pl.when((e == EXPERTS - 1) & (f == NF - 1))
    def _():
        out_ref[...] = mix_ref[...].astype(BF)
        weights, cgrad = combine_ref[...], cgrad_ref[...]
        mean = jnp.sum(weights * cgrad, axis=1, keepdims=True)
        logit_grad = (weights * (cgrad - mean)).astype(BF)
        small_ref[0:8, :] = dot(logit_grad, moe_low, TN)[0:8]
        moe_grad = moe_grad_ref[...] + dot(logit_grad[:, 0:8], wr_ref[...])
        resid = resid_ref[...]
        inverse = lax.rsqrt(jnp.mean(resid * resid, axis=1, keepdims=True) + EPSILON)
        n = resid * inverse
        small_ref[8:16, :] = jnp.broadcast_to(jnp.sum(moe_grad * n, axis=0, keepdims=True), (8, D))
        scaled = moe_grad * gain_ref[...].astype(F32).reshape(1, D)
        resid_grad = grad_out + inverse * (
            scaled - n * jnp.mean(n * scaled, axis=1, keepdims=True)
        )
        resid_grad_ref[...] = resid_grad
        grad_t_ref[...] = swap(resid_grad).astype(BF)
        grad_att = dot(wo_ref[...], resid_grad.astype(BF), NT).astype(BF)
        for h in range(HQ):
            grad_att_ref[device_of(h)] = grad_att[HD * h : HD * (h + 1)]


def experts(resid, moe_low, combine, missing, cotangent, gain, w_router, w_output, w_gate, w_up, w_down):
    def whole(*shape):
        return pl.BlockSpec(shape, lambda e, f: (0,) * len(shape))

    def columns():
        return pl.BlockSpec((1, D, FC), lambda e, f: (e, 0, f))

    def rows():
        return pl.BlockSpec((1, FC, D), lambda e, f: (e, f, 0))

    return pl.pallas_call(
        experts_kernel,
        grid=(EXPERTS, NF),
        in_specs=[
            whole(T, D), whole(T, D), whole(T, T), whole(16, T), whole(T, D), whole(D), whole(8, D),
            whole(D, D), columns(), columns(), rows(),
        ],
        out_specs=(
            whole(T, D), whole(T, D), whole(HQ, HD, T), whole(D, T), whole(NC, ACTS, T),
            whole(16, D),
        ),
        out_shape=(
            jax.ShapeDtypeStruct((T, D), BF),
            jax.ShapeDtypeStruct((T, D), F32),
            jax.ShapeDtypeStruct((HQ, HD, T), BF),
            jax.ShapeDtypeStruct((D, T), BF),
            jax.ShapeDtypeStruct((NC, ACTS, T), BF),
            jax.ShapeDtypeStruct((16, D), F32),
        ),
        scratch_shapes=[
            pltpu.VMEM((T, D), F32),
            pltpu.VMEM((T, D), F32),
            pltpu.VMEM((T, T), F32),
        ],
        cost_estimate=cost(13),
        name="experts",
    )(resid, moe_low, combine, missing, cotangent, gain, w_router, w_output, w_gate, w_up, w_down)


def side_by_side(ref, i, j):
    return jnp.concatenate([ref[i], ref[j]], axis=1)


def expert_weights_kernel(
    acts0_ref, acts1_ref, acts2_ref, acts3_ref, other_ref, moe_ref,
    cot0_ref, cot1_ref, cot2_ref, cot3_ref, out_ref, wide_ref, down_ref,
):
    core, y = lax.axis_index("core"), lax.axis_index("y")
    cot_refs = (cot0_ref, cot1_ref, cot2_ref, cot3_ref)
    for back, acts_ref in enumerate((acts0_ref, acts1_ref, acts2_ref, acts3_ref)):
        chip = 2 * ((y - back) & 3)
        near, far = chip + core, chip + 1 - core
        acts = jnp.concatenate([acts_ref[0], other_ref[back]], axis=1)
        missing = acts[SLOTS : SLOTS + 1].astype(F32)
        first, last = (jnp.where(missing == e, 0.0, 1.0).astype(BF) for e in (0.0, 2.0))

        def by_expert(at, rows):
            a, b = acts[at : at + rows], acts[at + rows : at + 2 * rows]
            middle = a * (1 - first) + b * (1 - last)
            return jnp.concatenate([a * first, middle, b * last], axis=0)

        wide = dot(side_by_side(moe_ref, near, far), by_expert(0, 2 * FS), NT)
        down = dot(by_expert(4 * FS, FS), cot_refs[back][...].reshape(2 * T, D))
        if back == 0:
            wide_ref[...] = wide
            down_ref[...] = down
        else:
            wide_ref[...] += wide
            down_ref[...] += down
    for i in range(NR):
        for e in range(EXPERTS):
            out_ref[i, 64 * e : 64 * (e + 1), :] = wide_ref[
                64 * i : 64 * (i + 1), 128 * e : 128 * (e + 1)
            ].astype(BF)
        half, lanes = 96 * (i % 2), 128 * (i // 2)
        out_ref[i, 192:288, :] = down_ref[half : half + 96, lanes : lanes + 128].astype(BF)


def expert_weights(acts, others, moe, cotangent):
    return pl.pallas_call(
        expert_weights_kernel,
        out_shape=jax.ShapeDtypeStruct((NR, PART, T), BF),
        scratch_shapes=[pltpu.VMEM((D, GU), F32), pltpu.VMEM((FS * EXPERTS, D), F32)],
        cost_estimate=cost(5),
        name="expert_weights",
    )(*acts, others, moe, *cotangent)


def own_rows(half):
    return pl.ds(pl.multiple_of(HD * half, HD), HD), pl.ds(pl.multiple_of(HD * (1 - half), HD), HD)


def project_weights_kernel(
    mine_ref, theirs_ref, normed_ref, back_ref, out_ref
):
    own, partner = own_rows(lax.axis_index("xl"))
    for b in range(NC):
        back_ref[b, own, :] = mine_ref[b, 0:HD, :]
        back_ref[b, partner, :] = theirs_ref[b, 0:HD, :]
        back_ref[b, 2 * HD :, :] = (
            mine_ref[b, HD:, :].astype(F32) + theirs_ref[b, HD:, :].astype(F32)
        ).astype(BF)
    total = jnp.zeros((D, 4 * HD), F32)
    for b in range(0, NC, 2):
        total += dot(side_by_side(normed_ref, b, b + 1), side_by_side(back_ref, b, b + 1), NT)
    low = total.astype(BF)
    for i in range(NR):
        out_ref[i, 0:64, :] = low[64 * i : 64 * (i + 1), 0:128]
        out_ref[i, 64:128, :] = low[64 * i : 64 * (i + 1), 128:256]


def project_weights(mine, theirs, normed):
    return pl.pallas_call(
        project_weights_kernel,
        out_shape=(
            jax.ShapeDtypeStruct((NC, 4 * HD, T), BF),
            jax.ShapeDtypeStruct((NR, MINE, T), BF),
        ),
        cost_estimate=cost(4),
        name="project_weights",
    )(mine, theirs, normed)


def output_weights_kernel(
    att_ref, att_other_ref, grad_ref, parts_ref, out_ref, heads_ref
):
    own, partner = own_rows(lax.axis_index("xl"))
    y = lax.axis_index("y")
    o = jnp.zeros((2 * HD, D), F32)
    for b in range(NC):
        heads_ref[b, own, :] = att_ref[b]
        heads_ref[b, partner, :] = att_other_ref[b]
    for b in range(0, NC, 2):
        o += dot(side_by_side(heads_ref, b, b + 1), side_by_side(grad_ref, b, b + 1), NT)
    low = o.astype(BF)
    for i in range(NR):
        half, lanes = 64 * (i % 2), 128 * (i // 2)
        at = 4 * ((i // 4 - y) & 3) + i % 4
        out_ref[at, 0:128, :] = parts_ref[i, 0:128, :]
        out_ref[at, 128:192, :] = low[half : half + 64, lanes : lanes + 128]


def output_weights(attended, attended_other, grad, parts):
    return pl.pallas_call(
        output_weights_kernel,
        out_shape=jax.ShapeDtypeStruct((NR, MINE, T), BF),
        scratch_shapes=[pltpu.VMEM((NC, 2 * HD, T), BF)],
        cost_estimate=cost(3),
        name="output_weights",
    )(attended, attended_other, grad, parts)


def project_back_kernel(
    g_ref, tok_ref, gain_ref, wq_ref, wk_ref, wv_ref, resid_grad_ref, small_ref, out_ref, sums_ref
):
    x = tok_ref[...].astype(F32)
    gain = gain_ref[...].astype(F32).reshape(1, D)
    inverse = lax.rsqrt(jnp.mean(x * x, axis=1, keepdims=True) + EPSILON)
    n = x * inverse

    def rows(first, last):
        a = g_ref[:, first:last, :]
        return swap(a.reshape(NC * (last - first), T).astype(F32)).astype(BF)

    normed_grad = dot(rows(0, 2 * HD), wq_ref[...], NT)
    normed_grad += dot(rows(2 * HD, 3 * HD), wk_ref[...], NT)
    normed_grad += dot(rows(3 * HD, 4 * HD), wv_ref[...], NT)
    scaled = normed_grad * gain
    out_ref[...] = (
        resid_grad_ref[...] + inverse * (scaled - n * jnp.mean(n * scaled, axis=1, keepdims=True))
    ).astype(BF)
    gain_grad = jnp.sum(normed_grad * n, axis=0, keepdims=True)
    row = lax.broadcasted_iota(jnp.int32, (8, D), 0)
    sums_ref[...] = jnp.where(
        row < EXPERTS, small_ref[0:8], jnp.where(row == EXPERTS, small_ref[8:16], gain_grad)
    )


def project_back(grads, tokens, gain, w_query, w_key, w_value, resid_grad, small):
    return pl.pallas_call(
        project_back_kernel,
        out_shape=(jax.ShapeDtypeStruct((T, D), BF), jax.ShapeDtypeStruct((8, D), F32)),
        cost_estimate=cost(5),
        name="project_back",
    )(grads, tokens, gain, w_query, w_key, w_value, resid_grad, small)


def assemble_kernel(
    g0_ref, g1_ref, g2_ref, p0_ref, p1_ref,
    q_ref, k_ref, v_ref, o_ref, g_ref, u_ref, d_ref,
):
    low_half = lax.broadcasted_iota(jnp.int32, (64, T), 1) < 64

    def rows(refs, pick, first, last):
        found = []
        for at, ref in enumerate(refs):
            begin, end = max(first - PIECE * at, 0), min(last - PIECE * at, PIECE)
            if begin < end:
                found.append(pick(ref)[begin:end])
        whole = found[0] if len(found) == 1 else jnp.concatenate(found, axis=0)
        return whole.astype(F32)

    def turned(a):
        return pltpu.roll(a, 64, 1)

    for c in range(2):
        here = slice(64 * c, 64 * (c + 1))

        def expert_rows(j, first, last, c=c):
            refs = (g0_ref, g1_ref, g2_ref)
            return rows(refs, lambda ref: ref[j // 2, 0, 0, c, j % 2], first, last)

        def project_rows(j, first, last, c=c):
            return rows((p0_ref, p1_ref), lambda ref: ref[0, j // 2, 0, c, j % 2], first, last)

        for m in range(NC // 2):
            tile = slice(T * m, T * (m + 1))
            for e in range(EXPERTS):
                a, b = (expert_rows(2 * m + i, 64 * e, 64 * (e + 1)) for i in range(2))
                g_ref[e, here, tile] = jnp.where(low_half, a, turned(b))
                u_ref[e, here, tile] = jnp.where(low_half, turned(a), b)
            a, b = (project_rows(2 * m + i, 64, 128) for i in range(2))
            k_ref[here, tile] = jnp.where(low_half, a, turned(b))
            v_ref[here, tile] = jnp.where(low_half, turned(a), b)
        for j in range(NC):
            q_ref[here, T * j : T * (j + 1)] = project_rows(j, 0, 64)
            o_ref[j, c] = project_rows(j, 128, 192)
            a = expert_rows(j, 192, 288)
            if c == 0:
                d_ref[0, j] = a[0:64]
                d_ref[1, j, 0:32] = a[64:96]
            else:
                d_ref[1, j, 32:64] = a[0:32]
                d_ref[2, j] = a[32:96]


def assemble(gathered):
    def experts_of(at):
        return pl.BlockSpec((4, 1, 1, 2, 2, PIECE, T), lambda a, b: (0, a, b, 0, 0, at, 0))

    def project_of(at):
        return pl.BlockSpec((1, 4, 1, 2, 2, PIECE, T), lambda a, b: (a, 0, b, 0, 0, at, 0))

    def rows(width):
        return pl.BlockSpec((T, width), lambda a, b: (2 * a + b, 0))

    def stack():
        return pl.BlockSpec((EXPERTS, T, FF), lambda a, b: (0, 2 * a + b, 0))

    return pl.pallas_call(
        assemble_kernel,
        grid=(4, 2),
        in_specs=[experts_of(0), experts_of(1), experts_of(2), project_of(3), project_of(4)],
        out_specs=(
            rows(D), rows(FF), rows(FF),
            pl.BlockSpec((NC, 2, HD, T), lambda a, b: (0, 0, 0, 2 * a + b)),
            stack(), stack(),
            pl.BlockSpec((EXPERTS, NC, FS, T), lambda a, b: (0, 0, 0, 2 * a + b)),
        ),
        out_shape=(
            jax.ShapeDtypeStruct((D, D), F32),
            jax.ShapeDtypeStruct((D, FF), F32),
            jax.ShapeDtypeStruct((D, FF), F32),
            jax.ShapeDtypeStruct((NC, 2, HD, D), F32),
            jax.ShapeDtypeStruct((EXPERTS, D, FF), F32),
            jax.ShapeDtypeStruct((EXPERTS, D, FF), F32),
            jax.ShapeDtypeStruct((EXPERTS, NC, FS, D), F32),
        ),
        cost_estimate=cost(20),
        name="assemble",
    )(*(gathered,) * 5)


def exchange(array, axes=SEQ):
    return lax.all_to_all(array, axes, 0, 0, tiled=True)


def swapped(array, axis):
    return lax.ppermute(array, axis, [(0, 1), (1, 0)])


def ring_moved(array, back):
    return lax.ppermute(array, "y", [(i, (i + back) % 4) for i in range(4)])


def gather(array, axes):
    return lax.all_gather(array, axes, axis=0)


def spread_sum(part, axes, count):
    parts = exchange(jnp.broadcast_to(part[None], (count, *part.shape)), axes)
    return jnp.sum(parts.astype(F32), axis=0)


def part_sum(parts, axes):
    return jnp.sum(exchange(parts, axes).astype(F32), axis=0).astype(BF)


def after(array, *others):
    return lax.optimization_barrier((array, *others))


def shards(
    tokens, cotangent, segment, routes, attn_gain, w_query, w_key, w_value, w_output,
    expert_norm_gain, w_router, w_gate, w_up, w_down,
):
    tokens, cotangent = tokens[0], cotangent[0]
    router_rows = jnp.pad(w_router.T, ((0, 8 - EXPERTS), (0, 0)))

    projected = project(tokens, segment, attn_gain, w_query, w_key, w_value)
    projected, cot = after(projected, cotangent)
    received = exchange(projected)
    cot = jnp.stack([cot, swapped(cot, "core")])
    received, normed, cot, cot3 = after(
        received, normed_columns(tokens, attn_gain), cot, ring_moved(cot, 3)
    )
    cot1, cot2 = ring_moved(cot, 1), ring_moved(cot, 2)
    normed_all = gather(normed, COLUMN)
    attended, att_mine, att_sent, full, log_total, q, k, cosine, sine = attend(received)
    attended, cot1, cot2, att_theirs = after(
        exchange(attended), cot1, cot2, swapped(att_sent, "xl")
    )
    resid, moe_low, moe_columns, combine, missing = residual(
        attended, tokens, routes[0], expert_norm_gain, router_rows, w_output
    )
    moe_all = gather(moe_columns, RING)
    output, resid_grad, grad_att, grad_columns, acts, small = experts(
        resid, moe_low, combine, missing, cotangent, expert_norm_gain, router_rows, w_output,
        w_gate, w_up, w_down,
    )
    grad_att, normed_all = after(grad_att, normed_all)
    grad_all = gather(grad_columns, COLUMN)
    acts = [acts[2 * back : 2 * back + 2] for back in range(4)]
    grad_att, *acts = after(exchange(grad_att), *acts)
    acts = acts[:1] + [ring_moved(acts[back], back) for back in (1, 2, 3)]
    mine, sent = attend_back(
        received, grad_att, full, log_total, q, k, cosine, sine
    )
    sent, *acts = after(sent, *acts)
    theirs = swapped(sent, "xl")
    acts_theirs = swapped(jnp.stack([a[1] for a in acts]), "core")
    parts = expert_weights(acts, acts_theirs, moe_all, (cot, cot1, cot2, cot3))
    theirs, parts = after(theirs, parts)
    expert_part = part_sum(parts, PLANE)
    grads, weights = project_weights(mine, theirs, normed_all)
    weights = output_weights(att_mine, att_theirs, grad_all, weights)
    ring = [weights[0:4]] + [ring_moved(weights[4 * r : 4 * r + 4], r) for r in (1, 2, 3)]
    weights = sum(a.astype(F32) for a in ring).astype(BF)
    expert_part, weights = after(expert_part, weights)
    project_part = part_sum(weights, ("xh", "xl"))
    gathered = gather(jnp.concatenate([expert_part, project_part], axis=0), ALL)
    grads, project_part = after(grads, project_part)
    token_grad, small = project_back(
        exchange(grads, COLUMN), tokens, attn_gain, w_query, w_key, w_value, resid_grad, small
    )
    small = spread_sum(spread_sum(small.astype(BF), REST, NR), COLUMN, NC)
    dwq, dwk, dwv, dwo, dwg, dwu, dwd = assemble(
        gathered.reshape(4, 4, 2, 2, 2, PART + MINE, T)
    )
    return (
        output[None], token_grad[None], small[4], dwq, dwk, dwv, dwo.reshape(D, D), small[3],
        small[:EXPERTS].T, dwg, dwu, dwd.reshape(EXPERTS, FF, D),
    )


def solution(mesh):
    fine = Mesh(mesh.devices.reshape(4, 2, 4, 2, 2), AXES)
    by_token = P(ROWS, SEQ, None)
    return jax.shard_map(
        shards,
        mesh=fine,
        in_specs=(by_token, by_token, P(ROWS, SEQ), by_token) + (P(),) * 10,
        out_specs=(by_token, by_token) + (P(),) * 10,
        check_vma=False,
    )
```
